32 devices in a mesh: seq: 8 (over y, x, core), tp: 4 (over z).
Axes of the slice: x: 2, y: 2, z: 4, core: 2. Of those that a mesh axis runs over, the one named last changes fastest.
Arguments:
- tokens: bfloat16 [128, 17, 1152], P('seq'), may hold values from -6 to 6
- cotangent: bfloat16 [128, 17, 1152], P('seq'), may hold values from -6 to 6
- caption: bfloat16 [4, 300, 1152], replicated, may hold values from -6 to 6
- condition: float32 [4, 1152], replicated, may hold values from -6 to 6
- frames: int32 [4], replicated, may hold values from 1 to 17, 44 in all
- cap_len: int32 [4], replicated, may hold values from 1 to 300, 600 in all
- clip_of: int32 [128], P('seq'), may hold values from 0 to 3
- w_qkv: bfloat16 [1152, 3, 1152], P('seq', None, 'tp'), may hold values from -0.1875 to 0.1875
- w_out: bfloat16 [1152, 1152], P('tp', 'seq'), may hold values from -0.375 to 0.375
- w_query2: bfloat16 [1152, 1152], P('seq', 'tp'), may hold values from -0.1875 to 0.1875
- w_kv2: bfloat16 [1152, 2, 1152], P('seq', None, 'tp'), may hold values from -0.1875 to 0.1875
- w_out2: bfloat16 [1152, 1152], P('tp', 'seq'), may hold values from -0.75 to 0.75
- w_up: bfloat16 [1152, 4608], P('seq', 'tp'), may hold values from -0.1875 to 0.1875
- w_down: bfloat16 [4608, 1152], P('tp', 'seq'), may hold values from -0.09375 to 0.09375
- w_ada: bfloat16 [1152, 6912], P('seq', 'tp'), may hold values from -0.1875 to 0.1875
Outputs:
- output: bfloat16 [128, 17, 1152], P('seq')
- d_tokens: bfloat16 [128, 17, 1152], P('seq')
- d_caption: float32 [4, 300, 1152], P(None, None, 'tp')
- d_condition: float32 [4, 1152], replicated
- d_w_qkv: float32 [1152, 3, 1152], P('seq', None, 'tp')
- d_w_out: float32 [1152, 1152], P('tp', 'seq')
- d_w_query2: float32 [1152, 1152], P('seq', 'tp')
- d_w_kv2: float32 [1152, 2, 1152], P('seq', None, 'tp')
- d_w_out2: float32 [1152, 1152], P('tp', 'seq')
- d_w_up: float32 [1152, 4608], P('seq', 'tp')
- d_w_down: float32 [4608, 1152], P('tp', 'seq')
- d_w_ada: float32 [1152, 6912], P('seq', 'tp')
The draws below stay inside these ranges and needn't reach their ends.
Inputs may be any that keep to these rules, and one draw needn't show every extreme that they name: frames of each clip; they add up to 44 and one clip has 17. `cap_len`: live caption tokens of each clip, the first ones of its slots; they add up to 600 and one clip has 300.
All inputs are finite; a program needn't handle non-finite values.
Results may differ from the reference program's by a relative error of at most 0.024.
Values may be sent and summed in bfloat16 or wider, within the bound.
No kernel may reach another device: no remote copies, remote signals or barrier semaphores. Data moves between devices by JAX's collectives and lax.ppermute only.
A program may use at most 128 MiB of HBM per device.

```python
import math
import jax
import jax.numpy as jnp
import numpy as np
from jax import lax

D = 1152
HEADS = 16
FF = 4608
HDIM = 72
CAP = 300
CLIPS = 4
FMAX = 17
SEQS = 128


def place_ends(values, stream_key, smallest, high):
    longest = values.shape.index(max(values.shape))
    spots = []
    for shift in (0, 1):
        where = [jax.random.randint(jax.random.fold_in(stream_key, axis), (), 0, length) for axis, length in enumerate(values.shape)]
        where[longest] = (where[longest] + shift) % values.shape[longest]
        spots.append(tuple(where))
    return values.at[spots[0]].set(smallest).at[spots[1]].set(high)


def shard_levels(rng, extent, shards, smallest, high):
    def one(position, shards_of):
        steps = jax.random.uniform(jax.random.fold_in(jax.random.fold_in(rng, 6), position), (shards_of,), jnp.float32, smallest / len(shards), high / len(shards))
        return jnp.repeat(jnp.exp(steps), extent[position] // shards_of).reshape((-1,) + (1,) * (len(extent) - position - 1))

    level = one(*shards[0])
    for cut in shards[1:]:
        level = level * one(*cut)
    return level


def length_profile(amount, total, most, slope):
    weights = [(1 << 20) // math.isqrt(standing ** slope) + 1 for standing in range(2, amount + 1)]
    rest, given = total - most - (amount - 1), [1] * (amount - 1)
    while rest > 0:
        free = [i for i in range(amount - 1) if given[i] < most]
        whole, left = sum([weights[i] for i in free]), rest
        for i in free:
            addition = min(most - given[i], max(1, left * weights[i] // whole), rest)
            given[i] = given[i] + addition
            rest = rest - addition
    return np.array([most] + given)


def uneven_parts(own_key, number_of, total, most, lean):
    if number_of == 2:
        one = jax.random.randint(own_key, (), max(1, total - most), min(most, total - 1) + 1)
        return jnp.stack([one, total - one])
    sizes = jnp.asarray(length_profile(number_of, total, most, lean), jnp.int32)
    couples = (number_of - 1) // 2
    donor, taker = sizes[1:1 + 2 * couples:2], sizes[2:2 + 2 * couples:2]
    margin = jnp.minimum(donor - 1, most - taker)
    passed = jax.random.randint(jax.random.fold_in(own_key, 1), (couples,), 0, 1 << 20) % (margin + 1)
    sizes = sizes.at[1:1 + 2 * couples:2].set(donor - passed).at[2:2 + 2 * couples:2].set(taker + passed)
    return sizes[jax.random.permutation(jax.random.fold_in(own_key, 2), number_of)]


def bell_draw(rng, dims, deviation, most, cuts=(), held_as=jnp.bfloat16):
    loudness = shard_levels(rng, dims, cuts, -0.22, 0.18) if cuts else 1.0
    values = jax.random.normal(rng, dims, jnp.float32) * deviation * loudness
    return jnp.minimum(jnp.maximum(values, -most), most).astype(held_as)


def setup_inputs(seed: int = 0) -> dict:
    keys = jax.random.split(jax.random.key(seed), 16)
    return {
        "tokens": bell_draw(keys[0], (SEQS, FMAX, D), 1.0, 6.0, ((0, 8),)),
        "cotangent": bell_draw(keys[1], (SEQS, FMAX, D), 1.0, 6.0, ((0, 8),)),
        "caption": bell_draw(keys[2], (CLIPS, CAP, D), 1.0, 6.0),
        "condition": bell_draw(keys[3], (CLIPS, D), 1.0, 6.0, (), jnp.float32),
        "frames": uneven_parts(keys[4], CLIPS, 2 * FMAX + 10, FMAX, 0).astype(jnp.int32),
        "cap_len": uneven_parts(keys[5], CLIPS, 2 * CAP, CAP, 0).astype(jnp.int32),
        "clip_of": place_ends(jax.random.randint(keys[6], (SEQS,), 0, CLIPS), jax.random.fold_in(keys[6], 1), 0, CLIPS - 1).astype(jnp.int32),
        "w_qkv": bell_draw(keys[7], (D, 3, D), D ** -0.5, 0.1875, ((0, 8), (2, 4))),
        "w_out": bell_draw(keys[8], (D, D), (D // 4) ** -0.5, 0.375, ((0, 4), (1, 8))),
        "w_query2": bell_draw(keys[9], (D, D), D ** -0.5, 0.1875, ((0, 8), (1, 4))),
        "w_kv2": bell_draw(keys[10], (D, 2, D), D ** -0.5, 0.1875, ((0, 8), (2, 4))),
        "w_out2": bell_draw(keys[11], (D, D), (D // 16) ** -0.5, 0.75, ((0, 4), (1, 8))),
        "w_up": bell_draw(keys[12], (D, FF), D ** -0.5, 0.1875, ((0, 8), (1, 4))),
        "w_down": bell_draw(keys[13], (FF, D), FF ** -0.5, 0.09375, ((0, 4), (1, 8))),
        "w_ada": bell_draw(keys[14], (D, 6 * D), D ** -0.5, 0.1875, ((0, 8), (1, 4))),
    }


@jax.custom_vjp
def low(v):
    return lax.optimization_barrier(v.astype(jnp.bfloat16)).astype(jnp.float32)

@jax.custom_vjp
def low_back(v):
    return v

def low_keep(v):
    return (low(v), None)

def low_pass(kept, grad):
    return (grad,)

def back_keep(v):
    return (v, None)

def back_low(kept, grad):
    return (low(grad),)
low.defvjp(low_keep, low_pass)
low_back.defvjp(back_keep, back_low)
EPSILON = 1e-06
NEG_FILL = -1e+30
HIGHEST = lax.Precision.HIGHEST

def normalize(rows):
    center = rows - lax.optimization_barrier(jnp.mean(rows, -1, keepdims=True))
    return center * lax.rsqrt(lax.optimization_barrier(jnp.mean(center * center, -1, keepdims=True)) + EPSILON)

def rounded(value):
    return low(low_back(value))

def reference(tokens, cotangent, caption, condition, frames, cap_len, clip_of, w_qkv, w_out, w_query2, w_kv2, w_out2, w_up, w_down, w_ada):
    head_scale = HDIM ** (-0.5)
    clip_ids = jnp.arange(CLIPS).astype(jnp.int32)
    clip_hot = (clip_of[:, None] == clip_ids[None, :]).astype(jnp.float32)
    seq_frames = lax.optimization_barrier(jnp.sum(jnp.where(clip_hot > 0, frames[None, :], 0), 1))
    live = (jnp.arange(FMAX)[None, :] < seq_frames[:, None]).astype(jnp.float32)
    key_count = CLIPS * CAP
    key_clip = (jnp.arange(key_count) // CAP).astype(jnp.int32)
    key_len = lax.optimization_barrier(jnp.sum(jnp.where(key_clip[:, None] == clip_ids[None, :], cap_len[None, :], 0), 1))
    key_live = jnp.arange(key_count) % CAP < key_len
    key_match = (clip_of[:, None] == key_clip[None, :]) & key_live[None, :]
    group = math.gcd(SEQS, 128)
    blocks = SEQS // group

    def forward(rows_all, cap, cond, wqkv, wout, wq2, wkv2, wout2, wup, wdown, wada):
        scaled = low(jax.nn.silu(cond))
        mods = jnp.dot(scaled, wada, precision=HIGHEST).reshape(CLIPS, 6, D)
        seq_mods = jnp.einsum('sc,cjd->sjd', clip_hot, mods, precision=HIGHEST)
        cross_kv = rounded(jnp.dot(cap.reshape(key_count, D), wkv2.reshape(D, 2 * D), precision=HIGHEST)).reshape(key_count, 2, HEADS, HDIM)
        cross_key = cross_kv[:, 0]
        cross_value = cross_kv[:, 1]

        def group_pass(pieces):
            rows_in, mod_rows, live_rows, match_rows = pieces
            attn_in = low(normalize(rows_in) * (1.0 + mod_rows[:, 1:2]) + mod_rows[:, 0:1])
            triple = rounded(jnp.einsum('sfd,dc->sfc', attn_in, wqkv.reshape(D, 3 * D), precision=HIGHEST)).reshape(-1, FMAX, 3, HEADS, HDIM)
            raw = low_back(jnp.einsum('sfhe,sghe->shfg', triple[:, :, 0], triple[:, :, 1], precision=HIGHEST) * head_scale)
            scores = jnp.where(live_rows[:, None, None, :] > 0, raw, NEG_FILL)
            probs = low(jax.nn.softmax(scores, axis=-1))
            frame_out = rounded(jnp.einsum('shfg,sghe->sfhe', probs, triple[:, :, 2], precision=HIGHEST)).reshape(-1, FMAX, D)
            branch_one = low_back(jnp.einsum('sfc,cd->sfd', frame_out, wout, precision=HIGHEST))
            first = rows_in + mod_rows[:, 2:3] * branch_one
            first_low = low(first)
            cross_query = rounded(jnp.einsum('sfd,dc->sfc', first_low, wq2, precision=HIGHEST)).reshape(-1, FMAX, HEADS, HDIM)
            cross_raw = low_back(jnp.einsum('sfhe,khe->sfhk', cross_query, cross_key, precision=HIGHEST) * head_scale)
            cross_scores = jnp.where(match_rows[:, None, None, :], cross_raw, NEG_FILL)
            cross_probs = low(jax.nn.softmax(cross_scores, axis=-1))
            cross_out = rounded(jnp.einsum('sfhk,khe->sfhe', cross_probs, cross_value, precision=HIGHEST)).reshape(-1, FMAX, D)
            second = first + low_back(jnp.einsum('sfc,cd->sfd', cross_out, wout2, precision=HIGHEST))
            mlp_in = low(normalize(second) * (1.0 + mod_rows[:, 4:5]) + mod_rows[:, 3:4])
            hidden_pre = low_back(jnp.einsum('sfd,dk->sfk', mlp_in, wup, precision=HIGHEST))
            hidden = low(jax.nn.gelu(hidden_pre, approximate=True))
            branch_three = low_back(jnp.einsum('sfk,kd->sfd', hidden, wdown, precision=HIGHEST))
            third = second + mod_rows[:, 5:6] * branch_three
            return third * live_rows[:, :, None]
        results = lax.map(jax.checkpoint(group_pass), (rows_all.reshape(blocks, group, FMAX, D), seq_mods.reshape(blocks, group, 6, D), live.reshape(blocks, group, FMAX), key_match.reshape(blocks, group, key_count)))
        return results.reshape(SEQS, FMAX, D)
    primals = (tokens.astype(jnp.float32), caption.astype(jnp.float32), condition.astype(jnp.float32), w_qkv.astype(jnp.float32), w_out.astype(jnp.float32), w_query2.astype(jnp.float32), w_kv2.astype(jnp.float32), w_out2.astype(jnp.float32), w_up.astype(jnp.float32), w_down.astype(jnp.float32), w_ada.astype(jnp.float32))
    result, pullback = jax.vjp(forward, *primals)
    grads = pullback(cotangent.astype(jnp.float32))
    return (result.astype(jnp.bfloat16), grads[0].astype(jnp.bfloat16), grads[1], grads[2], grads[3], grads[4], grads[5], grads[6], grads[7], grads[8], grads[9], grads[10])
```

```python
import functools

import jax
import jax.numpy as jnp
from jax import lax
from jax.experimental import pallas as pl
from jax.experimental.pallas import tpu as pltpu
from jax.sharding import PartitionSpec as P

HDIM = 72
EPSILON = 1e-06
NEG_FILL = -1e30
F32 = jnp.float32
BF16 = jnp.bfloat16
SCALE = HDIM ** (-0.5)
VMEM_LIMIT = 48 << 20


def dot_nn(a, b):
    return lax.dot_general(a, b, (((1,), (0,)), ((), ())), preferred_element_type=F32)


def dot_nt(a, b):
    return lax.dot_general(a, b, (((1,), (1,)), ((), ())), preferred_element_type=F32)


def dot_tn(a, b):
    return lax.dot_general(a, b, (((0,), (0,)), ((), ())), preferred_element_type=F32)


def call(body, outs, *args, name, specs=None, flops=0):
    vmem = pl.BlockSpec(memory_space=pltpu.VMEM)
    in_specs = [vmem] * len(args) if specs is None else [vmem if s is None else s for s in specs]
    moved = sum(a.size * a.dtype.itemsize for a in args)
    moved += sum(o.size * o.dtype.itemsize for o in outs)
    return pl.pallas_call(
        body,
        out_shape=tuple(outs),
        in_specs=in_specs,
        out_specs=tuple(vmem for _ in outs),
        compiler_params=pltpu.CompilerParams(vmem_limit_bytes=VMEM_LIMIT),
        cost_estimate=pl.CostEstimate(flops=flops, transcendentals=0, bytes_accessed=moved),
        name=name,
    )(*args)


def sds(shape, dtype=BF16):
    return jax.ShapeDtypeStruct(shape, dtype)


def norm_parts(rows):
    center = rows - jnp.mean(rows, -1, keepdims=True)
    inv = lax.rsqrt(jnp.mean(center * center, -1, keepdims=True) + EPSILON)
    return center * inv, inv


def expand(hot, table):
    high = table.astype(BF16)
    low = (table - high.astype(F32)).astype(BF16)
    return dot_nn(hot, high) + dot_nn(hot, low)


def clip_sums(hot, values):
    return dot_tn(hot, values.astype(BF16))


def norm_back(grad, n, inv):
    return inv * (grad - jnp.mean(grad, -1, keepdims=True) - n * jnp.mean(grad * n, -1, keepdims=True))


def softmax_rows(scores):
    top = jnp.max(scores, -1, keepdims=True)
    weights = jnp.exp(scores - top)
    return weights / jnp.sum(weights, -1, keepdims=True)


def pack_rows(out_ref, value, tp):
    own, n = value.shape[0] // tp, value.shape[1]
    for r in range(tp):
        out_ref[:, r * n : (r + 1) * n] = value[r * own : (r + 1) * own]


def unpack_heads(pieces, tp, n):
    rows = []
    for b in range(tp):
        cols = []
        for k in range(tp):
            r = (b - k) % tp
            cols.append(pieces[k][:, r * n : (r + 1) * n])
        rows.append(jnp.concatenate(cols, axis=1))
    return jnp.concatenate(rows, axis=0)


def frame_forward(tp, tok, hot, mods, row_id, key_id, w_qkv, attn_o, qkv_o, prob_o, fo_o, pack_o):
    n, _ = norm_parts(tok[...].astype(F32))
    low = (n * (1.0 + expand(hot[...], mods[1])) + expand(hot[...], mods[0])).astype(BF16)
    attn_o[...] = low
    qkv = dot_nn(low, w_qkv[...]).astype(BF16)
    qkv_o[...] = qkv
    inner = qkv.shape[1] // 3
    allowed = row_id[...] == key_id[...]
    outs = []
    for h in range(inner // HDIM):
        q, k, v = (qkv[:, i * inner + h * HDIM : i * inner + (h + 1) * HDIM] for i in range(3))
        probs = softmax_rows(jnp.where(allowed, dot_nt(q, k) * SCALE, NEG_FILL)).astype(BF16)
        prob_o[h] = probs
        outs.append(dot_nn(probs, v).astype(BF16))
    result = jnp.concatenate(outs, axis=1)
    fo_o[...] = result
    pack_rows(pack_o, result, tp)


def key_values(cap, w_kv, kv_o):
    kv_o[...] = dot_nn(cap[...], w_kv[...]).astype(BF16)


def cross_forward(tp, inner, *refs):
    pieces = [r[...] for r in refs[:tp]]
    tok, hot, mods, row_clip, key_clip, w_b, kv = refs[tp : tp + 7]
    x1_o, low_o, own_o, cq_o, prob_o, co_o, pack_o = refs[tp + 7 :]
    own, width = own_o.shape
    branch = dot_nt(unpack_heads(pieces, tp, inner), w_b[:, :width])
    own_o[...] = branch[:own]
    first = tok[...].astype(F32) + expand(hot[...], mods[2]) * branch
    x1_o[...] = first
    low = first.astype(BF16)
    low_o[...] = low
    cq = dot_nn(low, w_b[:, width + 2 * inner : width + 3 * inner]).astype(BF16)
    cq_o[...] = cq
    allowed = row_clip[...] == key_clip[...]
    outs = []
    for h in range(inner // HDIM):
        cols = slice(h * HDIM, (h + 1) * HDIM)
        key = kv[:, h * HDIM : (h + 1) * HDIM]
        value = kv[:, inner + h * HDIM : inner + (h + 1) * HDIM]
        scores = jnp.where(allowed, dot_nt(cq[:, cols], key) * SCALE, NEG_FILL)
        probs = softmax_rows(scores).astype(BF16)
        prob_o[h] = probs
        outs.append(dot_nn(probs, value).astype(BF16))
    result = jnp.concatenate(outs, axis=1)
    co_o[...] = result
    pack_rows(pack_o, result, tp)


GELU_C = 0.7978845608028654


def mlp_both(tp, inner, *refs):
    pieces = [r[...] for r in refs[:tp]]
    first, cot, live, hot, mods, w_c = refs[tp : tp + 6]
    outs = refs[tp + 6 :]
    x2_o, mlp_o, hid_o, db3_o, dpre_o = outs[:5]
    b3_o, dm_o = outs[5 : 5 + tp], outs[5 + tp :]
    own, width = x2_o.shape
    hid = hid_o.shape[1]
    w_up, w_down = w_c[:, width : width + hid], w_c[:, width + hid :]
    second = first[...] + dot_nt(unpack_heads(pieces, tp, inner), w_c[:, :width])
    x2_o[...] = second[:own]
    n, _ = norm_parts(second)
    low = (n * (1.0 + expand(hot[...], mods[4])) + expand(hot[...], mods[3])).astype(BF16)
    mlp_o[...] = low
    pre = dot_nn(low, w_up)
    inside = GELU_C * (pre + 0.044715 * (pre * pre * pre))
    th = jnp.tanh(inside)
    hidden = (0.5 * pre * (1.0 + th)).astype(BF16)
    hid_o[...] = hidden
    d_b3 = (expand(hot[...], mods[5]) * (cot[...].astype(F32) * live[...])).astype(BF16)
    db3_o[...] = d_b3
    slope = 0.5 * (1.0 + th) + 0.5 * pre * (1.0 - th * th) * (
        GELU_C * (1.0 + 3.0 * 0.044715 * (pre * pre))
    )
    d_pre = (slope * dot_nn(d_b3, w_down)).astype(BF16)
    dpre_o[...] = d_pre
    d_m = dot_nt(d_pre, w_up).astype(BF16)
    for r in range(tp):
        dm_o[r][...] = d_m[r * own : (r + 1) * own]
    b3 = dot_nt(hidden, w_down).astype(BF16)
    for r in range(tp):
        b3_o[r][...] = b3[r * own : (r + 1) * own]


def second_back(tp, *refs):
    d_m = refs[0][...].astype(F32)
    for r in refs[1:tp]:
        d_m = d_m + r[...].astype(F32)
    x2, cot, live, hot, mods, g2_o, db2_o, sums_o = refs[tp:]
    n, inv = norm_parts(x2[...])
    grad = d_m * (1.0 + expand(hot[...], mods[4]))
    g2 = cot[...].astype(F32) * live[...] + norm_back(grad, n, inv)
    g2_o[...] = g2
    db2_o[...] = g2.astype(BF16)
    sums_o[0] = clip_sums(hot[...], d_m)
    sums_o[1] = clip_sums(hot[...], d_m * n)


def out_rows(tp, *refs):
    b3 = refs[0][...].astype(F32)
    for r in refs[1:tp]:
        b3 = b3 + r[...].astype(F32)
    x2, cot, live, hot, mods, out_o, sums_o = refs[tp:]
    third = x2[...] + expand(hot[...], mods[5]) * b3
    out_o[...] = (third * live[...]).astype(BF16)
    sums_o[...] = clip_sums(hot[...], cot[...].astype(F32) * live[...] * b3)


def cross_back(tp, inner, *refs):
    d_b2 = jnp.concatenate([r[...] for r in refs[:tp]], axis=0)
    w_out2, prob, kv, cq, db2_o, dcq_o, dkv_o, pack_o = refs[tp:]
    db2_o[...] = d_b2
    d_co = dot_nn(d_b2, w_out2[...]).astype(BF16)
    d_q, d_k, d_v = [], [], []
    for h in range(inner // HDIM):
        cols = slice(h * HDIM, (h + 1) * HDIM)
        key = kv[:, h * HDIM : (h + 1) * HDIM]
        value = kv[:, inner + h * HDIM : inner + (h + 1) * HDIM]
        probs = prob[h]
        d_v.append(dot_tn(probs, d_co[:, cols]).astype(BF16))
        d_p = dot_nt(d_co[:, cols], value)
        wide = probs.astype(F32)
        d_s = (wide * (d_p - jnp.sum(wide * d_p, -1, keepdims=True))).astype(BF16)
        d_q.append((dot_nn(d_s, key) * SCALE).astype(BF16))
        d_k.append((dot_tn(d_s, cq[:, cols]) * SCALE).astype(BF16))
    result = jnp.concatenate(d_q, axis=1)
    dcq_o[...] = result
    pack_rows(pack_o, result, tp)
    dkv_o[...] = jnp.concatenate(d_k + d_v, axis=1)


def frame_back(tp, inner, *refs):
    pieces = [r[...] for r in refs[:tp]]
    rest = refs[tp:]
    d_b2, g2, own_b1, tok, hot, mods, w_b, w_q2, w_qkv, qkv, prob = rest[:11]
    outs = rest[11:]
    g1_o, db1_o, dqkv_o, sums_o = outs[:4]
    da_o = outs[4:]
    own, width = g1_o.shape
    d_cq = unpack_heads(pieces, tp, inner)
    d_x1 = dot_nt(d_cq[:, :inner], w_b[:, width + 2 * inner : width + 3 * inner]) + dot_nt(d_cq[:, inner:], w_q2[...])
    g1_own = g2[...] + d_x1[:own]
    g1_o[...] = g1_own
    d_b1 = (expand(hot[...], mods[2]) * (d_b2[...].astype(F32) + d_x1)).astype(BF16)
    db1_o[...] = d_b1
    d_fo = dot_nn(d_b1, w_b[:, :inner]).astype(BF16)
    d_q, d_k, d_v = [], [], []
    for h in range(inner // HDIM):
        q, k, v = (qkv[:, i * inner + h * HDIM : i * inner + (h + 1) * HDIM] for i in range(3))
        grad = d_fo[:, h * HDIM : (h + 1) * HDIM]
        probs = prob[h]
        d_v.append(dot_tn(probs, grad).astype(BF16))
        d_p = dot_nt(grad, v)
        wide = probs.astype(F32)
        d_s = (wide * (d_p - jnp.sum(wide * d_p, -1, keepdims=True))).astype(BF16)
        d_q.append((dot_nn(d_s, k) * SCALE).astype(BF16))
        d_k.append((dot_tn(d_s, q) * SCALE).astype(BF16))
    d_qkv = jnp.concatenate(d_q + d_k + d_v, axis=1)
    dqkv_o[...] = d_qkv
    d_a = dot_nt(d_qkv, w_qkv[...])
    low = d_a.astype(BF16)
    for r in range(tp):
        da_o[r][...] = low[r * own : (r + 1) * own]
    n, _ = norm_parts(tok[...].astype(F32))
    sums_o[0] = dot_tn(hot[...], low)
    sums_o[1] = clip_sums(hot[...], d_a * n)
    sums_o[2] = clip_sums(hot[:own], g1_own * own_b1[...])


def token_rows(tp, *refs):
    d_a = refs[0][...].astype(F32)
    for r in refs[1:tp]:
        d_a = d_a + r[...].astype(F32)
    tok, g1, hot, mods, out_o = refs[tp:]
    n, inv = norm_parts(tok[...].astype(F32))
    grad = d_a * (1.0 + expand(hot[...], mods[1]))
    out_o[...] = (g1[...] + norm_back(grad, n, inv)).astype(BF16)


def weight_grads(*refs):
    out_o = refs[-1]
    start = 0
    for i in range(0, len(refs) - 1, 2):
        width = refs[i + 1].shape[1]
        out_o[:, start : start + width] = dot_tn(refs[i][...], refs[i + 1][...]).astype(BF16)
        start += width


def weight_grads_relative(rank, *refs):
    out_o = refs[-1]
    blocks, size = out_o.shape[0], out_o.shape[1]
    start = 0
    for i in range(0, len(refs) - 1, 2):
        width = refs[i + 1].shape[1]
        grads = dot_tn(refs[i][...], refs[i + 1][...]).astype(BF16)
        for s in range(blocks):
            other = lax.bitwise_xor(rank[0], s)
            place = (other % 2) * (blocks // 2) + other // 2
            out_o[place, :, start : start + width] = grads[s * size : (s + 1) * size]
        start += width


def caption_rows(tp, rank, dkv, w_kv, out_o):
    size = out_o.shape[2]
    for r in range(tp):
        block = lax.rem(rank[0] - r + tp, tp)
        rows = w_kv[pl.ds(pl.multiple_of(block * size, size), size), :]
        out_o[r] = dot_nt(dkv[...], rows).astype(BF16)


def tp_gather(value, tp):
    return [value] + [
        lax.ppermute(value, "tp", [(i, (i + k) % tp) for i in range(tp)]) for k in range(1, tp)
    ]


def tp_scatter(chunks, tp):
    return [chunks[0]] + [
        lax.ppermute(chunks[r], "tp", [(i, (i - r) % tp) for i in range(tp)]) for r in range(1, tp)
    ]


def seq_xor(value, mask, nseq):
    return lax.ppermute(value, "seq", [(i, i ^ mask) for i in range(nseq)])


def seq_total(value, nseq):
    mask = 1
    while mask < nseq:
        value = value + seq_xor(value, mask, nseq)
        mask *= 2
    return value


def padded(value, size, axis):
    if value.shape[axis] == size:
        return value
    pads = [(0, 0)] * value.ndim
    pads[axis] = (0, size - value.shape[axis])
    return jnp.pad(value, pads)


def shards(
    tokens,
    cotangent,
    caption,
    condition,
    frames,
    cap_len,
    clip_of,
    w_qkv,
    w_out,
    w_query2,
    w_kv2,
    w_out2,
    w_up,
    w_down,
    w_ada,
):
    tp, nseq = lax.axis_size("tp"), lax.axis_size("seq")
    me, spot = lax.axis_index("tp"), lax.axis_index("seq")
    seqs, fmax, width = tokens.shape
    clips, slots = caption.shape[:2]
    inner, hid = w_query2.shape[1], w_up.shape[1]
    heads = inner // HDIM
    drows = w_query2.shape[0]
    own_seqs = seqs // tp
    own = -(-own_seqs * fmax // 8) * 8
    rows = tp * own
    clip_pad = 8
    keys = -(-(clips * slots // 2) // 128) * 128

    z_pack = jnp.concatenate([w_out.T, w_query2, w_out2.T], axis=1)
    z_parts = tp_gather(z_pack, tp)
    z_out, z_q2, z_out2 = (
        [p[:, i * inner : (i + 1) * inner] for p in z_parts] for i in range(3)
    )
    section = padded(jnp.concatenate([w_kv2.reshape(drows, 2 * inner), w_query2], 1), width, 1)
    pack_a = w_qkv.reshape(drows, 3 * inner)
    pack_b = jnp.concatenate(z_out + [section], axis=1)
    pack_c = jnp.concatenate(z_out2 + [w_up, w_down.T], axis=1)
    pack_d = jnp.concatenate(z_q2[1:], axis=1)
    full_a = lax.all_gather(pack_a, "seq", axis=0, tiled=True)
    full_b = lax.all_gather(pack_b, "seq", axis=0, tiled=True)
    full_c = lax.all_gather(pack_c, "seq", axis=0, tiled=True)
    full_d = lax.all_gather(pack_d, "seq", axis=0, tiled=True)
    full_kv = full_b[:, width : width + 2 * inner]
    own_out2 = full_c[:, :inner]

    scaled = jax.nn.silu(condition).astype(BF16)
    scaled_own = lax.dynamic_slice_in_dim(scaled, spot * drows, drows, 1)
    mod_part = seq_total(jnp.dot(scaled_own, w_ada, preferred_element_type=F32), nseq)
    mod_parts = tp_gather(mod_part, tp)
    mod_all = jnp.zeros((tp,) + mod_part.shape, F32)
    for k in range(tp):
        mod_all = lax.dynamic_update_index_in_dim(mod_all, mod_parts[k], (me - k) % tp, 0)
    mods = mod_all.transpose(1, 0, 2).reshape(clips, 6, width).transpose(1, 0, 2)
    mods = padded(mods, clip_pad, 1)

    def relative(value):
        parts = [
            lax.dynamic_slice_in_dim(value, ((me - k) % tp) * own_seqs, own_seqs, 0)
            for k in range(tp)
        ]
        return jnp.stack(parts)

    def row_form(value, fill=0):
        flat = relative(value).reshape((tp, own_seqs * fmax) + value.shape[2:])
        pads = [(0, 0), (0, own - own_seqs * fmax)] + [(0, 0)] * (flat.ndim - 2)
        flat = jnp.pad(flat, pads, constant_values=fill)
        return flat.reshape((rows,) + value.shape[2:])

    tok = row_form(tokens)
    cot = row_form(cotangent)
    ids = jnp.arange(clips)
    seq_hot = clip_of[:, None] == ids[None, :]
    seq_frames = jnp.sum(jnp.where(seq_hot, frames[None, :], 0), 1)
    live2 = jnp.arange(fmax)[None, :] < seq_frames[:, None]
    seq_index = jnp.broadcast_to(jnp.arange(seqs)[:, None], live2.shape)
    row_clip = row_form(jnp.broadcast_to(clip_of[:, None], live2.shape), -1)
    live = row_form(live2.astype(F32))[:, None]
    row_id = row_form(seq_index, -1)[:, None]
    key_id = row_form(jnp.where(live2, seq_index, -2), -2)[None, :]
    hot = (row_clip[:, None] == jnp.arange(clip_pad)[None, :]).astype(BF16)
    row_clip = row_clip[:, None]

    starts = jnp.cumsum(cap_len) - cap_len
    place = jnp.arange(keys)
    key_clip = jnp.sum((place[:, None] >= starts[None, :]).astype(jnp.int32), 1) - 1
    key_clip = jnp.where(place < jnp.sum(cap_len), key_clip, -9)[None, :]
    cap = jnp.zeros((keys + slots, width), BF16)
    for c in range(clips):
        cap = lax.dynamic_update_slice_in_dim(cap, caption[c], starts[c], 0)
    cap = jnp.where((place < jnp.sum(cap_len))[:, None], cap[:keys], 0)

    attn_in, qkv, probs, frame_out, frame_pack = call(
        functools.partial(frame_forward, tp),
        [
            sds((rows, width)),
            sds((rows, 3 * inner)),
            sds((heads, rows, rows)),
            sds((rows, inner)),
            sds((own, tp * inner)),
        ],
        tok,
        hot,
        mods,
        row_id,
        key_id,
        full_a,
        name="frame_forward",
    )
    (kv,) = call(
        key_values,
        [sds((keys, 2 * inner))],
        cap,
        full_kv,
        name="key_values",
    )
    frame_parts = tp_gather(frame_pack, tp)
    first, first_low, own_b1, cq, cprobs, cross_out, cross_pack = call(
        functools.partial(cross_forward, tp, inner),
        [
            sds((rows, width), F32),
            sds((rows, width)),
            sds((own, width), F32),
            sds((rows, inner)),
            sds((heads, rows, keys)),
            sds((rows, inner)),
            sds((own, tp * inner)),
        ],
        *frame_parts,
        tok,
        hot,
        mods,
        row_clip,
        key_clip,
        full_b,
        kv,
        name="cross_forward",
    )
    cross_parts = tp_gather(cross_pack, tp)
    outs = call(
        functools.partial(mlp_both, tp, inner),
        [sds((own, width), F32), sds((rows, width)), sds((rows, hid)), sds((rows, width)), sds((rows, hid))]
        + [sds((own, width))] * (2 * tp),
        *cross_parts,
        first,
        cot,
        live,
        hot,
        mods,
        full_c,
        name="mlp_both",
    )
    x2_own, mlp_in, hidden, d_b3, d_pre = outs[:5]
    b3_chunks, dm_chunks = outs[5 : 5 + tp], outs[5 + tp :]
    cot_own, live_own, hot_own, tok_own = cot[:own], live[:own], hot[:own], tok[:own]

    dm_parts = tp_scatter(dm_chunks, tp)
    g2_own, db2_own, sums_two = call(
        functools.partial(second_back, tp),
        [sds((own, width), F32), sds((own, width)), sds((2, clip_pad, width), F32)],
        *dm_parts,
        x2_own,
        cot_own,
        live_own,
        hot_own,
        mods,
        name="second_back",
    )
    (grad_one,) = call(
        weight_grads,
        [sds((width, 2 * hid))],
        mlp_in,
        d_pre,
        d_b3,
        hidden,
        name="grads_mlp",
    )
    sum_one = lax.psum_scatter(grad_one, "seq", scatter_dimension=0, tiled=True)
    db2_parts = tp_gather(db2_own, tp)
    d_b2, d_cq, d_kv, dcq_pack = call(
        functools.partial(cross_back, tp, inner),
        [sds((rows, width)), sds((rows, inner)), sds((keys, 2 * inner)), sds((own, tp * inner))],
        *db2_parts,
        own_out2,
        cprobs,
        kv,
        cq,
        name="cross_back",
    )
    dcq_parts = tp_gather(dcq_pack, tp)
    b3_parts = tp_scatter(b3_chunks, tp)
    out_own, sum_gate2 = call(
        functools.partial(out_rows, tp),
        [sds((own, width)), sds((clip_pad, width), F32)],
        *b3_parts,
        x2_own,
        cot_own,
        live_own,
        hot_own,
        mods,
        name="out_rows",
    )
    out_parts = tp_gather(out_own, tp)
    outs = call(
        functools.partial(frame_back, tp, inner),
        [
            sds((own, width), F32),
            sds((rows, width)),
            sds((rows, 3 * inner)),
            sds((3, clip_pad, width), F32),
        ]
        + [sds((own, width))] * tp,
        *dcq_parts,
        d_b2,
        g2_own,
        own_b1,
        tok,
        hot,
        mods,
        full_b,
        full_d,
        full_a,
        qkv,
        probs,
        name="frame_back",
    )
    g1_own, d_b1, d_qkv, sums_one = outs[:4]
    da_parts = tp_scatter(outs[4:], tp)
    (dtok_own,) = call(
        functools.partial(token_rows, tp),
        [sds((own, width))],
        *da_parts,
        tok_own,
        g1_own,
        hot_own,
        mods,
        name="token_rows",
    )
    dtok_parts = tp_gather(dtok_own, tp)

    def canonical(parts):
        whole = jnp.zeros((tp, own_seqs, fmax, width), BF16)
        for k in range(tp):
            part = parts[k][: own_seqs * fmax].reshape(own_seqs, fmax, width)
            whole = lax.dynamic_update_index_in_dim(whole, part, (me - k) % tp, 0)
        return whole.reshape(seqs, fmax, width)

    output = canonical(out_parts)
    d_tokens = canonical(dtok_parts)

    (grad_two,) = call(
        weight_grads,
        [sds((width, 4 * inner))],
        first_low,
        d_cq,
        cap,
        d_kv,
        d_b2,
        cross_out,
        name="grads_cross",
    )
    sum_two = lax.psum_scatter(grad_two, "seq", scatter_dimension=0, tiled=True)
    smem = pl.BlockSpec(memory_space=pltpu.SMEM)
    (grad_three,) = call(
        weight_grads_relative,
        [sds((nseq, drows, 4 * inner))],
        spot.reshape(1).astype(jnp.int32),
        attn_in,
        d_qkv,
        d_b1,
        frame_out,
        specs=[smem, None, None, None, None],
        name="grads_frame",
    )
    half = nseq // 2
    away = seq_xor(grad_three[half:], 1, nseq)
    near = (grad_three[:half].astype(F32) + away.astype(F32)).astype(BF16)
    sum_three = near[0].astype(F32)
    for c in range(1, half):
        sum_three = sum_three + seq_xor(near[c], 2 * c, nseq).astype(F32)

    grad_up = sum_one[:, :hid].astype(F32)
    grad_down = sum_one[:, hid:].astype(F32).T
    grad_q2 = sum_two[:, :inner].astype(F32)
    grad_kv2 = sum_two[:, inner : 3 * inner].astype(F32).reshape(drows, 2, inner)
    grad_out2 = sum_two[:, 3 * inner :].astype(F32).T
    grad_qkv = sum_three[:, : 3 * inner].reshape(drows, 3, inner)
    grad_out = sum_three[:, 3 * inner :].T

    kv_own = lax.psum_scatter(d_kv, "seq", scatter_dimension=0, tiled=True)
    feats = width // tp
    (cap_chunks,) = call(
        functools.partial(caption_rows, tp),
        [sds((tp, keys // nseq, feats))],
        me.reshape(1).astype(jnp.int32),
        kv_own,
        full_kv,
        specs=[smem, None, None],
        name="caption_rows",
    )
    cap_parts = tp_scatter([cap_chunks[r] for r in range(tp)], tp)
    cap_own = sum(p.astype(F32) for p in cap_parts).astype(BF16)
    cap_all = lax.all_gather(cap_own, "seq", axis=0, tiled=True)
    cap_all = jnp.pad(cap_all, ((0, slots), (0, 0)))
    d_caption = jnp.stack(
        [
            jnp.where(
                (jnp.arange(slots) < cap_len[c])[:, None],
                lax.dynamic_slice_in_dim(cap_all, starts[c], slots, 0).astype(F32),
                0.0,
            )
            for c in range(clips)
        ]
    )

    sums = jnp.stack(
        [sums_one[0], sums_one[1], sums_one[2], sums_two[0], sums_two[1], sum_gate2]
    )[:, :clips]
    d_mods = sums.transpose(1, 0, 2).reshape(clips, tp, 6 * width // tp)
    chunks = [lax.dynamic_index_in_dim(d_mods, (me - r) % tp, 1, False) for r in range(tp)]
    mod_cols = seq_total(sum(tp_scatter(chunks, tp)), nseq)
    grad_ada = lax.dot_general(
        scaled_own.astype(F32), mod_cols, (((0,), (0,)), ((), ())), precision=lax.Precision.HIGHEST
    )
    cond_part = lax.dot_general(
        mod_cols, w_ada.astype(F32), (((1,), (1,)), ((), ())), precision=lax.Precision.HIGHEST
    )
    cond_part = sum(tp_gather(cond_part, tp))
    cond_wide = lax.dynamic_update_slice_in_dim(
        jnp.zeros((clips, width), F32), cond_part, spot * drows, 1
    )
    cond_all = seq_total(cond_wide, nseq)
    d_condition = jax.vjp(jax.nn.silu, condition)[1](cond_all)[0]

    return (
        output,
        d_tokens,
        d_caption,
        d_condition,
        grad_qkv,
        grad_out,
        grad_q2,
        grad_kv2,
        grad_out2,
        grad_up,
        grad_down,
        grad_ada,
    )


def solution(mesh):
    return jax.shard_map(
        shards,
        mesh=mesh,
        in_specs=(
            P("seq", None, None),
            P("seq", None, None),
            P(),
            P(),
            P(),
            P(),
            P("seq"),
            P("seq", None, "tp"),
            P("tp", "seq"),
            P("seq", "tp"),
            P("seq", None, "tp"),
            P("tp", "seq"),
            P("seq", "tp"),
            P("tp", "seq"),
            P("seq", "tp"),
        ),
        out_specs=(
            P("seq", None, None),
            P("seq", None, None),
            P(None, None, "tp"),
            P(),
            P("seq", None, "tp"),
            P("tp", "seq"),
            P("seq", "tp"),
            P("seq", None, "tp"),
            P("tp", "seq"),
            P("seq", "tp"),
            P("tp", "seq"),
            P("seq", "tp"),
        ),
        check_vma=False,
    )
```

```python
import functools

import jax
import jax.numpy as jnp
from jax import lax
from jax.experimental import pallas as pl
from jax.experimental.pallas import tpu as pltpu
from jax.sharding import PartitionSpec as P

HDIM = 72
EPSILON = 1e-06
NEG_FILL = -1e30
F32 = jnp.float32
BF16 = jnp.bfloat16
SCALE = HDIM ** (-0.5)
VMEM_LIMIT = 48 << 20


def dot_nn(a, b):
    return lax.dot_general(a, b, (((1,), (0,)), ((), ())), preferred_element_type=F32)


def dot_nt(a, b):
    return lax.dot_general(a, b, (((1,), (1,)), ((), ())), preferred_element_type=F32)


def dot_tn(a, b):
    return lax.dot_general(a, b, (((0,), (0,)), ((), ())), preferred_element_type=F32)


def sds(shape, dtype=BF16):
    return jax.ShapeDtypeStruct(shape, dtype)


class Blocks:
    def __init__(self, pieces):
        self.pieces = pieces


class Cols:
    def __init__(self, whole, start, size):
        self.whole, self.start, self.size = whole, start, size


class Near:
    def __init__(self, whole):
        self.whole = whole


class Split:
    def __init__(self, parts, blocks, width):
        self.parts, self.blocks, self.width = parts, blocks, width


class In:
    def __init__(self, buf, copies):
        self.buf, self.copies, self.ready = buf, copies, not copies

    @property
    def shape(self):
        return self.buf.shape

    def __getitem__(self, index):
        if not self.ready:
            for copy in self.copies:
                copy.wait()
            self.ready = True
        return self.buf[index]


class Out:
    def __init__(self, bufs, copies):
        self.bufs, self.copies, self.sent = bufs, copies, False

    @property
    def shape(self):
        return self.bufs[0].shape

    def __getitem__(self, index):
        return self.bufs[0][index]

    def __setitem__(self, index, value):
        self.bufs[0][index] = value

    def send(self):
        if not self.sent:
            for copy in self.copies:
                copy.start()
            self.sent = True


def call(body, outs, ins, *, name, smem=(), order=(), limit=VMEM_LIMIT):
    vmem, hbm = pl.BlockSpec(memory_space=pltpu.VMEM), pl.BlockSpec(memory_space=pltpu.HBM)
    pin = lambda value: pltpu.with_memory_space_constraint(value, pltpu.HBM)
    ops, in_specs, in_plan, scratch_in = [], [], [], []
    n_in = 0
    for arg in ins:
        if isinstance(arg, Near):
            in_plan.append((len(ops), None, arg, 0))
            ops.append(arg.whole)
            in_specs.append(vmem)
            continue
        pieces = arg.pieces if isinstance(arg, Blocks) else [arg.whole if isinstance(arg, Cols) else arg]
        shape = pieces[0].shape
        if isinstance(arg, Blocks):
            shape = (shape[0] * len(pieces),) + shape[1:]
        elif isinstance(arg, Cols):
            shape = (shape[0], arg.size)
        in_plan.append((len(ops), len(scratch_in), arg, n_in))
        scratch_in.append(pltpu.VMEM(shape, pieces[0].dtype))
        n_in += len(pieces)
        ops += [pin(p) for p in pieces]
        in_specs += [hbm] * len(pieces)
    n_read = len(ops)
    for arg in order:
        ops.append(arg.whole if isinstance(arg, Near) else pin(arg))
        in_specs.append(vmem if isinstance(arg, Near) else hbm)
    results, out_plan, scratch_out = [], [], []
    n_out = 0
    for out in outs:
        out_plan.append((len(results), len(scratch_out), out, n_out))
        if isinstance(out, Split):
            half = out.blocks // 2
            results += [sds((half, sum(out.parts), out.width))] * 2
            scratch_out += [pltpu.VMEM((out.blocks, p, out.width), BF16) for p in out.parts]
            n_out += len(out.parts) * out.blocks
        else:
            results.append(out)
            scratch_out.append(pltpu.VMEM(out.shape, out.dtype))
            n_out += 1
    n_s, n_i, n_o = len(smem), len(ops), len(results)

    def kernel(*refs):
        scalars = refs[:n_s]
        src = refs[n_s : n_s + n_read]
        dst = refs[n_s + n_i : n_s + n_i + n_o]
        scratch = refs[n_s + n_i + n_o :]
        bufs = scratch[: len(scratch_in)]
        obufs = scratch[len(scratch_in) : len(scratch_in) + len(scratch_out)]
        in_sem, out_sem = scratch[-2:]
        lazy = []
        for start, at, arg, sem in in_plan:
            if at is None:
                lazy.append(In(src[start], []))
                continue
            copies = []
            if isinstance(arg, Blocks):
                rows = src[start].shape[0]
                for m in range(len(arg.pieces)):
                    block = lax.bitwise_xor(scalars[0][1], m)
                    place = bufs[at].at[pl.ds(pl.multiple_of(block * rows, 8), rows)]
                    copies.append(pltpu.make_async_copy(src[start + m], place, in_sem.at[sem + m]))
            else:
                part = src[start]
                if isinstance(arg, Cols):
                    part = part.at[:, pl.ds(arg.start, arg.size)]
                copies.append(pltpu.make_async_copy(part, bufs[at], in_sem.at[sem]))
            for copy in copies:
                copy.start()
            lazy.append(In(bufs[at], copies))
        made = []
        for first, at, out, sem in out_plan:
            if not isinstance(out, Split):
                copy = pltpu.make_async_copy(obufs[at], dst[first], out_sem.at[sem])
                made.append(Out([obufs[at]], [copy]))
                continue
            copies = []
            row = 0
            for j, part in enumerate(out.parts):
                for c in range(out.blocks // 2):
                    for h in range(2):
                        block = lax.bitwise_xor(scalars[0][1], 2 * c + 1 - h)
                        copies.append(
                            pltpu.make_async_copy(
                                obufs[at + j].at[block],
                                dst[first + h].at[c, pl.ds(row, part)],
                                out_sem.at[sem],
                            )
                        )
                        sem += 1
                row += part
            made.append(Out(obufs[at : at + len(out.parts)], copies))
        body(scalars, lazy, made)
        for item in lazy:
            if not item.ready:
                item[...]
        for out in made:
            out.send()
        for out in made:
            for copy in out.copies:
                copy.wait()

    moved = sum(a.size * a.dtype.itemsize for a in ops[:n_read])
    moved += sum(o.size * jnp.dtype(o.dtype).itemsize for o in results)
    return pl.pallas_call(
        kernel,
        out_shape=tuple(pltpu.HBM(o.shape, o.dtype) for o in results),
        in_specs=[pl.BlockSpec(memory_space=pltpu.SMEM)] * n_s + in_specs,
        out_specs=tuple([hbm] * n_o),
        scratch_shapes=scratch_in
        + scratch_out
        + [pltpu.SemaphoreType.DMA((max(n_in, 1),)), pltpu.SemaphoreType.DMA((max(n_out, 1),))],
        compiler_params=pltpu.CompilerParams(vmem_limit_bytes=limit),
        cost_estimate=pl.CostEstimate(flops=0, transcendentals=0, bytes_accessed=moved),
        name=name,
    )(*smem, *ops)


def norm_parts(rows):
    center = rows - jnp.mean(rows, -1, keepdims=True)
    inv = lax.rsqrt(jnp.mean(center * center, -1, keepdims=True) + EPSILON)
    return center * inv, inv


def expand(hot, table):
    high = table.astype(BF16)
    low = (table - high.astype(F32)).astype(BF16)
    return dot_nn(hot, high) + dot_nn(hot, low)


def split_dot(dot, a, b):
    high = a.astype(BF16)
    low = (a - high.astype(F32)).astype(BF16)
    return dot(high, b) + dot(low, b)


def clip_sums(clips_hot, values):
    return dot_nn(clips_hot, values.astype(BF16))


def norm_back(grad, n, inv):
    return inv * (grad - jnp.mean(grad, -1, keepdims=True) - n * jnp.mean(grad * n, -1, keepdims=True))


def softmax_rows(scores):
    top = jnp.max(scores, -1, keepdims=True)
    weights = jnp.exp(scores - top)
    return weights / jnp.sum(weights, -1, keepdims=True)


def pack_rows(out, value, tp):
    own, n = value.shape[0] // tp, value.shape[1]
    for r in range(tp):
        out[:, r * n : (r + 1) * n] = value[r * own : (r + 1) * own]


def unpack_heads(pieces, tp, n):
    pieces = [p[...] for p in pieces]
    rows = []
    for b in range(tp):
        cols = []
        for k in range(tp):
            r = (b - k) % tp
            cols.append(pieces[k][:, r * n : (r + 1) * n])
        rows.append(jnp.concatenate(cols, axis=1))
    return jnp.concatenate(rows, axis=0)


def far(parts):
    return [parts[0]] + [Near(p) for p in parts[1:]]


def total(parts):
    value = parts[0][...].astype(F32)
    for part in parts[1:]:
        value = value + part[...].astype(F32)
    return value


def prepare_rows(tp, fmax, scalars, ins, outs):
    rank, clip_of, frames = scalars
    tokens, cotangent = ins
    tok_o, g3_o, hot_o, clip_o, id_o, key_o, live_o, turned_o = outs
    rows, width = tok_o.shape
    own = rows // tp
    own_seqs = tokens.shape[0] // tp
    spare = own - own_seqs * fmax
    place = lax.broadcasted_iota(jnp.int32, key_o.shape, 1)
    keys = jnp.full(key_o.shape, -2, jnp.int32)
    owner = jnp.full(key_o.shape, -1, jnp.int32)
    frame = lax.broadcasted_iota(jnp.int32, (fmax, 1), 0)
    lane = lax.broadcasted_iota(jnp.int32, (fmax, hot_o.shape[1]), 1)
    for k in range(tp):
        base = lax.rem(rank[0] - k + tp, tp) * own_seqs
        parts = [[] for _ in range(6)]
        for j in range(own_seqs):
            clip = clip_of[base + j]
            count = frames[clip]
            alive = (frame < count).astype(F32)
            parts[0].append(tokens[base + j].astype(F32))
            parts[1].append(cotangent[base + j].astype(F32) * alive)
            parts[2].append(jnp.where(lane == clip, 1.0, 0.0))
            parts[3].append(jnp.full((fmax, 1), 0, jnp.int32) + clip)
            parts[4].append(jnp.full((fmax, 1), k * own_seqs + j, jnp.int32))
            parts[5].append(alive)
            start = k * own + j * fmax
            keys = jnp.where((place >= start) & (place < start + count), k * own_seqs + j, keys)
            owner = jnp.where((place >= start) & (place < start + fmax), clip, owner)
        for out, part, fill in zip((tok_o, g3_o, hot_o, clip_o, id_o, live_o), parts, (0, 0, 0, -1, -1, 0)):
            if spare:
                part.append(jnp.full((spare, part[0].shape[1]), fill, part[0].dtype))
            value = jnp.concatenate(part, axis=0).astype(out.bufs[0].dtype)
            out[k * own : (k + 1) * own] = value
    key_o[...] = keys
    which = lax.broadcasted_iota(jnp.int32, turned_o.shape, 0)
    turned_o[...] = jnp.where(which == owner, 1.0, 0.0).astype(BF16)


def live_captions(scalars, ins, outs):
    (cap_len,) = scalars
    (caption,) = ins
    cap_o, clip_o = outs
    keys = cap_o.shape[0]
    clips, slots = caption.shape[:2]
    row = lax.broadcasted_iota(jnp.int32, (keys, 1), 0)
    col = lax.broadcasted_iota(jnp.int32, (1, keys), 1)
    slot = lax.broadcasted_iota(jnp.int32, (keys, slots), 1)
    clip = jnp.full((1, keys), -9, jnp.int32)
    start = jnp.int32(0)
    value = jnp.zeros(cap_o.shape, F32)
    for c in range(clips):
        end = start + cap_len[c]
        clip = jnp.where((col >= start) & (col < end), c, clip)
        pick = (row - start == slot) & (row >= start) & (row < end)
        value = value + dot_nn(jnp.where(pick, 1.0, 0.0).astype(BF16), caption[c])
        start = end
    cap_o[...] = value.astype(BF16)
    clip_o[...] = clip


def modulations(tp, clips, first, scalars, ins, outs):
    (rank,) = scalars
    (mods_o,) = outs
    width = mods_o.shape[2]
    groups = (ins[0].shape[0] - first) // (2 * clips)

    def joined(ref):
        cols = []
        for g in range(groups):
            at = first + g * clips
            high = ref[at : at + clips].astype(F32)
            cols.append(high + ref[at + groups * clips : at + (groups + 1) * clips].astype(F32))
        return jnp.concatenate(cols, axis=1)

    parts = [joined(ref) for ref in ins]
    cols = []
    for q in range(tp):
        value = parts[0]
        for k in range(1, tp):
            value = jnp.where(lax.rem(rank[0] - k + tp, tp) == q, parts[k], value)
        cols.append(value)
    whole = jnp.concatenate(cols, axis=1)
    mods_o[...] = jnp.zeros(mods_o.shape, F32)
    for j in range(6):
        mods_o[j, :clips] = whole[:, j * width : (j + 1) * width]


def frame_forward(tp, scalars, ins, outs):
    tok, hot, mods, row_id, key_id, w_a = ins
    attn_o, qkv_o, prob_o, fo_o = outs[:4]
    branch_o = outs[4:]
    inner = fo_o.shape[1]
    own = branch_o[0].shape[0]
    n, _ = norm_parts(tok[...].astype(F32))
    low = (n * (1.0 + expand(hot[...], mods[1])) + expand(hot[...], mods[0])).astype(BF16)
    attn_o[...] = low
    attn_o.send()
    qkv = dot_nn(low, w_a[:, : 3 * inner]).astype(BF16)
    qkv_o[...] = qkv
    qkv_o.send()
    allowed = row_id[...] == key_id[...]
    made = []
    for h in range(inner // HDIM):
        q, k, v = (qkv[:, i * inner + h * HDIM : i * inner + (h + 1) * HDIM] for i in range(3))
        probs = softmax_rows(jnp.where(allowed, dot_nt(q, k) * SCALE, NEG_FILL)).astype(BF16)
        prob_o[h] = probs
        made.append(dot_nn(probs, v).astype(BF16))
    result = jnp.concatenate(made, axis=1)
    prob_o.send()
    fo_o[...] = result
    fo_o.send()
    branch = dot_nt(result, w_a[:, 3 * inner : 4 * inner]).astype(BF16)
    for r in range(tp):
        branch_o[r][...] = branch[r * own : (r + 1) * own]
        branch_o[r].send()


def first_rows(tp, scalars, ins, outs):
    tok, hot, mods = ins[tp:]
    x1_o, low_o, branch_o = outs
    own = x1_o.shape[0]
    gate = expand(hot[:own], mods[2])
    branch = total(ins[:tp])
    branch_o[...] = branch
    branch_o.send()
    first = tok[:own].astype(F32) + gate * branch
    x1_o[...] = first
    low_o[...] = first.astype(BF16)


def key_values(scalars, ins, outs):
    cap, w_kv = ins
    (kv_o,) = outs
    kv_o[...] = dot_nn(cap[...], w_kv[...]).astype(BF16)


def cross_forward(tp, inner, scalars, ins, outs):
    row_clip, key_clip, w_q2, kv = ins[tp:]
    low_o, cq_o, prob_o, co_o, pack_o = outs
    low = jnp.concatenate([r[...] for r in ins[:tp]], axis=0)
    low_o[...] = low
    low_o.send()
    cq = dot_nn(low, w_q2[:, :inner]).astype(BF16)
    cq_o[...] = cq
    cq_o.send()
    allowed = row_clip[...] == key_clip[...]
    made = []
    for h in range(inner // HDIM):
        cols = slice(h * HDIM, (h + 1) * HDIM)
        key = kv[:, h * HDIM : (h + 1) * HDIM]
        value = kv[:, inner + h * HDIM : inner + (h + 1) * HDIM]
        scores = jnp.where(allowed, dot_nt(cq[:, cols], key) * SCALE, NEG_FILL)
        probs = softmax_rows(scores).astype(BF16)
        prob_o[h] = probs
        made.append(dot_nn(probs, value).astype(BF16))
    result = jnp.concatenate(made, axis=1)
    pack_rows(pack_o, result, tp)
    pack_o.send()
    prob_o.send()
    co_o[...] = result


GELU_C = 0.7978845608028654


def mlp_both(tp, inner, scalars, ins, outs):
    pieces = ins[:tp]
    first, low_first, g3, hot, mods, w_out2, w_up, w_down, turned = ins[tp:]
    x2_o, mlp_o, hid_o, db3_o, dpre_o, sums_o = outs[:6]
    dm_o, b3_o = outs[6 : 6 + tp], outs[6 + tp :]
    own, width = x2_o.shape
    d_b3 = (expand(hot[...], mods[5]) * g3[...].astype(F32)).astype(BF16)
    db3_o[...] = d_b3
    db3_o.send()
    rows = unpack_heads(pieces, tp, inner)
    branch = dot_nt(rows, w_out2[...])
    second = jnp.concatenate(
        [first[...] + branch[:own], low_first[own:].astype(F32) + branch[own:]], axis=0
    )
    x2_o[...] = second[:own]
    x2_o.send()
    n, _ = norm_parts(second)
    low = (n * (1.0 + expand(hot[...], mods[4])) + expand(hot[...], mods[3])).astype(BF16)
    mlp_o[...] = low
    mlp_o.send()
    hid = hid_o.shape[1]
    pre = dot_nn(low, w_up[:, :hid])
    inside = GELU_C * (pre + 0.044715 * (pre * pre * pre))
    th = jnp.tanh(inside)
    hidden = (0.5 * pre * (1.0 + th)).astype(BF16)
    hid_o[...] = hidden
    hid_o.send()
    slope = 0.5 * (1.0 + th) + 0.5 * pre * (1.0 - th * th) * (
        GELU_C * (1.0 + 3.0 * 0.044715 * (pre * pre))
    )
    d_pre = (slope * dot_nn(d_b3, w_down[:, :hid])).astype(BF16)
    dpre_o[...] = d_pre
    dpre_o.send()
    d_m = dot_nt(d_pre, w_up[:, :hid]).astype(BF16)
    for r in range(tp):
        dm_o[r][...] = d_m[r * own : (r + 1) * own]
        dm_o[r].send()
    b3 = dot_nt(hidden, w_down[:, :hid]).astype(BF16)
    for r in range(tp):
        b3_o[r][...] = b3[r * own : (r + 1) * own]
        b3_o[r].send()
    sums_o[...] = clip_sums(turned[...], b3.astype(F32) * g3[...].astype(F32))


def second_back(tp, scalars, ins, outs):
    x2, g3, hot, mods, turned = ins[tp:]
    g2_o, db2_o, sums_o = outs
    own = g2_o.shape[0]
    n, inv = norm_parts(x2[...])
    scale = 1.0 + expand(hot[:own], mods[4])
    d_m = total(ins[:tp])
    g2 = g3[:own].astype(F32) + norm_back(d_m * scale, n, inv)
    db2_o[...] = g2.astype(BF16)
    db2_o.send()
    g2_o[...] = g2
    sums_o[0] = clip_sums(turned[:, :own], d_m)
    sums_o[1] = clip_sums(turned[:, :own], d_m * n)


def cross_back(tp, inner, scalars, ins, outs):
    w_out2, prob, kv, cq = ins[tp:]
    db2_o, dcq_o, dkv_o, pack_o = outs
    d_b2 = jnp.concatenate([r[...] for r in ins[:tp]], axis=0)
    db2_o[...] = d_b2
    db2_o.send()
    d_co = dot_nn(d_b2, w_out2[:, :inner]).astype(BF16)
    d_q, scores = [], []
    heads = inner // HDIM
    for h in range(heads):
        cols = slice(h * HDIM, (h + 1) * HDIM)
        key = kv[:, h * HDIM : (h + 1) * HDIM]
        value = kv[:, inner + h * HDIM : inner + (h + 1) * HDIM]
        wide = prob[h].astype(F32)
        d_p = dot_nt(d_co[:, cols], value)
        d_s = (wide * (d_p - jnp.sum(wide * d_p, -1, keepdims=True))).astype(BF16)
        scores.append(d_s)
        d_q.append((dot_nn(d_s, key) * SCALE).astype(BF16))
    result = jnp.concatenate(d_q, axis=1)
    pack_rows(pack_o, result, tp)
    pack_o.send()
    dcq_o[...] = result
    dcq_o.send()
    d_k = [
        (dot_tn(scores[h], cq[:, h * HDIM : (h + 1) * HDIM]) * SCALE).astype(BF16)
        for h in range(heads)
    ]
    d_v = [
        dot_tn(prob[h], d_co[:, h * HDIM : (h + 1) * HDIM]).astype(BF16) for h in range(heads)
    ]
    dkv_o[...] = jnp.concatenate(d_k + d_v, axis=1)


def frame_back(tp, inner, scalars, ins, outs):
    pieces = ins[:tp]
    (rank,) = scalars
    d_b2, g2, hot, mods, w_q2, w_far, w_a, qkv, prob, tok, own_b1, sums, gate2, turned = ins[tp:]
    g1_o, db1_o, dqkv_o = outs[:3]
    da_o = outs[3:]
    own, width = g1_o.shape
    d_cq = unpack_heads(pieces, tp, inner)
    d_x1 = dot_nt(d_cq[:, :inner], w_q2[:, :inner]) + dot_nt(d_cq[:, inner:], w_far[...])
    g1_own = g2[...] + d_x1[:own]
    g1_o[...] = g1_own
    g1_o.send()
    d_b1 = (expand(hot[...], mods[2]) * (d_b2[...].astype(F32) + d_x1)).astype(BF16)
    db1_o[...] = d_b1
    db1_o.send()
    d_fo = dot_nn(d_b1, w_a[:, 3 * inner : 4 * inner]).astype(BF16)
    d_q, d_k, d_v = [], [], []
    for h in range(inner // HDIM):
        q, k, v = (qkv[:, i * inner + h * HDIM : i * inner + (h + 1) * HDIM] for i in range(3))
        grad = d_fo[:, h * HDIM : (h + 1) * HDIM]
        probs = prob[h]
        d_v.append(dot_tn(probs, grad).astype(BF16))
        d_p = dot_nt(grad, v)
        wide = probs.astype(F32)
        d_s = (wide * (d_p - jnp.sum(wide * d_p, -1, keepdims=True))).astype(BF16)
        d_q.append((dot_nn(d_s, k) * SCALE).astype(BF16))
        d_k.append((dot_tn(d_s, q) * SCALE).astype(BF16))
    d_qkv = jnp.concatenate(d_q + d_k + d_v, axis=1)
    dqkv_o[...] = d_qkv
    dqkv_o.send()
    d_a = dot_nt(d_qkv, w_a[:, : 3 * inner])
    low = d_a.astype(BF16)
    for r in range(tp):
        da_o[r][:own] = low[r * own : (r + 1) * own]
    n, _ = norm_parts(tok[...].astype(F32))
    shift = dot_nn(turned[...], low)
    scale = clip_sums(turned[...], low.astype(F32) * n)
    gate1 = clip_sums(turned[:, :own], g1_o[...] * own_b1[...])
    whole = jnp.concatenate([shift, scale, gate1, sums[0], sums[1], gate2[...]], axis=1)
    size = whole.shape[1] // tp
    clips = (da_o[0].shape[0] - own) // -(-size // width)
    for r in range(tp):
        value = whole[:, :size]
        for q in range(1, tp):
            here = lax.rem(rank[0] - r + tp, tp) == q
            value = jnp.where(here, whole[:, q * size : (q + 1) * size], value)
        for g in range(-(-size // width)):
            part = value[:, g * width : (g + 1) * width].astype(BF16)
            da_o[r][own + g * clips : own + (g + 1) * clips, : part.shape[1]] = part
        da_o[r].send()


def token_rows(tp, scalars, ins, outs):
    tok, g1, hot, mods, x2, live = ins[2 * tp :]
    both_o, cols_o = outs
    own, width = g1.shape
    n, inv = norm_parts(tok[:own].astype(F32))
    scale = 1.0 + expand(hot[:own], mods[1])
    gate = expand(hot[:own], mods[5])
    sums = total(ins[:tp])
    both_o[:own] = (g1[...] + norm_back(sums[:own] * scale, n, inv)).astype(BF16)
    both_o[own:] = ((x2[...] + gate * total(ins[tp : 2 * tp])) * live[:own]).astype(BF16)
    both_o.send()
    clips, size = cols_o.shape
    for g in range(-(-size // width)):
        at = own + g * clips
        part = sums[at : at + clips, : size - g * width]
        cols_o[:, g * width : g * width + part.shape[1]] = part


def place_rows(tp, fmax, scalars, ins, outs):
    (rank,) = scalars
    own_seqs = outs[0].shape[0] // tp
    own = ins[0].shape[0] // 2
    for i, out in enumerate(outs):
        for k in range(tp):
            base = lax.rem(rank[0] - k + tp, tp) * own_seqs
            wide = ins[k][i * own : (i + 1) * own].astype(F32)
            for j in range(own_seqs):
                out[base + j] = wide[j * fmax : (j + 1) * fmax].astype(BF16)
        out.send()


def weight_grads(pairs, extra, scalars, ins, outs):
    (out,) = outs
    buf = out.bufs[0]
    if len(buf.shape) == 2:
        start = 0
        for i in range(pairs):
            width = ins[2 * i + 1].shape[1]
            buf[:, start : start + width] = dot_tn(ins[2 * i][...], ins[2 * i + 1][...]).astype(BF16)
            start += width
        return
    blocks, size = buf.shape[:2]
    start = 0
    for i in range(pairs):
        width = ins[2 * i + 1].shape[1]
        grads = dot_tn(ins[2 * i][...], ins[2 * i + 1][...]).astype(BF16)
        for s in range(blocks):
            buf[s, :, start : start + width] = grads[s * size : (s + 1) * size]
        start += width
    if extra:
        more = out.bufs[1]
        value = ins[2 * pairs][...]
        n = value.shape[1]
        size = more.shape[1]
        for s in range(blocks):
            for j in range(extra):
                at = (s * extra + j) * size
                more[s, :, j * n : (j + 1) * n] = value[at : at + size]


def add_halves(scalars, ins, outs):
    near, away = ins
    for c, out in enumerate(outs):
        out[...] = (near[c].astype(F32) + away[c].astype(F32)).astype(BF16)
        out.send()


def finish_mlp(scalars, ins, outs):
    up_o, down_o = outs
    hid = up_o.shape[1]
    value = total(ins)
    up_o[...] = value[:, :hid]
    up_o.send()
    down_o[...] = value[:, hid:]


def finish_cross(tp, inner, extra, scalars, ins, outs):
    (rank,) = scalars
    w_kv, parts = ins[0], ins[1:]
    q2_o, kv2_o, out2_o = outs[:3]
    chunk_o = outs[3:]
    drows = q2_o.shape[0]
    value = total(parts)
    more = value[drows:]
    n = 2 * inner
    dkv = jnp.concatenate([more[:, j * n : (j + 1) * n] for j in range(extra)], axis=0).astype(BF16)
    feats = chunk_o[0].shape[1]
    w_kv[:8]
    for r, out in enumerate(chunk_o):
        block = lax.rem(rank[0] - r + tp, tp)
        at = pl.ds(pl.multiple_of(block * feats, 8), feats)
        out[...] = dot_nt(dkv, w_kv[at, :]).astype(BF16)
        out.send()
    q2_o[...] = value[:drows, :inner]
    for i in range(2):
        kv2_o[i] = value[:drows, (i + 1) * inner : (i + 2) * inner]
    out2_o[...] = value[:drows, 3 * inner :]


def finish_frame(inner, scalars, ins, outs):
    qkv_o, out_o = outs
    value = total(ins)
    for i in range(3):
        qkv_o[i] = value[:, i * inner : (i + 1) * inner]
    qkv_o.send()
    out_o[...] = value[:, 3 * inner :]


def place_captions(scalars, ins, outs):
    rank, cap_len = scalars
    (parts,) = ins
    out_o, rows = outs
    clips, slots = out_o.shape[:2]
    blocks, size = parts.shape[:2]
    keys = blocks * size
    for m in range(blocks):
        at = pl.multiple_of(lax.bitwise_xor(rank[1], m) * size, 8)
        rows.bufs[0][pl.ds(at, size), :] = parts[m]
    slot = lax.broadcasted_iota(jnp.int32, (slots, keys), 0)
    key = lax.broadcasted_iota(jnp.int32, (slots, keys), 1)
    start = jnp.int32(0)
    for c in range(clips):
        pick = (slot + start == key) & (slot < cap_len[c])
        out_o[c] = dot_nn(jnp.where(pick, 1.0, 0.0).astype(BF16), rows[...])
        start = start + cap_len[c]


def ada_grads(scalars, ins, outs):
    mod_cols, scaled, w_ada = ins
    grad_o, cond_o = outs
    high = mod_cols[...].astype(BF16)
    low = (mod_cols[...] - high.astype(F32)).astype(BF16)
    grad_o[...] = dot_tn(scaled[...], high) + dot_tn(scaled[...], low)
    grad_o.send()
    cond_o[...] = split_dot(dot_nt, mod_cols[...], w_ada[...])


def after(value, *first):
    return lax.optimization_barrier((value,) + first)[0]


def tp_gather(value, tp):
    return [value] + [
        lax.ppermute(value, "tp", [(i, (i + k) % tp) for i in range(tp)]) for k in range(1, tp)
    ]


def tp_scatter(chunks, tp):
    return [chunks[0]] + [
        lax.ppermute(chunks[r], "tp", [(i, (i - r) % tp) for i in range(tp)]) for r in range(1, tp)
    ]


def seq_xor(value, mask, nseq):
    return lax.ppermute(value, "seq", [(i, i ^ mask) for i in range(nseq)])


def seq_total(value, nseq):
    mask = 1
    while mask < nseq:
        value = value + seq_xor(value, mask, nseq)
        mask *= 2
    return value


def far_gather(value, nseq):
    return [value] + [seq_xor(value, m, nseq) for m in range(2, nseq, 2)]


def near_gather(far, nseq):
    pieces = []
    for value in far:
        pieces += [value, seq_xor(value, 1, nseq)]
    return pieces


def seq_scatter(pair, nseq, name, width, rows, hold=()):
    half = nseq // 2
    other = seq_xor(pair[0], 1, nseq)
    sums = call(
        add_halves,
        [sds((rows, width))] * half,
        [pair[1], Near(other)],
        name=name,
    )
    return [sums[0]] + [seq_xor(sums[c], 2 * c, nseq) for c in range(1, half)]


def padded(value, size, axis):
    if value.shape[axis] == size:
        return value
    pads = [(0, 0)] * value.ndim
    pads[axis] = (0, size - value.shape[axis])
    return jnp.pad(value, pads)


def shards(
    tokens,
    cotangent,
    caption,
    condition,
    frames,
    cap_len,
    clip_of,
    w_qkv,
    w_out,
    w_query2,
    w_kv2,
    w_out2,
    w_up,
    w_down,
    w_ada,
):
    tp, nseq = lax.axis_size("tp"), lax.axis_size("seq")
    me, spot = lax.axis_index("tp"), lax.axis_index("seq")
    seqs, fmax, width = tokens.shape
    clips, slots = caption.shape[:2]
    inner, hid = w_query2.shape[1], w_up.shape[1]
    heads = inner // HDIM
    drows = w_query2.shape[0]
    own_seqs = seqs // tp
    own = -(-own_seqs * fmax // 8) * 8
    rows = tp * own
    clip_pad = 8
    keys = -(-(clips * slots // 2) // 128) * 128
    mod_size = 6 * width // tp
    rank = jnp.stack([me, spot]).astype(jnp.int32)
    part = functools.partial

    tok, g3, hot, row_clip, row_id, key_id, live, turned = call(
        part(prepare_rows, tp, fmax),
        [
            sds((rows, width)),
            sds((rows, width)),
            sds((rows, clip_pad)),
            sds((rows, 1), jnp.int32),
            sds((rows, 1), jnp.int32),
            sds((1, rows), jnp.int32),
            sds((rows, 1), F32),
            sds((clip_pad, rows)),
        ],
        [tokens, cotangent],
        smem=[rank, clip_of, frames],
        name="prepare_rows",
    )
    cap, key_clip = call(
        live_captions,
        [sds((keys, width)), sds((1, keys), jnp.int32)],
        [caption],
        smem=[cap_len],
        name="live_captions",
    )
    lane = lambda n: -(-n // 128) * 128
    section = jnp.concatenate(
        [padded(w_query2, lane(inner), 1), w_kv2.reshape(drows, 2 * inner)], axis=1
    )
    full_b = lax.all_gather(section, "seq", axis=0, tiled=True)
    pack_a = jnp.concatenate([w_qkv.reshape(drows, 3 * inner), w_out.T], axis=1)
    far_a = far_gather(pack_a, nseq)
    scaled = jax.nn.silu(condition).astype(BF16)
    scaled_own = lax.dynamic_slice_in_dim(scaled, spot * drows, drows, 1)
    mod_part = jnp.dot(scaled_own, w_ada, preferred_element_type=F32)
    mod_part = mod_part + seq_xor(mod_part, 1, nseq)
    mod_part = after(mod_part, tok, cap, *far_a[1:])
    mask = 2
    while mask < nseq:
        mod_part = mod_part + seq_xor(mod_part, mask, nseq)
        mask *= 2
    z_pack = jnp.concatenate([w_query2, w_out2.T], axis=1)
    groups = mod_size // (2 * inner)
    high = lax.reduce_precision(mod_part, 8, 7)
    mod_rows = [
        part_[:, g * 2 * inner : (g + 1) * 2 * inner].astype(BF16)
        for part_ in (high, mod_part - high)
        for g in range(groups)
    ]
    z_rest = tp_gather(jnp.concatenate([z_pack] + mod_rows, axis=0), tp)
    (mods,) = call(
        part(modulations, tp, clips, drows),
        [sds((6, clip_pad, width), F32)],
        [Near(p) for p in z_rest],
        smem=[rank],
        name="modulations",
    )
    z_q2 = [p[:drows, :inner] for p in z_rest[1:]]
    z_out2 = [p[:drows, inner:] for p in z_rest]
    pack_c = jnp.concatenate(
        z_out2 + [padded(w_up, lane(hid), 1), padded(w_down.T, lane(hid), 1)], axis=1
    )
    full_c = lax.all_gather(pack_c, "seq", axis=0, tiled=True)
    full_d = lax.all_gather(jnp.concatenate(z_q2, axis=1), "seq", axis=0, tiled=True)
    w_q2 = Cols(full_b, 0, lane(inner))
    w_kv = Cols(full_b, lane(inner), 2 * inner)
    w_d = Cols(full_d, 0, full_d.shape[1])

    w_a = Blocks(near_gather(far_a, nseq))

    outs = call(
        part(frame_forward, tp),
        [
            sds((rows, width)),
            sds((rows, 3 * inner)),
            sds((heads, rows, rows)),
            sds((rows, inner)),
        ]
        + [sds((own, width))] * tp,
        [tok, hot, mods, row_id, key_id, w_a],
        smem=[rank],
        name="frame_forward",
    )
    attn_in, qkv, probs, frame_out = outs[:4]
    branch_parts = tp_scatter(outs[4:], tp)
    x1_own, low_own, own_b1 = call(
        part(first_rows, tp),
        [sds((own, width), F32), sds((own, width)), sds((own, width), F32)],
        [*far(branch_parts), tok, hot, mods],
        name="first_rows",
    )
    low_parts = tp_gather(low_own, tp)
    (kv,) = call(
        key_values,
        [sds((keys, 2 * inner))],
        [cap, w_kv],
        name="key_values",
    )
    first_low, cq, cprobs, cross_out, cross_pack = call(
        part(cross_forward, tp, inner),
        [
            sds((rows, width)),
            sds((rows, inner)),
            sds((heads, rows, keys)),
            sds((rows, inner)),
            sds((own, tp * inner)),
        ],
        [*far(low_parts), row_clip, key_clip, w_q2, kv],
        name="cross_forward",
    )
    cross_parts = tp_gather(cross_pack, tp)
    outs = call(
        part(mlp_both, tp, inner),
        [
            sds((own, width), F32),
            sds((rows, width)),
            sds((rows, hid)),
            sds((rows, width)),
            sds((rows, hid)),
        ]
        + [sds((clip_pad, width), F32)]
        + [sds((own, width))] * (2 * tp),
        [
            *far(cross_parts),
            x1_own,
            first_low,
            g3,
            hot,
            mods,
            Cols(full_c, 0, width),
            Cols(full_c, width, lane(hid)),
            Cols(full_c, width + lane(hid), lane(hid)),
            turned,
        ],
        smem=[rank],
        name="mlp_both",
    )
    x2_own, mlp_in, hidden, d_b3, d_pre = outs[:5]
    sum_gate2 = outs[5]
    dm_chunks, b3_chunks = outs[6 : 6 + tp], outs[6 + tp :]

    dm_parts = tp_scatter(dm_chunks, tp)
    (grad_one,) = call(
        part(weight_grads, 2, 0),
        [sds((width, 2 * hid))],
        [mlp_in, d_pre, d_b3, hidden],
        name="grads_mlp",
    )
    g2_own, db2_own, sums_two = call(
        part(second_back, tp),
        [sds((own, width), F32), sds((own, width)), sds((2, clip_pad, width), F32)],
        [*far(dm_parts), x2_own, g3, hot, mods, turned],
        order=[grad_one],
        name="second_back",
    )
    sum_one = lax.psum_scatter(after(grad_one, db2_own), "seq", scatter_dimension=0, tiled=True)
    db2_parts = tp_gather(db2_own, tp)
    d_b2, d_cq, d_kv, dcq_pack = call(
        part(cross_back, tp, inner),
        [sds((rows, width)), sds((rows, inner)), sds((keys, 2 * inner)), sds((own, tp * inner))],
        [*far(db2_parts), Cols(full_c, 0, lane(inner)), cprobs, kv, cq],
        name="cross_back",
    )
    dcq_parts = tp_gather(dcq_pack, tp)
    extra = width // (2 * inner)
    while (keys // nseq) % (8 * extra):
        extra -= 1
    more = keys // nseq // extra
    pair_two = call(
        part(weight_grads, 3, extra),
        [Split([drows, more], nseq, 4 * inner)],
        [first_low, d_cq, cap, d_kv, d_b2, cross_out, d_kv],
        smem=[rank],
        name="grads_cross",
    )
    parts_two = seq_scatter([after(pair_two[0], *dcq_parts[1:]), pair_two[1]], nseq, "add_cross", 4 * inner, drows + more)
    outs = call(
        part(frame_back, tp, inner),
        [sds((own, width), F32), sds((rows, width)), sds((rows, 3 * inner))]
        + [sds((own + clip_pad * -(-mod_size // width), width))] * tp,
        [
            *far(dcq_parts),
            d_b2,
            g2_own,
            hot,
            mods,
            w_q2,
            w_d,
            w_a,
            qkv,
            probs,
            tok,
            own_b1,
            sums_two,
            sum_gate2,
            turned,
        ],
        smem=[rank],
        order=[parts_two[0]],
        name="frame_back",
    )
    g1_own, d_b1, d_qkv = outs[:3]
    da_chunks = outs[3:]
    b3_parts = tp_scatter([after(b, *dcq_parts[1:]) for b in b3_chunks], tp)
    da_parts = tp_scatter([after(d, *b3_parts[1:]) for d in da_chunks], tp)
    (grad_three,) = call(
        part(weight_grads, 2, 0),
        [sds((width, 4 * inner))],
        [attn_in, d_qkv, d_b1, frame_out],
        name="grads_frame",
    )
    sum_three = lax.psum_scatter(
        after(grad_three, sum_one, *da_parts[1:]), "seq", scatter_dimension=0, tiled=True
    )
    both_own, mod_cols = call(
        part(token_rows, tp),
        [sds((2 * own, width)), sds((clip_pad, mod_size), F32)],
        [*far(da_parts), *far(b3_parts), tok, g1_own, hot, mods, x2_own, live],
        order=[grad_three],
        name="token_rows",
    )
    both_parts = tp_gather(both_own, tp)
    mod_cols = seq_total(mod_cols, nseq)

    grad_up, grad_down = call(
        finish_mlp,
        [sds((drows, hid), F32), sds((drows, hid), F32)],
        [sum_one],
        name="finish_mlp",
    )
    feats = width // tp
    outs = call(
        part(finish_cross, tp, inner, extra),
        [sds((drows, inner), F32), sds((2, drows, inner), F32), sds((drows, inner), F32)]
        + [sds((keys // nseq, feats))] * tp,
        [w_kv, *far(parts_two)],
        smem=[rank],
        name="finish_cross",
    )
    grad_q2, grad_kv2, grad_out2 = outs[:3]
    cap_parts = tp_scatter(outs[3:], tp)
    cap_all = sum(p.astype(F32) for p in cap_parts).astype(BF16)[None]
    mask = 1
    while mask < nseq:
        cap_all = jnp.concatenate([cap_all, seq_xor(cap_all, mask, nseq)])
        mask *= 2
    d_caption, _ = call(
        place_captions,
        [sds((clips, slots, feats), F32), sds((keys, feats))],
        [Near(cap_all)],
        smem=[rank, cap_len],
        name="place_captions",
    )
    grad_qkv, grad_out = call(
        part(finish_frame, inner),
        [sds((3, drows, inner), F32), sds((drows, inner), F32)],
        [sum_three],
        name="finish_frame",
    )

    grad_ada, cond_part = call(
        ada_grads,
        [sds(w_ada.shape, F32), sds((clip_pad, drows), F32)],
        [Near(mod_cols), Near(padded(scaled_own, clip_pad, 0)), w_ada],
        name="ada_grads",
    )
    cond_part = sum(tp_gather(cond_part[:clips], tp))
    cond_wide = lax.dynamic_update_slice_in_dim(
        jnp.zeros((clips, width), F32), cond_part, spot * drows, 1
    )
    d_condition = jax.vjp(jax.nn.silu, condition)[1](seq_total(cond_wide, nseq))[0]

    d_tokens, output = call(
        part(place_rows, tp, fmax),
        [sds((seqs, fmax, width))] * 2,
        far(both_parts),
        smem=[rank],
        order=[grad_up, grad_q2, d_caption, grad_ada],
        name="place_rows",
    )

    return (
        output,
        d_tokens,
        d_caption,
        d_condition,
        grad_qkv.transpose(1, 0, 2),
        grad_out.T,
        grad_q2,
        grad_kv2.transpose(1, 0, 2),
        grad_out2.T,
        grad_up,
        grad_down.T,
        grad_ada,
    )


def solution(mesh):
    return jax.shard_map(
        shards,
        mesh=mesh,
        in_specs=(
            P("seq", None, None),
            P("seq", None, None),
            P(),
            P(),
            P(),
            P(),
            P("seq"),
            P("seq", None, "tp"),
            P("tp", "seq"),
            P("seq", "tp"),
            P("seq", None, "tp"),
            P("tp", "seq"),
            P("seq", "tp"),
            P("tp", "seq"),
            P("seq", "tp"),
        ),
        out_specs=(
            P("seq", None, None),
            P("seq", None, None),
            P(None, None, "tp"),
            P(),
            P("seq", None, "tp"),
            P("tp", "seq"),
            P("seq", "tp"),
            P("seq", None, "tp"),
            P("tp", "seq"),
            P("seq", "tp"),
            P("tp", "seq"),
            P("seq", "tp"),
        ),
        check_vma=False,
    )
```

```python
import functools
import math

import jax
import jax.numpy as jnp
from jax import lax
from jax.experimental import pallas as pl
from jax.experimental.pallas import tpu as pltpu
from jax.sharding import PartitionSpec as P

HDIM = 72
EPSILON = 1e-06
NEG_FILL = -1e30
F32 = jnp.float32
BF16 = jnp.bfloat16
SCALE = HDIM ** (-0.5)
VMEM_LIMIT = 48 << 20


def dot_nn(a, b):
    return lax.dot_general(a, b, (((1,), (0,)), ((), ())), preferred_element_type=F32)


def dot_nt(a, b):
    return lax.dot_general(a, b, (((1,), (1,)), ((), ())), preferred_element_type=F32)


def dot_tn(a, b):
    return lax.dot_general(a, b, (((0,), (0,)), ((), ())), preferred_element_type=F32)


def sds(shape, dtype=BF16):
    return jax.ShapeDtypeStruct(shape, dtype)


class Blocks:
    def __init__(self, pieces):
        self.pieces = pieces


class Cols:
    def __init__(self, whole, start, size):
        self.whole, self.start, self.size = whole, start, size


class Near:
    def __init__(self, whole):
        self.whole = whole


class Half:
    def __init__(self, shape, start, size):
        self.shape, self.dtype, self.start, self.size = shape, BF16, start, size


class In:
    def __init__(self, buf, copies):
        self.buf, self.copies, self.ready = buf, copies, not copies

    @property
    def shape(self):
        return self.buf.shape

    def ref(self):
        if not self.ready:
            for copy in self.copies:
                copy.wait()
            self.ready = True
        return self.buf

    def __getitem__(self, index):
        return self.ref()[index]


class Out:
    def __init__(self, bufs, copies):
        self.bufs, self.copies, self.sent = bufs, copies, False

    @property
    def shape(self):
        return self.bufs[0].shape

    def __getitem__(self, index):
        return self.bufs[0][index]

    def __setitem__(self, index, value):
        self.bufs[0][index] = value

    def send(self):
        if not self.sent:
            for copy in self.copies:
                copy.start()
            self.sent = True


def call(body, outs, ins, *, name, smem=(), order=(), keep=False, work=(), limit=VMEM_LIMIT):
    vmem, hbm = pl.BlockSpec(memory_space=pltpu.VMEM), pl.BlockSpec(memory_space=pltpu.HBM)
    pin = lambda value: pltpu.with_memory_space_constraint(value, pltpu.HBM)
    ops, in_specs, in_plan, scratch_in = [], [], [], []
    n_in = 0
    for arg in ins:
        if isinstance(arg, Near):
            in_plan.append((len(ops), None, arg, 0))
            ops.append(arg.whole)
            in_specs.append(vmem)
            continue
        pieces = arg.pieces if isinstance(arg, Blocks) else [arg.whole if isinstance(arg, Cols) else arg]
        shape = pieces[0].shape
        if isinstance(arg, Blocks):
            shape = (shape[0] * len(pieces),) + shape[1:]
        elif isinstance(arg, Cols):
            shape = (shape[0], arg.size)
        in_plan.append((len(ops), len(scratch_in), arg, n_in))
        scratch_in.append(pltpu.VMEM(shape, pieces[0].dtype))
        n_in += len(pieces)
        ops += [pin(p) for p in pieces]
        in_specs += [hbm] * len(pieces)
    n_read = len(ops)
    for arg in order:
        ops.append(arg.whole if isinstance(arg, Near) else pin(arg))
        in_specs.append(vmem if isinstance(arg, Near) else hbm)
    results, out_plan, scratch_out = [], [], []
    n_out = 0
    for out in outs:
        out_plan.append((len(results), len(scratch_out), out, n_out))
        results.append(out)
        wide = (out.shape[0], out.size) if isinstance(out, Half) else out.shape
        scratch_out.append(pltpu.VMEM(wide, out.dtype))
        n_out += 1
    n_s, n_i, n_o = len(smem), len(ops), len(results)

    def kernel(*refs):
        scalars = refs[:n_s]
        src = refs[n_s : n_s + n_read]
        dst = refs[n_s + n_i : n_s + n_i + n_o]
        scratch = refs[n_s + n_i + n_o :]
        bufs = scratch[: len(scratch_in)]
        obufs = scratch[len(scratch_in) : len(scratch_in) + len(scratch_out)]
        extra = list(scratch[len(scratch_in) + len(scratch_out) : -2])
        in_sem, out_sem = scratch[-2:]
        lazy = []
        for start, at, arg, sem in in_plan:
            if at is None:
                lazy.append(In(src[start], []))
                continue
            copies = []
            if isinstance(arg, Blocks):
                rows = src[start].shape[0]
                for m in range(len(arg.pieces)):
                    block = lax.bitwise_xor(scalars[0][1], m)
                    place = bufs[at].at[pl.ds(pl.multiple_of(block * rows, 8), rows)]
                    copies.append(pltpu.make_async_copy(src[start + m], place, in_sem.at[sem + m]))
            else:
                part = src[start]
                if isinstance(arg, Cols):
                    part = part.at[:, pl.ds(arg.start, arg.size)]
                copies.append(pltpu.make_async_copy(part, bufs[at], in_sem.at[sem]))
            for copy in copies:
                copy.start()
            lazy.append(In(bufs[at], copies))
        made = []
        for first, at, out, sem in out_plan:
            place = dst[first]
            if isinstance(out, Half):
                place = place.at[:, pl.ds(out.start, out.size)]
            copy = pltpu.make_async_copy(obufs[at], place, out_sem.at[sem])
            made.append(Out([obufs[at]], [copy]))
        body(scalars, lazy, made + extra)
        for item in lazy:
            if not item.ready:
                item[...]
        for out in made:
            out.send()
        for out in made:
            for copy in out.copies:
                copy.wait()

    moved = sum(a.size * a.dtype.itemsize for a in ops[:n_read])
    moved += sum(math.prod(o.shape) * jnp.dtype(o.dtype).itemsize for o in results)
    return pl.pallas_call(
        kernel,
        out_shape=tuple(pltpu.HBM(o.shape, o.dtype) for o in results),
        in_specs=[pl.BlockSpec(memory_space=pltpu.SMEM)] * n_s + in_specs,
        out_specs=tuple([hbm] * n_o),
        scratch_shapes=scratch_in
        + scratch_out
        + [pltpu.VMEM(w.shape, w.dtype) for w in work]
        + [pltpu.SemaphoreType.DMA((max(n_in, 1),)), pltpu.SemaphoreType.DMA((max(n_out, 1),))],
        input_output_aliases={n_s + n_read: 0} if keep else {},
        compiler_params=pltpu.CompilerParams(vmem_limit_bytes=limit),
        cost_estimate=pl.CostEstimate(flops=0, transcendentals=0, bytes_accessed=moved),
        name=name,
    )(*smem, *ops)


def norm_parts(rows):
    center = rows - jnp.mean(rows, -1, keepdims=True)
    inv = lax.rsqrt(jnp.mean(center * center, -1, keepdims=True) + EPSILON)
    return center * inv, inv


def expand(hot, table):
    high = table.astype(BF16)
    low = (table - high.astype(F32)).astype(BF16)
    return dot_nn(hot, high) + dot_nn(hot, low)


def split_dot(dot, a, b):
    high = a.astype(BF16)
    low = (a - high.astype(F32)).astype(BF16)
    return dot(high, b) + dot(low, b)


def clip_sums(clips_hot, values):
    return dot_nn(clips_hot, values.astype(BF16))


def norm_back(grad, n, inv):
    return inv * (grad - jnp.mean(grad, -1, keepdims=True) - n * jnp.mean(grad * n, -1, keepdims=True))


def softmax_rows(scores):
    top = jnp.max(scores, -1, keepdims=True)
    weights = jnp.exp(scores - top)
    return weights / jnp.sum(weights, -1, keepdims=True)


def pack_rows(out, value, tp):
    own, n = value.shape[0] // tp, value.shape[1]
    for r in range(tp):
        out[:, r * n : (r + 1) * n] = value[r * own : (r + 1) * own]


def unpack_heads(pieces, tp, n):
    pieces = [p[...] for p in pieces]
    rows = []
    for b in range(tp):
        cols = []
        for k in range(tp):
            r = (b - k) % tp
            cols.append(pieces[k][:, r * n : (r + 1) * n])
        rows.append(jnp.concatenate(cols, axis=1))
    return jnp.concatenate(rows, axis=0)


def far(parts):
    return [parts[0]] + [Near(p) for p in parts[1:]]


def put_heads(work, value, start=0):
    for h in range(work.shape[0]):
        work[h] = value[:, start + h * HDIM : start + (h + 1) * HDIM]


def take_heads(work):
    return jnp.concatenate([work[h] for h in range(work.shape[0])], axis=1)


def for_heads(count, body):
    def step(h, carry):
        body(h)
        return carry

    lax.fori_loop(0, count, step, 0)


def for_columns(width, body, most=384):
    size = math.gcd(width, most)

    def step(i, carry):
        body(pl.ds(pl.multiple_of(i * size, size), size))
        return carry

    lax.fori_loop(0, width // size, step, 0)


def total(parts):
    value = parts[0][...].astype(F32)
    for part in parts[1:]:
        value = value + part[...].astype(F32)
    return value


def prepare_rows(tp, scalars, ins, outs):
    rank, clip_of, frames = scalars
    tok_o, g3_o, hot_o, clip_o, id_o, key_o, live_o, turned_o, canon = outs
    rows, width = tok_o.shape
    own = rows // tp
    fmax, seqs = ins[0].shape[:2]
    own_seqs = seqs // tp
    used = own_seqs * fmax
    row = lax.broadcasted_iota(jnp.int32, (own, 1), 0)
    spot = lax.rem(row, own_seqs)
    place = lax.broadcasted_iota(jnp.int32, key_o.shape, 1)
    keys = jnp.full(key_o.shape, -2, jnp.int32)
    owner = jnp.full(key_o.shape, -1, jnp.int32)
    alive = []
    for k in range(tp):
        base = lax.rem(rank[0] - k + tp, tp) * own_seqs
        at = slice(k * own, (k + 1) * own)
        clip = jnp.full((own, 1), -1, jnp.int32)
        name = jnp.full((own, 1), -1, jnp.int32)
        limit = jnp.zeros((own, 1), jnp.int32)
        inside = place - k * own
        mine = (inside >= 0) & (inside < used)
        turn = lax.rem(jnp.maximum(inside, 0), own_seqs)
        for j in range(own_seqs):
            c = clip_of[base + j]
            count = frames[c] * own_seqs
            here = (spot == j) & (row < used)
            clip = jnp.where(here, c, clip)
            name = jnp.where(here, k * own_seqs + j, name)
            limit = jnp.where(here, count, limit)
            there = mine & (turn == j)
            owner = jnp.where(there, c, owner)
            keys = jnp.where(there & (inside < count), k * own_seqs + j, keys)
        live = jnp.where(row < limit, 1.0, 0.0)
        alive.append(live)
        live_o[at] = live
        clip_o[at] = clip
        id_o[at] = name
        lane = lax.broadcasted_iota(jnp.int32, (own, hot_o.shape[1]), 1)
        hot_o[at] = jnp.where(lane == clip, 1.0, 0.0).astype(BF16)
    key_o[...] = keys
    which = lax.broadcasted_iota(jnp.int32, turned_o.shape, 0)
    turned_o[...] = jnp.where(which == owner, 1.0, 0.0).astype(BF16)
    for source, out, mask in ((ins[0], tok_o, False), (ins[1], g3_o, True)):
        if own > used:
            canon[:, used:] = jnp.zeros((tp, own - used, width), BF16)
        for f in range(fmax):
            for q in range(tp):
                group = source[f, q * own_seqs : (q + 1) * own_seqs]
                canon[q, f * own_seqs : (f + 1) * own_seqs] = group
        for k in range(tp):
            value = canon[lax.rem(rank[0] - k + tp, tp)]
            if mask:
                value = (value.astype(F32) * alive[k]).astype(BF16)
            out[k * own : (k + 1) * own] = value
        out.send()


def live_captions(scalars, ins, outs):
    (cap_len,) = scalars
    (caption,) = ins
    cap_o, clip_o = outs
    keys = cap_o.shape[0]
    clips, slots = caption.shape[:2]
    col = lax.broadcasted_iota(jnp.int32, (1, keys), 1)
    clip = jnp.full((1, keys), -9, jnp.int32)
    start = jnp.int32(0)
    spans = []
    for c in range(clips):
        end = start + cap_len[c]
        clip = jnp.where((col >= start) & (col < end), c, clip)
        spans.append((start, end))
        start = end
    clip_o[...] = clip
    source, target = caption.ref(), cap_o.bufs[0]
    step = math.gcd(keys, 128)

    def some(i, carry):
        row = lax.broadcasted_iota(jnp.int32, (step, slots), 0) + i * step
        slot = lax.broadcasted_iota(jnp.int32, (step, slots), 1)
        value = jnp.zeros((step, target.shape[1]), F32)
        for c, (begin, end) in enumerate(spans):
            pick = (row - begin == slot) & (row < end)
            value = value + dot_nn(jnp.where(pick, 1.0, 0.0).astype(BF16), source[c])
        target[pl.ds(pl.multiple_of(i * step, step), step)] = value.astype(BF16)
        return carry

    lax.fori_loop(0, keys // step, some, 0)


def modulations(tp, clips, first, scalars, ins, outs):
    (rank,) = scalars
    (mods_o,) = outs
    width = mods_o.shape[2]
    groups = (ins[0].shape[0] - first) // (2 * clips)

    def joined(ref):
        cols = []
        for g in range(groups):
            at = first + g * clips
            high = ref[at : at + clips].astype(F32)
            cols.append(high + ref[at + groups * clips : at + (groups + 1) * clips].astype(F32))
        return jnp.concatenate(cols, axis=1)

    parts = [joined(ref) for ref in ins]
    cols = []
    for q in range(tp):
        value = parts[0]
        for k in range(1, tp):
            value = jnp.where(lax.rem(rank[0] - k + tp, tp) == q, parts[k], value)
        cols.append(value)
    whole = jnp.concatenate(cols, axis=1)
    mods_o[...] = jnp.zeros(mods_o.shape, F32)
    for j in range(6):
        mods_o[j, :clips] = whole[:, j * width : (j + 1) * width]


def frame_forward(tp, scalars, ins, outs):
    tok, hot, mods, row_id, key_id, w_a = ins
    attn_o, qkv_o, prob_o, fo_o = outs[:4]
    branch_o = outs[4:-2]
    heads, made = outs[-2:]
    inner = fo_o.shape[1]
    own = branch_o[0].shape[0]
    n, _ = norm_parts(tok[...].astype(F32))
    low = (n * (1.0 + expand(hot[...], mods[1])) + expand(hot[...], mods[0])).astype(BF16)
    attn_o[...] = low
    attn_o.send()
    qkv = dot_nn(low, w_a[:, : 3 * inner]).astype(BF16)
    qkv_o[...] = qkv
    qkv_o.send()
    allowed = row_id[...] == key_id[...]
    for i in range(3):
        put_heads(heads.at[i], qkv, i * inner)
    prob = prob_o.bufs[0]

    def one(h):
        scores = dot_nt(heads[0, h], heads[1, h]) * SCALE
        probs = softmax_rows(jnp.where(allowed, scores, NEG_FILL)).astype(BF16)
        prob[h] = probs
        made[h] = dot_nn(probs, heads[2, h]).astype(BF16)

    for_heads(inner // HDIM, one)
    result = take_heads(made)
    prob_o.send()
    fo_o[...] = result
    fo_o.send()
    weights, low_out = w_a.ref(), fo_o.bufs[0]

    def last(cols):
        branch = dot_nt(low_out[...], weights[cols, 3 * inner : 4 * inner]).astype(BF16)
        for r in range(tp):
            branch_o[r].bufs[0][:, cols] = branch[r * own : (r + 1) * own]

    for_columns(weights.shape[0], last)
    for out in branch_o:
        out.send()


def first_rows(tp, scalars, ins, outs):
    tok, hot, mods = ins[tp:]
    x1_o, low_o, branch_o = outs
    own = x1_o.shape[0]
    gate = expand(hot[:own], mods[2])
    branch = total(ins[:tp])
    branch_o[...] = branch
    branch_o.send()
    first = tok[:own].astype(F32) + gate * branch
    x1_o[...] = first
    low_o[...] = first.astype(BF16)


def key_values(scalars, ins, outs):
    cap, w_kv = (item.ref() for item in ins)
    kv = outs[0].bufs[0]
    step = math.gcd(kv.shape[0], 128)

    def some(i, carry):
        at = pl.ds(pl.multiple_of(i * step, 16), step)
        kv[at] = dot_nn(cap[at], w_kv[...]).astype(BF16)
        return carry

    lax.fori_loop(0, kv.shape[0] // step, some, 0)


def cross_forward(tp, inner, scalars, ins, outs):
    row_clip, key_clip, w_q2, kv = ins[tp:]
    low_o, cq_o, prob_o, co_o, pack_o, query, pair, made = outs
    low = jnp.concatenate([r[...] for r in ins[:tp]], axis=0)
    low_o[...] = low
    low_o.send()
    cq = dot_nn(low, w_q2[:, :inner]).astype(BF16)
    cq_o[...] = cq
    cq_o.send()
    allowed = row_clip[...] == key_clip[...]
    put_heads(query, cq)
    for i in range(2):
        put_heads(pair.at[i], kv.ref(), i * inner)
    prob = prob_o.bufs[0]

    def one(h):
        scores = jnp.where(allowed, dot_nt(query[h], pair[0, h]) * SCALE, NEG_FILL)
        probs = softmax_rows(scores).astype(BF16)
        prob[h] = probs
        made[h] = dot_nn(probs, pair[1, h]).astype(BF16)

    for_heads(inner // HDIM, one)
    result = take_heads(made)
    pack_rows(pack_o, result, tp)
    pack_o.send()
    prob_o.send()
    co_o[...] = result


GELU_C = 0.7978845608028654


def mlp_both(tp, inner, scalars, ins, outs):
    pieces = ins[:tp]
    first, low_first, g3, hot, mods, w_out2, w_up, w_down, turned = ins[tp:]
    x2_o, mlp_o, hid_o, db3_o, dpre_o, sums_o = outs[:6]
    dm_o, b3_o = outs[6 : 6 + tp], outs[6 + tp :]
    own, width = x2_o.shape
    hid = hid_o.shape[1]
    d_b3 = (expand(hot[...], mods[5]) * g3[...].astype(F32)).astype(BF16)
    db3_o[...] = d_b3
    db3_o.send()
    rows = unpack_heads(pieces, tp, inner)
    branch = dot_nt(rows, w_out2[...])
    second = jnp.concatenate(
        [first[...] + branch[:own], low_first[own:].astype(F32) + branch[own:]], axis=0
    )
    x2_o[...] = second[:own]
    x2_o.send()
    n, _ = norm_parts(second)
    mlp_o[...] = (n * (1.0 + expand(hot[...], mods[4])) + expand(hot[...], mods[3])).astype(BF16)
    mlp_o.send()
    low, d_low, hiddens, d_pres = (o.bufs[0] for o in (mlp_o, db3_o, hid_o, dpre_o))
    up, down = w_up.ref(), w_down.ref()

    def some(cols):
        pre = dot_nn(low[...], up[:, cols])
        th = jnp.tanh(GELU_C * (pre + 0.044715 * (pre * pre * pre)))
        hiddens[:, cols] = (0.5 * pre * (1.0 + th)).astype(BF16)
        slope = 0.5 * (1.0 + th) + 0.5 * pre * (1.0 - th * th) * (
            GELU_C * (1.0 + 3.0 * 0.044715 * (pre * pre))
        )
        d_pres[:, cols] = (slope * dot_nn(d_low[...], down[:, cols])).astype(BF16)

    if hid % 128:
        some(slice(0, hid))
    else:
        for_columns(hid, some)
    hid_o.send()
    dpre_o.send()
    turn, held, found = turned[...], g3.ref(), sums_o.bufs[0]

    def back(cols):
        d_m = dot_nt(d_pres[...], up[cols, :hid]).astype(BF16)
        for r in range(tp):
            dm_o[r].bufs[0][:, cols] = d_m[r * own : (r + 1) * own]

    for_columns(width, back)
    for out in dm_o:
        out.send()

    def ahead(cols):
        b3 = dot_nt(hiddens[...], down[cols, :hid]).astype(BF16)
        for r in range(tp):
            b3_o[r].bufs[0][:, cols] = b3[r * own : (r + 1) * own]
        found[:, cols] = clip_sums(turn, b3.astype(F32) * held[:, cols].astype(F32))

    for_columns(width, ahead)


def second_back(tp, scalars, ins, outs):
    x2, g3, hot, mods, turned = ins[tp:]
    g2_o, db2_o, sums_o = outs
    own = g2_o.shape[0]
    n, inv = norm_parts(x2[...])
    scale = 1.0 + expand(hot[:own], mods[4])
    d_m = total(ins[:tp])
    g2 = g3[:own].astype(F32) + norm_back(d_m * scale, n, inv)
    db2_o[...] = g2.astype(BF16)
    db2_o.send()
    g2_o[...] = g2
    sums_o[0] = clip_sums(turned[:, :own], d_m)
    sums_o[1] = clip_sums(turned[:, :own], d_m * n)


def cross_back(tp, inner, scalars, ins, outs):
    (rank,) = scalars
    w_out2, prob, kv, cq = ins[tp:]
    db2_o, dcq_o, dkv_o, pack_o, rel_o, query, pair, grads, made, scores, back = outs
    d_b2 = jnp.concatenate([r[...] for r in ins[:tp]], axis=0)
    db2_o[...] = d_b2
    db2_o.send()
    d_co = dot_nn(d_b2, w_out2[:, :inner]).astype(BF16)
    put_heads(grads, d_co)
    put_heads(query, cq.ref())
    for i in range(2):
        put_heads(pair.at[i], kv.ref(), i * inner)
    probs = prob.ref()

    def one(h):
        wide = probs[h].astype(F32)
        d_p = dot_nt(grads[h], pair[1, h])
        d_s = (wide * (d_p - jnp.sum(wide * d_p, -1, keepdims=True))).astype(BF16)
        scores[h] = d_s
        made[h] = (dot_nn(d_s, pair[0, h]) * SCALE).astype(BF16)

    for_heads(inner // HDIM, one)
    result = take_heads(made)
    pack_rows(pack_o, result, tp)
    pack_o.send()
    dcq_o[...] = result
    dcq_o.send()

    def two(h):
        back[0, h] = (dot_tn(scores[h], query[h]) * SCALE).astype(BF16)
        back[1, h] = dot_tn(probs[h], grads[h]).astype(BF16)

    for_heads(inner // HDIM, two)
    d_kv = jnp.concatenate([take_heads(back.at[0]), take_heads(back.at[1])], axis=1)
    blocks, size = rel_o.shape[:2]
    for b in range(blocks):
        other = lax.bitwise_xor(rank[1], b)
        rel_o[(other % 2) * (blocks // 2) + other // 2] = d_kv[b * size : (b + 1) * size]
    rel_o.send()
    dkv_o[...] = d_kv


def frame_back(tp, inner, scalars, ins, outs):
    pieces = ins[:tp]
    (rank,) = scalars
    d_b2, g2, hot, mods, w_q2, w_far, w_a, qkv, prob, tok, own_b1, sums, gate2, turned = ins[tp:]
    g1_o, db1_o, dqkv_o = outs[:3]
    da_o = outs[3:-6]
    heads, grads, made, cqs, norms, found = outs[-6:]
    own, width = g1_o.shape
    d_cq = unpack_heads(pieces, tp, inner)
    cqs[...] = d_cq
    near_w, far_w, held, second, table = (r.ref() for r in (w_q2, w_far, d_b2, g2, mods))
    pick = hot[...]
    g1s, d_b1s = g1_o.bufs[0], db1_o.bufs[0]

    def first(cols):
        d_x1 = dot_nt(cqs[:, :inner], near_w[cols, :inner]) + dot_nt(cqs[:, inner:], far_w[cols])
        g1s[:, cols] = second[:, cols] + d_x1[:own]
        gate = expand(pick, table[2, :, cols])
        d_b1s[:, cols] = (gate * (held[:, cols].astype(F32) + d_x1)).astype(BF16)

    for_columns(width, first)
    g1_o.send()
    db1_o.send()
    d_fo = dot_nn(d_b1s[...], w_a[:, 3 * inner : 4 * inner]).astype(BF16)
    put_heads(grads, d_fo)
    for i in range(3):
        put_heads(heads.at[i], qkv.ref(), i * inner)
    probs = prob.ref()

    def one(h):
        grad = grads[h]
        wide = probs[h].astype(F32)
        made[2, h] = dot_tn(probs[h], grad).astype(BF16)
        d_p = dot_nt(grad, heads[2, h])
        d_s = (wide * (d_p - jnp.sum(wide * d_p, -1, keepdims=True))).astype(BF16)
        made[0, h] = (dot_nn(d_s, heads[1, h]) * SCALE).astype(BF16)
        made[1, h] = (dot_tn(d_s, heads[0, h]) * SCALE).astype(BF16)

    for_heads(inner // HDIM, one)
    d_qkv = jnp.concatenate([take_heads(made.at[i]) for i in range(3)], axis=1)
    dqkv_o[...] = d_qkv
    d_qkvs = dqkv_o.bufs[0]
    dqkv_o.send()
    n, _ = norm_parts(tok[...].astype(F32))
    norms[...] = n
    weights, turn, extra = w_a.ref(), turned[...], own_b1.ref()

    def last(cols):
        low = dot_nt(d_qkvs[...], weights[cols, : 3 * inner]).astype(BF16)
        for r in range(tp):
            da_o[r].bufs[0][:own, cols] = low[r * own : (r + 1) * own]
        found[0, :, cols] = dot_nn(turn, low)
        found[1, :, cols] = clip_sums(turn, low.astype(F32) * norms[:, cols])
        found[2, :, cols] = clip_sums(turn[:, :own], g1s[:, cols] * extra[:, cols])

    for_columns(width, last)
    shift, scale, gate1 = found[0], found[1], found[2]
    whole = jnp.concatenate([shift, scale, gate1, sums[0], sums[1], gate2[...]], axis=1)
    size = whole.shape[1] // tp
    clips = (da_o[0].shape[0] - own) // -(-size // width)
    for r in range(tp):
        value = whole[:, :size]
        for q in range(1, tp):
            here = lax.rem(rank[0] - r + tp, tp) == q
            value = jnp.where(here, whole[:, q * size : (q + 1) * size], value)
        for g in range(-(-size // width)):
            part = value[:, g * width : (g + 1) * width].astype(BF16)
            da_o[r][own + g * clips : own + (g + 1) * clips, : part.shape[1]] = part
        da_o[r].send()


def token_rows(tp, scalars, ins, outs):
    tok, g1, hot, mods, x2, live = ins[2 * tp :]
    both_o, cols_o = outs
    own, width = g1.shape
    n, inv = norm_parts(tok[:own].astype(F32))
    scale = 1.0 + expand(hot[:own], mods[1])
    gate = expand(hot[:own], mods[5])
    sums = total(ins[:tp])
    both_o[:own] = (g1[...] + norm_back(sums[:own] * scale, n, inv)).astype(BF16)
    both_o[own:] = ((x2[...] + gate * total(ins[tp : 2 * tp])) * live[:own]).astype(BF16)
    both_o.send()
    clips, size = cols_o.shape
    for g in range(-(-size // width)):
        at = own + g * clips
        part = sums[at : at + clips, : size - g * width]
        cols_o[:, g * width : g * width + part.shape[1]] = part


def place_rows(tp, scalars, ins, outs):
    (rank,) = scalars
    results, canon = outs[:-1], outs[-1]
    fmax, seqs = results[0].shape[:2]
    own_seqs = seqs // tp
    own = ins[0].shape[0] // 2
    for k in range(tp):
        canon[lax.rem(rank[0] - k + tp, tp)] = ins[k][...]
    for i, out in enumerate(results):
        for f in range(fmax):
            for q in range(tp):
                at = i * own + f * own_seqs
                out[f, q * own_seqs : (q + 1) * own_seqs] = canon[q, at : at + own_seqs]
        out.send()


def weight_grads(pairs, scalars, ins, outs):
    out = outs[0].bufs[0]
    refs = [item.ref() for item in ins]
    step = math.gcd(out.shape[0], 128)
    filled = sum(refs[2 * j + 1].shape[1] for j in range(pairs))
    if filled < out.shape[1]:
        out[:, filled:] = jnp.zeros((out.shape[0], out.shape[1] - filled), BF16)

    def some(i, carry):
        at = pl.ds(pl.multiple_of(i * step, step), step)
        start = 0
        for j in range(pairs):
            left, right = refs[2 * j], refs[2 * j + 1]
            width = right.shape[1]
            out[at, start : start + width] = dot_tn(left[:, at], right[...]).astype(BF16)
            start += width
        return carry

    lax.fori_loop(0, out.shape[0] // step, some, 0)


def finish_mlp(scalars, ins, outs):
    up_o, down_o = outs
    hid = up_o.shape[1]
    value = total(ins)
    up_o[...] = value[:, :hid]
    up_o.send()
    down_o[...] = value[:, hid:]


def caption_chunks(tp, scalars, ins, outs):
    (rank,) = scalars
    w_kv, d_kv = ins
    feats = outs[0].shape[1]
    w_kv[:8]
    for r, out in enumerate(outs):
        block = lax.rem(rank[0] - r + tp, tp)
        at = pl.ds(pl.multiple_of(block * feats, 8), feats)
        out[...] = dot_nt(d_kv[...], w_kv[at, :]).astype(BF16)
        out.send()


def finish_rest(scalars, ins, outs):
    (value,) = ins
    q2_o, kv2_o, out2_o, qkv_o, out_o = outs
    inner = q2_o.shape[1]
    half = value.shape[1] // 2

    def part(i):
        at = (i // 4) * half + (i % 4) * inner
        return value[:, at : at + inner].astype(F32)

    q2_o[...] = part(0)
    q2_o.send()
    for i in range(2):
        kv2_o[:, i, :] = part(1 + i)
    kv2_o.send()
    out2_o[...] = part(3)
    out2_o.send()
    for i in range(3):
        qkv_o[i] = part(4 + i)
    qkv_o.send()
    out_o[...] = part(7)


def join_rows(keys, clips, scalars, ins, outs):
    (out_o,) = outs
    value = total(ins)
    half = value.shape[1] // 2
    out_o[...] = value.astype(BF16)
    cond = value[keys : keys + clips, :half] + value[keys : keys + clips, half:]
    high = cond.astype(BF16)
    out_o[keys : keys + clips, :half] = high
    out_o[keys : keys + clips, half:] = (cond - high.astype(F32)).astype(BF16)


def place_captions(clips, scalars, ins, outs):
    (cap_len,) = scalars
    parts, condition = ins
    out_o, cond_o, rows = outs
    slots = out_o.shape[2]
    keys, feats = rows.shape
    blocks = parts.shape[0]
    size = keys // blocks
    half = cond_o.shape[1] // blocks
    wide = parts.shape[2] // 2
    conds = []
    for m in range(blocks):
        rows[m * size : (m + 1) * size] = parts[m, :size, :feats]
        value = parts[m, size : size + clips].astype(F32)
        conds.append(value[:, :half] + value[:, wide : wide + half])
    value = condition[...]
    sig = jax.nn.sigmoid(value)
    cond_o[...] = jnp.concatenate(conds, axis=1) * (sig + value * sig * (1.0 - sig))
    cond_o.send()
    slot = lax.broadcasted_iota(jnp.int32, (keys, slots), 1)
    key = lax.broadcasted_iota(jnp.int32, (keys, slots), 0)
    target = out_o.bufs[0]

    def some(c, start):
        pick = (slot + start == key) & (slot < cap_len[c])
        target[c] = dot_tn(rows[...], jnp.where(pick, 1.0, 0.0).astype(BF16))
        return start + cap_len[c]

    lax.fori_loop(0, clips, some, jnp.int32(0))


def ada_grads(scalars, ins, outs):
    mod_cols, scaled, w_ada = ins
    grad_o, cond_o = outs
    high = mod_cols[...].astype(BF16)
    low = (mod_cols[...] - high.astype(F32)).astype(BF16)
    grad_o[...] = dot_tn(scaled[...], high) + dot_tn(scaled[...], low)
    grad_o.send()
    cond = split_dot(dot_nt, mod_cols[...], w_ada[...])
    top = cond.astype(BF16)
    half = cond_o.shape[1] // 2
    cond_o[...] = jnp.zeros(cond_o.shape, BF16)
    cond_o[:, : cond.shape[1]] = top
    cond_o[:, half : half + cond.shape[1]] = (cond - top.astype(F32)).astype(BF16)


def after(value, *first):
    return lax.optimization_barrier((value,) + first)[0]


def tp_gather(value, tp):
    return [value] + [
        lax.ppermute(value, "tp", [(i, (i + k) % tp) for i in range(tp)]) for k in range(1, tp)
    ]


def tp_scatter(chunks, tp):
    return [chunks[0]] + [
        lax.ppermute(chunks[r], "tp", [(i, (i - r) % tp) for i in range(tp)]) for r in range(1, tp)
    ]


def seq_xor(value, mask, nseq):
    return lax.ppermute(value, "seq", [(i, i ^ mask) for i in range(nseq)])


def seq_total(value, nseq):
    mask = 1
    while mask < nseq:
        value = value + seq_xor(value, mask, nseq)
        mask *= 2
    return value


def far_gather(value, nseq):
    return [value] + [seq_xor(value, m, nseq) for m in range(2, nseq, 2)]


def near_gather(far, nseq):
    pieces = []
    for value in far:
        pieces += [value, seq_xor(value, 1, nseq)]
    return pieces


def padded(value, size, axis):
    if value.shape[axis] == size:
        return value
    pads = [(0, 0)] * value.ndim
    pads[axis] = (0, size - value.shape[axis])
    return jnp.pad(value, pads)


def shards(
    tokens,
    cotangent,
    caption,
    condition,
    frames,
    cap_len,
    clip_of,
    w_qkv,
    w_out,
    w_query2,
    w_kv2,
    w_out2,
    w_up,
    w_down,
    w_ada,
):
    tp, nseq = lax.axis_size("tp"), lax.axis_size("seq")
    me, spot = lax.axis_index("tp"), lax.axis_index("seq")
    seqs, fmax, width = tokens.shape
    clips, slots = caption.shape[:2]
    inner, hid = w_query2.shape[1], w_up.shape[1]
    heads = inner // HDIM
    drows = w_query2.shape[0]
    own_seqs = seqs // tp
    own = -(-own_seqs * fmax // 8) * 8
    rows = tp * own
    clip_pad = 8
    keys = -(-(clips * slots // 2) // 128) * 128
    mod_size = 6 * width // tp
    rank = jnp.stack([me, spot]).astype(jnp.int32)
    part = functools.partial

    tok, g3, hot, row_clip, row_id, key_id, live, turned = call(
        part(prepare_rows, tp),
        [
            sds((rows, width)),
            sds((rows, width)),
            sds((rows, clip_pad)),
            sds((rows, 1), jnp.int32),
            sds((rows, 1), jnp.int32),
            sds((1, rows), jnp.int32),
            sds((rows, 1), F32),
            sds((clip_pad, rows)),
        ],
        [tokens.transpose(1, 0, 2), cotangent.transpose(1, 0, 2)],
        work=[sds((tp, own, width))],
        smem=[rank, clip_of, frames],
        name="prepare_rows",
    )
    cap, key_clip = call(
        live_captions,
        [sds((keys, width)), sds((1, keys), jnp.int32)],
        [caption],
        smem=[cap_len],
        name="live_captions",
    )
    lane = lambda n: -(-n // 128) * 128
    section = jnp.concatenate(
        [padded(w_query2, lane(inner), 1), w_kv2.reshape(drows, 2 * inner)], axis=1
    )
    full_b = lax.all_gather(section, "seq", axis=0, tiled=True)
    pack_a = jnp.concatenate([w_qkv.reshape(drows, 3 * inner), w_out.T], axis=1)
    scaled = jax.nn.silu(condition).astype(BF16)
    scaled_own = lax.dynamic_slice_in_dim(scaled, spot * drows, drows, 1)
    mod_part = jnp.dot(scaled_own, w_ada, preferred_element_type=F32)
    mod_part = seq_total(mod_part, nseq)
    far_a = far_gather(after(pack_a, mod_part), nseq)
    z_pack = jnp.concatenate([w_query2, w_out2.T], axis=1)
    groups = mod_size // (2 * inner)
    high = lax.reduce_precision(mod_part, 8, 7)
    mod_rows = [
        part_[:, g * 2 * inner : (g + 1) * 2 * inner].astype(BF16)
        for part_ in (high, mod_part - high)
        for g in range(groups)
    ]
    z_rest = tp_gather(jnp.concatenate([z_pack] + mod_rows, axis=0), tp)
    z_rest = lax.optimization_barrier((*z_rest, tok, cap, *far_a[1:]))[:tp]
    (mods,) = call(
        part(modulations, tp, clips, drows),
        [sds((6, clip_pad, width), F32)],
        [Near(p) for p in z_rest],
        smem=[rank],
        name="modulations",
    )
    z_q2 = [p[:drows, :inner] for p in z_rest[1:]]
    z_out2 = [p[:drows, inner:] for p in z_rest]
    pack_c = jnp.concatenate(
        z_out2 + [padded(w_up, lane(hid), 1), padded(w_down.T, lane(hid), 1)], axis=1
    )
    full_c = lax.all_gather(pack_c, "seq", axis=0, tiled=True)
    full_d = lax.all_gather(jnp.concatenate(z_q2, axis=1), "seq", axis=0, tiled=True)
    w_q2 = Cols(full_b, 0, lane(inner))
    w_kv = Cols(full_b, lane(inner), 2 * inner)
    w_d = Cols(full_d, 0, full_d.shape[1])

    w_a = Blocks(near_gather(far_a, nseq))

    outs = call(
        part(frame_forward, tp),
        [
            sds((rows, width)),
            sds((rows, 3 * inner)),
            sds((heads, rows, rows)),
            sds((rows, inner)),
        ]
        + [sds((own, width))] * tp,
        [tok, hot, mods, row_id, key_id, w_a],
        smem=[rank],
        work=[sds((3, heads, rows, HDIM)), sds((heads, rows, HDIM))],
        name="frame_forward",
    )
    attn_in, qkv, probs, frame_out = outs[:4]
    branch_parts = tp_scatter(outs[4:], tp)
    x1_own, low_own, own_b1 = call(
        part(first_rows, tp),
        [sds((own, width), F32), sds((own, width)), sds((own, width), F32)],
        [*far(branch_parts), tok, hot, mods],
        name="first_rows",
    )
    low_parts = tp_gather(low_own, tp)
    (kv,) = call(
        key_values,
        [sds((keys, 2 * inner))],
        [cap, w_kv],
        name="key_values",
    )
    first_low, cq, cprobs, cross_out, cross_pack = call(
        part(cross_forward, tp, inner),
        [
            sds((rows, width)),
            sds((rows, inner)),
            sds((heads, rows, keys)),
            sds((rows, inner)),
            sds((own, tp * inner)),
        ],
        [*far(low_parts), row_clip, key_clip, w_q2, kv],
        work=[
            sds((heads, rows, HDIM)),
            sds((2, heads, keys, HDIM)),
            sds((heads, rows, HDIM)),
        ],
        name="cross_forward",
    )
    cross_parts = tp_gather(cross_pack, tp)
    outs = call(
        part(mlp_both, tp, inner),
        [
            sds((own, width), F32),
            sds((rows, width)),
            sds((rows, hid)),
            sds((rows, width)),
            sds((rows, hid)),
        ]
        + [sds((clip_pad, width), F32)]
        + [sds((own, width))] * (2 * tp),
        [
            *far(cross_parts),
            x1_own,
            first_low,
            g3,
            hot,
            mods,
            Cols(full_c, 0, width),
            Cols(full_c, width, lane(hid)),
            Cols(full_c, width + lane(hid), lane(hid)),
            turned,
        ],
        smem=[rank],
        name="mlp_both",
    )
    x2_own, mlp_in, hidden, d_b3, d_pre = outs[:5]
    sum_gate2 = outs[5]
    dm_chunks, b3_chunks = outs[6 : 6 + tp], outs[6 + tp :]

    dm_parts = tp_scatter(dm_chunks, tp)
    (grad_one,) = call(
        part(weight_grads, 2),
        [sds((width, 2 * hid))],
        [mlp_in, d_pre, d_b3, hidden],
        name="grads_mlp",
    )
    g2_own, db2_own, sums_two = call(
        part(second_back, tp),
        [sds((own, width), F32), sds((own, width)), sds((2, clip_pad, width), F32)],
        [*far(dm_parts), x2_own, g3, hot, mods, turned],
        order=[grad_one],
        name="second_back",
    )
    sum_one = lax.psum_scatter(after(grad_one, db2_own), "seq", scatter_dimension=0, tiled=True)
    db2_parts = tp_gather(db2_own, tp)
    d_b2, d_cq, d_kv, dcq_pack, kv_rel = call(
        part(cross_back, tp, inner),
        [
            sds((rows, width)),
            sds((rows, inner)),
            sds((keys, 2 * inner)),
            sds((own, tp * inner)),
            sds((nseq, keys // nseq, 2 * inner)),
        ],
        [*far(db2_parts), Cols(full_c, 0, lane(inner)), cprobs, kv, cq],
        work=[
            sds((heads, rows, HDIM)),
            sds((2, heads, keys, HDIM)),
            sds((heads, rows, HDIM)),
            sds((heads, rows, HDIM)),
            sds((heads, rows, keys)),
            sds((2, heads, keys, HDIM)),
        ],
        smem=[rank],
        name="cross_back",
    )
    dcq_parts = tp_gather(dcq_pack, tp)
    (grad_two,) = call(
        part(weight_grads, 3),
        [Half((width, 2 * lane(4 * inner)), 0, lane(4 * inner))],
        [first_low, d_cq, cap, d_kv, d_b2, cross_out],
        name="grads_cross",
    )
    half = nseq // 2
    kv_away = seq_xor(kv_rel[half:], 1, nseq)
    kv_sums = (kv_rel[:half].astype(F32) + kv_away.astype(F32)).astype(BF16)
    kv_own = kv_sums[0].astype(F32)
    for c in range(1, half):
        kv_own = kv_own + seq_xor(kv_sums[c], 2 * c, nseq).astype(F32)
    kv_own = kv_own.astype(BF16)
    outs = call(
        part(frame_back, tp, inner),
        [sds((own, width), F32), sds((rows, width)), sds((rows, 3 * inner))]
        + [sds((own + clip_pad * -(-mod_size // width), width))] * tp,
        [
            *far(dcq_parts),
            d_b2,
            g2_own,
            hot,
            mods,
            w_q2,
            w_d,
            w_a,
            qkv,
            probs,
            tok,
            own_b1,
            sums_two,
            sum_gate2,
            turned,
        ],
        smem=[rank],
        order=[Near(kv_sums)],
        work=[
            sds((3, heads, rows, HDIM)),
            sds((heads, rows, HDIM)),
            sds((3, heads, rows, HDIM)),
            sds((rows, width)),
            sds((rows, width), F32),
            sds((3, clip_pad, width), F32),
        ],
        name="frame_back",
    )
    g1_own, d_b1, d_qkv = outs[:3]
    da_chunks = outs[3:]
    b3_parts = tp_scatter([after(b, grad_two, *dcq_parts[1:]) for b in b3_chunks], tp)
    da_parts = tp_scatter([after(d, *b3_parts[1:]) for d in da_chunks], tp)
    (grad_three,) = call(
        part(weight_grads, 2),
        [Half((width, 2 * lane(4 * inner)), lane(4 * inner), lane(4 * inner))],
        [attn_in, d_qkv, d_b1, frame_out],
        order=[grad_two],
        keep=True,
        name="grads_frame",
    )
    sum_rest = lax.psum_scatter(
        after(grad_three, *da_parts[1:]), "seq", scatter_dimension=0, tiled=True
    )
    grad_up, grad_down = call(
        finish_mlp,
        [sds((drows, hid), F32), sds((drows, hid), F32)],
        [sum_one],
        name="finish_mlp",
    )
    feats = width // tp
    cap_chunks = call(
        part(caption_chunks, tp),
        [sds((keys // nseq, feats))] * tp,
        [w_kv, Near(kv_own)],
        smem=[rank],
        name="caption_chunks",
    )
    both_own, mod_cols = call(
        part(token_rows, tp),
        [sds((2 * own, width)), sds((clip_pad, mod_size), F32)],
        [*far(da_parts), *far(b3_parts), tok, g1_own, hot, mods, x2_own, live],
        order=[grad_three, grad_up, cap_chunks[0]],
        name="token_rows",
    )
    both_parts = tp_gather(both_own, tp)
    mod_cols = seq_total(mod_cols, nseq)

    span = max(feats, 2 * drows)
    grad_ada, cond_rows = call(
        ada_grads,
        [sds(w_ada.shape, F32), sds((clip_pad, span))],
        [Near(mod_cols), Near(padded(scaled_own, clip_pad, 0)), w_ada],
        name="ada_grads",
    )
    shared = [jnp.concatenate([padded(c, span, 1), cond_rows], axis=0) for c in cap_chunks]
    shared = tp_scatter([after(c, *both_parts[1:]) for c in shared], tp)
    (block,) = call(
        part(join_rows, keys // nseq, clips),
        [sds((keys // nseq + clip_pad, span))],
        far(shared),
        name="join_rows",
    )
    blocks = lax.all_gather(block, "seq", axis=0)
    d_tokens, output = call(
        part(place_rows, tp),
        [sds((fmax, seqs, width))] * 2,
        far(both_parts),
        work=[sds((tp, 2 * own, width))],
        smem=[rank],
        name="place_rows",
    )

    d_caption, d_condition = call(
        part(place_captions, clips),
        [sds((clips, feats, slots), F32), sds((clips, width), F32)],
        [Near(blocks), condition],
        work=[sds((keys, feats))],
        smem=[cap_len],
        order=[output, grad_ada],
        name="place_captions",
    )

    grad_q2, grad_kv2, grad_out2, grad_qkv, grad_out = call(
        finish_rest,
        [
            sds((drows, inner), F32),
            sds((drows, 2, inner), F32),
            sds((drows, inner), F32),
            sds((3, drows, inner), F32),
            sds((drows, inner), F32),
        ],
        [sum_rest],
        order=[d_caption],
        name="finish_rest",
    )

    return (
        output.transpose(1, 0, 2),
        d_tokens.transpose(1, 0, 2),
        d_caption.transpose(0, 2, 1),
        d_condition,
        grad_qkv.transpose(1, 0, 2),
        grad_out.T,
        grad_q2,
        grad_kv2,
        grad_out2.T,
        grad_up,
        grad_down.T,
        grad_ada,
    )


def solution(mesh):
    return jax.shard_map(
        shards,
        mesh=mesh,
        in_specs=(
            P("seq", None, None),
            P("seq", None, None),
            P(),
            P(),
            P(),
            P(),
            P("seq"),
            P("seq", None, "tp"),
            P("tp", "seq"),
            P("seq", "tp"),
            P("seq", None, "tp"),
            P("tp", "seq"),
            P("seq", "tp"),
            P("tp", "seq"),
            P("seq", "tp"),
        ),
        out_specs=(
            P("seq", None, None),
            P("seq", None, None),
            P(None, None, "tp"),
            P(),
            P("seq", None, "tp"),
            P("tp", "seq"),
            P("seq", "tp"),
            P("seq", None, "tp"),
            P("tp", "seq"),
            P("seq", "tp"),
            P("tp", "seq"),
            P("seq", "tp"),
        ),
        check_vma=False,
    )
```

```python
import functools
import math

import jax
import jax.numpy as jnp
from jax import lax
from jax.experimental import pallas as pl
from jax.experimental.pallas import tpu as pltpu
from jax.sharding import PartitionSpec as P

HDIM = 72
EPSILON = 1e-06
NEG_FILL = -1e30
F32 = jnp.float32
BF16 = jnp.bfloat16
SCALE = HDIM ** (-0.5)
VMEM_LIMIT = 48 << 20


def dot_nn(a, b):
    return lax.dot_general(a, b, (((1,), (0,)), ((), ())), preferred_element_type=F32)


def dot_nt(a, b):
    return lax.dot_general(a, b, (((1,), (1,)), ((), ())), preferred_element_type=F32)


def dot_tn(a, b):
    return lax.dot_general(a, b, (((0,), (0,)), ((), ())), preferred_element_type=F32)


def sds(shape, dtype=BF16):
    return jax.ShapeDtypeStruct(shape, dtype)


class Blocks:
    def __init__(self, pieces):
        self.pieces = pieces


class Cols:
    def __init__(self, whole, start, size):
        self.whole, self.start, self.size = whole, start, size


class Near:
    def __init__(self, whole):
        self.whole = whole


class Half:
    def __init__(self, shape, start, size):
        self.shape, self.dtype, self.start, self.size = shape, BF16, start, size


class In:
    def __init__(self, buf, copies):
        self.buf, self.copies, self.ready = buf, copies, not copies

    @property
    def shape(self):
        return self.buf.shape

    def ref(self):
        if not self.ready:
            for copy in self.copies:
                copy.wait()
            self.ready = True
        return self.buf

    def __getitem__(self, index):
        return self.ref()[index]


class Out:
    def __init__(self, bufs, copies):
        self.bufs, self.copies, self.sent = bufs, copies, False

    @property
    def shape(self):
        return self.bufs[0].shape

    def __getitem__(self, index):
        return self.bufs[0][index]

    def __setitem__(self, index, value):
        self.bufs[0][index] = value

    def send(self):
        if not self.sent:
            for copy in self.copies:
                copy.start()
            self.sent = True


def call(body, outs, ins, *, name, smem=(), order=(), keep=False, work=(), limit=VMEM_LIMIT):
    vmem, hbm = pl.BlockSpec(memory_space=pltpu.VMEM), pl.BlockSpec(memory_space=pltpu.HBM)
    pin = lambda value: pltpu.with_memory_space_constraint(value, pltpu.HBM)
    ops, in_specs, in_plan, scratch_in = [], [], [], []
    n_in = 0
    for arg in ins:
        if isinstance(arg, Near):
            in_plan.append((len(ops), None, arg, 0))
            ops.append(arg.whole)
            in_specs.append(vmem)
            continue
        pieces = arg.pieces if isinstance(arg, Blocks) else [arg.whole if isinstance(arg, Cols) else arg]
        shape = pieces[0].shape
        if isinstance(arg, Blocks):
            shape = (shape[0] * len(pieces),) + shape[1:]
        elif isinstance(arg, Cols):
            shape = (shape[0], arg.size)
        in_plan.append((len(ops), len(scratch_in), arg, n_in))
        scratch_in.append(pltpu.VMEM(shape, pieces[0].dtype))
        n_in += len(pieces)
        ops += [pin(p) for p in pieces]
        in_specs += [hbm] * len(pieces)
    n_read = len(ops)
    for arg in order:
        ops.append(arg.whole if isinstance(arg, Near) else pin(arg))
        in_specs.append(vmem if isinstance(arg, Near) else hbm)
    results, out_plan, scratch_out = [], [], []
    n_out = 0
    for out in outs:
        out_plan.append((len(results), len(scratch_out), out, n_out))
        results.append(out)
        wide = (out.shape[0], out.size) if isinstance(out, Half) else out.shape
        scratch_out.append(pltpu.VMEM(wide, out.dtype))
        n_out += 1
    n_s, n_i, n_o = len(smem), len(ops), len(results)

    def kernel(*refs):
        scalars = refs[:n_s]
        src = refs[n_s : n_s + n_read]
        dst = refs[n_s + n_i : n_s + n_i + n_o]
        scratch = refs[n_s + n_i + n_o :]
        bufs = scratch[: len(scratch_in)]
        obufs = scratch[len(scratch_in) : len(scratch_in) + len(scratch_out)]
        extra = list(scratch[len(scratch_in) + len(scratch_out) : -2])
        in_sem, out_sem = scratch[-2:]
        lazy = []
        for start, at, arg, sem in in_plan:
            if at is None:
                lazy.append(In(src[start], []))
                continue
            copies = []
            if isinstance(arg, Blocks):
                rows = src[start].shape[0]
                for m in range(len(arg.pieces)):
                    block = lax.bitwise_xor(scalars[0][1], m)
                    place = bufs[at].at[pl.ds(pl.multiple_of(block * rows, 8), rows)]
                    copies.append(pltpu.make_async_copy(src[start + m], place, in_sem.at[sem + m]))
            else:
                part = src[start]
                if isinstance(arg, Cols):
                    part = part.at[:, pl.ds(arg.start, arg.size)]
                copies.append(pltpu.make_async_copy(part, bufs[at], in_sem.at[sem]))
            for copy in copies:
                copy.start()
            lazy.append(In(bufs[at], copies))
        made = []
        for first, at, out, sem in out_plan:
            place = dst[first]
            if isinstance(out, Half):
                place = place.at[:, pl.ds(out.start, out.size)]
            copy = pltpu.make_async_copy(obufs[at], place, out_sem.at[sem])
            made.append(Out([obufs[at]], [copy]))
        body(scalars, lazy, made + extra)
        for item in lazy:
            if not item.ready:
                item[...]
        for out in made:
            out.send()
        for out in made:
            for copy in out.copies:
                copy.wait()

    moved = sum(a.size * a.dtype.itemsize for a in ops[:n_read])
    moved += sum(math.prod(o.shape) * jnp.dtype(o.dtype).itemsize for o in results)
    return pl.pallas_call(
        kernel,
        out_shape=tuple(pltpu.HBM(o.shape, o.dtype) for o in results),
        in_specs=[pl.BlockSpec(memory_space=pltpu.SMEM)] * n_s + in_specs,
        out_specs=tuple([hbm] * n_o),
        scratch_shapes=scratch_in
        + scratch_out
        + [pltpu.VMEM(w.shape, w.dtype) for w in work]
        + [pltpu.SemaphoreType.DMA((max(n_in, 1),)), pltpu.SemaphoreType.DMA((max(n_out, 1),))],
        input_output_aliases={n_s + n_read: 0} if keep else {},
        compiler_params=pltpu.CompilerParams(vmem_limit_bytes=limit),
        cost_estimate=pl.CostEstimate(flops=0, transcendentals=0, bytes_accessed=moved),
        name=name,
    )(*smem, *ops)


def norm_parts(rows):
    center = rows - jnp.mean(rows, -1, keepdims=True)
    inv = lax.rsqrt(jnp.mean(center * center, -1, keepdims=True) + EPSILON)
    return center * inv, inv


def expand(hot, table):
    high = table.astype(BF16)
    low = (table - high.astype(F32)).astype(BF16)
    return dot_nn(hot, high) + dot_nn(hot, low)


def split_dot(dot, a, b):
    high = a.astype(BF16)
    low = (a - high.astype(F32)).astype(BF16)
    return dot(high, b) + dot(low, b)


def clip_sums(clips_hot, values):
    return dot_nn(clips_hot, values.astype(BF16))


def norm_back(grad, n, inv):
    return inv * (grad - jnp.mean(grad, -1, keepdims=True) - n * jnp.mean(grad * n, -1, keepdims=True))


def softmax_rows(scores):
    top = jnp.max(scores, -1, keepdims=True)
    weights = jnp.exp(scores - top)
    return weights / jnp.sum(weights, -1, keepdims=True)


def pack_rows(out, value, tp):
    own, n = value.shape[0] // tp, value.shape[1]
    for r in range(tp):
        out[:, r * n : (r + 1) * n] = value[r * own : (r + 1) * own]


def unpack_heads(pieces, tp, n):
    pieces = [p[...] for p in pieces]
    rows = []
    for b in range(tp):
        cols = []
        for k in range(tp):
            r = (b - k) % tp
            cols.append(pieces[k][:, r * n : (r + 1) * n])
        rows.append(jnp.concatenate(cols, axis=1))
    return jnp.concatenate(rows, axis=0)


def far(parts):
    return [parts[0]] + [Near(p) for p in parts[1:]]


def put_heads(work, value, start=0):
    for h in range(work.shape[0]):
        work[h] = value[:, start + h * HDIM : start + (h + 1) * HDIM]


def take_heads(work):
    return jnp.concatenate([work[h] for h in range(work.shape[0])], axis=1)


def for_heads(count, body):
    def step(h, carry):
        body(h)
        return carry

    lax.fori_loop(0, count, step, 0)


def for_columns(width, body, most=384):
    size = math.gcd(width, most)

    def step(i, carry):
        body(pl.ds(pl.multiple_of(i * size, size), size))
        return carry

    lax.fori_loop(0, width // size, step, 0)


def total(parts):
    value = parts[0][...].astype(F32)
    for part in parts[1:]:
        value = value + part[...].astype(F32)
    return value


def prepare_rows(tp, scalars, ins, outs):
    rank, clip_of, frames = scalars
    tok_o, g3_o, hot_o, clip_o, id_o, key_o, live_o, turned_o, canon = outs
    rows, width = tok_o.shape
    own = rows // tp
    fmax, seqs = ins[0].shape[:2]
    own_seqs = seqs // tp
    used = own_seqs * fmax
    row = lax.broadcasted_iota(jnp.int32, (own, 1), 0)
    spot = lax.rem(row, own_seqs)
    place = lax.broadcasted_iota(jnp.int32, key_o.shape, 1)
    keys = jnp.full(key_o.shape, -2, jnp.int32)
    owner = jnp.full(key_o.shape, -1, jnp.int32)
    alive = []
    for k in range(tp):
        base = lax.rem(rank[0] - k + tp, tp) * own_seqs
        at = slice(k * own, (k + 1) * own)
        clip = jnp.full((own, 1), -1, jnp.int32)
        name = jnp.full((own, 1), -1, jnp.int32)
        limit = jnp.zeros((own, 1), jnp.int32)
        inside = place - k * own
        mine = (inside >= 0) & (inside < used)
        turn = lax.rem(jnp.maximum(inside, 0), own_seqs)
        for j in range(own_seqs):
            c = clip_of[base + j]
            count = frames[c] * own_seqs
            here = (spot == j) & (row < used)
            clip = jnp.where(here, c, clip)
            name = jnp.where(here, k * own_seqs + j, name)
            limit = jnp.where(here, count, limit)
            there = mine & (turn == j)
            owner = jnp.where(there, c, owner)
            keys = jnp.where(there & (inside < count), k * own_seqs + j, keys)
        live = jnp.where(row < limit, 1.0, 0.0)
        alive.append(live)
        live_o[at] = live
        clip_o[at] = clip
        id_o[at] = name
        lane = lax.broadcasted_iota(jnp.int32, (own, hot_o.shape[1]), 1)
        hot_o[at] = jnp.where(lane == clip, 1.0, 0.0).astype(BF16)
    key_o[...] = keys
    which = lax.broadcasted_iota(jnp.int32, turned_o.shape, 0)
    turned_o[...] = jnp.where(which == owner, 1.0, 0.0).astype(BF16)
    for source, out, mask in ((ins[0], tok_o, False), (ins[1], g3_o, True)):
        if own > used:
            canon[:, used:] = jnp.zeros((tp, own - used, width), BF16)
        for f in range(fmax):
            for q in range(tp):
                group = source[f, q * own_seqs : (q + 1) * own_seqs]
                canon[q, f * own_seqs : (f + 1) * own_seqs] = group
        for k in range(tp):
            value = canon[lax.rem(rank[0] - k + tp, tp)]
            if mask:
                value = (value.astype(F32) * alive[k]).astype(BF16)
            out[k * own : (k + 1) * own] = value
        out.send()


def live_captions(scalars, ins, outs):
    (cap_len,) = scalars
    (caption,) = ins
    cap_o, clip_o = outs
    keys = cap_o.shape[0]
    clips, slots = caption.shape[:2]
    col = lax.broadcasted_iota(jnp.int32, (1, keys), 1)
    clip = jnp.full((1, keys), -9, jnp.int32)
    start = jnp.int32(0)
    spans = []
    for c in range(clips):
        end = start + cap_len[c]
        clip = jnp.where((col >= start) & (col < end), c, clip)
        spans.append((start, end))
        start = end
    clip_o[...] = clip
    source, target = caption.ref(), cap_o.bufs[0]
    step = math.gcd(keys, 128)

    def some(i, carry):
        row = lax.broadcasted_iota(jnp.int32, (step, slots), 0) + i * step
        slot = lax.broadcasted_iota(jnp.int32, (step, slots), 1)
        value = jnp.zeros((step, target.shape[1]), F32)
        for c, (begin, end) in enumerate(spans):
            pick = (row - begin == slot) & (row < end)
            value = value + dot_nn(jnp.where(pick, 1.0, 0.0).astype(BF16), source[c])
        target[pl.ds(pl.multiple_of(i * step, step), step)] = value.astype(BF16)
        return carry

    lax.fori_loop(0, keys // step, some, 0)


def modulations(tp, clips, first, scalars, ins, outs):
    (rank,) = scalars
    (mods_o,) = outs
    width = mods_o.shape[2]
    groups = (ins[0].shape[0] - first) // (2 * clips)

    def joined(ref):
        cols = []
        for g in range(groups):
            at = first + g * clips
            high = ref[at : at + clips].astype(F32)
            cols.append(high + ref[at + groups * clips : at + (groups + 1) * clips].astype(F32))
        return jnp.concatenate(cols, axis=1)

    parts = [joined(ref) for ref in ins]
    cols = []
    for q in range(tp):
        value = parts[0]
        for k in range(1, tp):
            value = jnp.where(lax.rem(rank[0] - k + tp, tp) == q, parts[k], value)
        cols.append(value)
    whole = jnp.concatenate(cols, axis=1)
    mods_o[...] = jnp.zeros(mods_o.shape, F32)
    for j in range(6):
        mods_o[j, :clips] = whole[:, j * width : (j + 1) * width]


def frame_forward(tp, scalars, ins, outs):
    tok, hot, mods, row_id, key_id, w_a = ins
    attn_o, qkv_o, prob_o, fo_o = outs[:4]
    branch_o = outs[4:-2]
    heads, made = outs[-2:]
    inner = fo_o.shape[1]
    own = branch_o[0].shape[0]
    n, _ = norm_parts(tok[...].astype(F32))
    low = (n * (1.0 + expand(hot[...], mods[1])) + expand(hot[...], mods[0])).astype(BF16)
    attn_o[...] = low
    attn_o.send()
    qkv = dot_nn(low, w_a[:, : 3 * inner]).astype(BF16)
    qkv_o[...] = qkv
    qkv_o.send()
    allowed = row_id[...] == key_id[...]
    for i in range(3):
        put_heads(heads.at[i], qkv, i * inner)
    prob = prob_o.bufs[0]

    def one(h):
        scores = dot_nt(heads[0, h], heads[1, h]) * SCALE
        probs = softmax_rows(jnp.where(allowed, scores, NEG_FILL)).astype(BF16)
        prob[h] = probs
        made[h] = dot_nn(probs, heads[2, h]).astype(BF16)

    for_heads(inner // HDIM, one)
    result = take_heads(made)
    prob_o.send()
    fo_o[...] = result
    fo_o.send()
    weights, low_out = w_a.ref(), fo_o.bufs[0]

    def last(cols):
        branch = dot_nt(low_out[...], weights[cols, 3 * inner : 4 * inner]).astype(BF16)
        for r in range(tp):
            branch_o[r].bufs[0][:, cols] = branch[r * own : (r + 1) * own]

    for_columns(weights.shape[0], last)
    for out in branch_o:
        out.send()


def first_rows(tp, scalars, ins, outs):
    tok, hot, mods = ins[tp:]
    x1_o, low_o, branch_o = outs
    own = x1_o.shape[0]
    gate = expand(hot[:own], mods[2])
    branch = total(ins[:tp])
    branch_o[...] = branch
    branch_o.send()
    first = tok[:own].astype(F32) + gate * branch
    x1_o[...] = first
    low_o[...] = first.astype(BF16)


def key_values(scalars, ins, outs):
    cap, w_kv = (item.ref() for item in ins)
    kv = outs[0].bufs[0]
    step = math.gcd(kv.shape[0], 128)

    def some(i, carry):
        at = pl.ds(pl.multiple_of(i * step, 16), step)
        kv[at] = dot_nn(cap[at], w_kv[...]).astype(BF16)
        return carry

    lax.fori_loop(0, kv.shape[0] // step, some, 0)


def cross_forward(tp, inner, scalars, ins, outs):
    row_clip, key_clip, w_q2, kv = ins[tp:]
    low_o, cq_o, prob_o, co_o, pack_o, query, pair, made = outs
    low = jnp.concatenate([r[...] for r in ins[:tp]], axis=0)
    low_o[...] = low
    low_o.send()
    cq = dot_nn(low, w_q2[:, :inner]).astype(BF16)
    cq_o[...] = cq
    cq_o.send()
    allowed = row_clip[...] == key_clip[...]
    put_heads(query, cq)
    for i in range(2):
        put_heads(pair.at[i], kv.ref(), i * inner)
    prob = prob_o.bufs[0]

    def one(h):
        scores = jnp.where(allowed, dot_nt(query[h], pair[0, h]) * SCALE, NEG_FILL)
        probs = softmax_rows(scores).astype(BF16)
        prob[h] = probs
        made[h] = dot_nn(probs, pair[1, h]).astype(BF16)

    for_heads(inner // HDIM, one)
    result = take_heads(made)
    pack_rows(pack_o, result, tp)
    pack_o.send()
    prob_o.send()
    co_o[...] = result


GELU_C = 0.7978845608028654


def mlp_both(tp, inner, scalars, ins, outs):
    pieces = ins[:tp]
    hot, mods, g3, w_out2, first, low_first, w_up, w_down, turned = ins[tp:]
    x2_o, mlp_o, hid_o, db3_o, dpre_o, sums_o = outs[:6]
    dm_o, b3_o = outs[6 : 6 + tp], outs[6 + tp :]
    own, width = x2_o.shape
    hid = hid_o.shape[1]
    d_b3 = (expand(hot[...], mods[5]) * g3[...].astype(F32)).astype(BF16)
    db3_o[...] = d_b3
    db3_o.send()
    rows = unpack_heads(pieces, tp, inner)
    branch = dot_nt(rows, w_out2[...])
    second = jnp.concatenate(
        [first[...] + branch[:own], low_first[own:].astype(F32) + branch[own:]], axis=0
    )
    x2_o[...] = second[:own]
    x2_o.send()
    n, _ = norm_parts(second)
    mlp_o[...] = (n * (1.0 + expand(hot[...], mods[4])) + expand(hot[...], mods[3])).astype(BF16)
    mlp_o.send()
    low, d_low, hiddens, d_pres = (o.bufs[0] for o in (mlp_o, db3_o, hid_o, dpre_o))
    up, down = w_up.ref(), w_down.ref()

    def some(cols):
        pre = dot_nn(low[...], up[:, cols])
        th = jnp.tanh(GELU_C * (pre + 0.044715 * (pre * pre * pre)))
        hiddens[:, cols] = (0.5 * pre * (1.0 + th)).astype(BF16)
        slope = 0.5 * (1.0 + th) + 0.5 * pre * (1.0 - th * th) * (
            GELU_C * (1.0 + 3.0 * 0.044715 * (pre * pre))
        )
        d_pres[:, cols] = (slope * dot_nn(d_low[...], down[:, cols])).astype(BF16)

    if hid % 128:
        some(slice(0, hid))
    else:
        for_columns(hid, some)
    hid_o.send()
    dpre_o.send()
    turn, held, found = turned[...], g3.ref(), sums_o.bufs[0]

    def back(cols):
        d_m = dot_nt(d_pres[...], up[cols, :hid]).astype(BF16)
        for r in range(tp):
            dm_o[r].bufs[0][:, cols] = d_m[r * own : (r + 1) * own]

    for_columns(width, back)
    for out in dm_o:
        out.send()

    def ahead(cols):
        b3 = dot_nt(hiddens[...], down[cols, :hid]).astype(BF16)
        for r in range(tp):
            b3_o[r].bufs[0][:, cols] = b3[r * own : (r + 1) * own]
        found[:, cols] = clip_sums(turn, b3.astype(F32) * held[:, cols].astype(F32))

    for_columns(width, ahead)


def second_back(tp, scalars, ins, outs):
    x2, g3, hot, mods, turned = ins[tp:]
    g2_o, db2_o, sums_o = outs
    own = g2_o.shape[0]
    n, inv = norm_parts(x2[...])
    scale = 1.0 + expand(hot[:own], mods[4])
    d_m = total(ins[:tp])
    g2 = g3[:own].astype(F32) + norm_back(d_m * scale, n, inv)
    db2_o[...] = g2.astype(BF16)
    db2_o.send()
    g2_o[...] = g2
    sums_o[0] = clip_sums(turned[:, :own], d_m)
    sums_o[1] = clip_sums(turned[:, :own], d_m * n)


def cross_back(tp, inner, scalars, ins, outs):
    (rank,) = scalars
    w_out2, prob, kv, cq = ins[tp:]
    db2_o, dcq_o, dkv_o, pack_o, rel_o, query, pair, grads, made, scores, back = outs
    d_b2 = jnp.concatenate([r[...] for r in ins[:tp]], axis=0)
    db2_o[...] = d_b2
    db2_o.send()
    d_co = dot_nn(d_b2, w_out2[:, :inner]).astype(BF16)
    put_heads(grads, d_co)
    put_heads(query, cq.ref())
    for i in range(2):
        put_heads(pair.at[i], kv.ref(), i * inner)
    probs = prob.ref()

    def one(h):
        wide = probs[h].astype(F32)
        d_p = dot_nt(grads[h], pair[1, h])
        d_s = (wide * (d_p - jnp.sum(wide * d_p, -1, keepdims=True))).astype(BF16)
        scores[h] = d_s
        made[h] = (dot_nn(d_s, pair[0, h]) * SCALE).astype(BF16)

    for_heads(inner // HDIM, one)
    result = take_heads(made)
    pack_rows(pack_o, result, tp)
    pack_o.send()
    dcq_o[...] = result
    dcq_o.send()

    def two(h):
        back[0, h] = (dot_tn(scores[h], query[h]) * SCALE).astype(BF16)
        back[1, h] = dot_tn(probs[h], grads[h]).astype(BF16)

    for_heads(inner // HDIM, two)
    d_kv = jnp.concatenate([take_heads(back.at[0]), take_heads(back.at[1])], axis=1)
    blocks, size = rel_o.shape[:2]
    for b in range(blocks):
        other = lax.bitwise_xor(rank[1], b)
        rel_o[(other % 2) * (blocks // 2) + other // 2] = d_kv[b * size : (b + 1) * size]
    rel_o.send()
    dkv_o[...] = d_kv


def frame_back(tp, inner, scalars, ins, outs):
    pieces = ins[:tp]
    (rank,) = scalars
    w_q2, w_far, hot, mods, d_b2, g2, w_a, qkv, prob, tok, own_b1, sums, gate2, turned = ins[tp:]
    g1_o, db1_o, dqkv_o = outs[:3]
    da_o = outs[3:-6]
    heads, grads, made, cqs, norms, found = outs[-6:]
    own, width = g1_o.shape
    d_cq = unpack_heads(pieces, tp, inner)
    cqs[...] = d_cq
    near_w, far_w, held, second, table = (r.ref() for r in (w_q2, w_far, d_b2, g2, mods))
    pick = hot[...]
    g1s, d_b1s = g1_o.bufs[0], db1_o.bufs[0]

    def first(cols):
        d_x1 = dot_nt(cqs[:, :inner], near_w[cols, :inner]) + dot_nt(cqs[:, inner:], far_w[cols])
        g1s[:, cols] = second[:, cols] + d_x1[:own]
        gate = expand(pick, table[2, :, cols])
        d_b1s[:, cols] = (gate * (held[:, cols].astype(F32) + d_x1)).astype(BF16)

    for_columns(width, first)
    g1_o.send()
    db1_o.send()
    d_fo = dot_nn(d_b1s[...], w_a[:, 3 * inner : 4 * inner]).astype(BF16)
    put_heads(grads, d_fo)
    for i in range(3):
        put_heads(heads.at[i], qkv.ref(), i * inner)
    probs = prob.ref()

    def one(h):
        grad = grads[h]
        wide = probs[h].astype(F32)
        made[2, h] = dot_tn(probs[h], grad).astype(BF16)
        d_p = dot_nt(grad, heads[2, h])
        d_s = (wide * (d_p - jnp.sum(wide * d_p, -1, keepdims=True))).astype(BF16)
        made[0, h] = (dot_nn(d_s, heads[1, h]) * SCALE).astype(BF16)
        made[1, h] = (dot_tn(d_s, heads[0, h]) * SCALE).astype(BF16)

    for_heads(inner // HDIM, one)
    d_qkv = jnp.concatenate([take_heads(made.at[i]) for i in range(3)], axis=1)
    dqkv_o[...] = d_qkv
    d_qkvs = dqkv_o.bufs[0]
    dqkv_o.send()
    n, _ = norm_parts(tok[...].astype(F32))
    norms[...] = n
    weights, turn, extra = w_a.ref(), turned[...], own_b1.ref()

    def last(cols):
        low = dot_nt(d_qkvs[...], weights[cols, : 3 * inner]).astype(BF16)
        for r in range(tp):
            da_o[r].bufs[0][:own, cols] = low[r * own : (r + 1) * own]
        found[0, :, cols] = dot_nn(turn, low)
        found[1, :, cols] = clip_sums(turn, low.astype(F32) * norms[:, cols])
        found[2, :, cols] = clip_sums(turn[:, :own], g1s[:, cols] * extra[:, cols])

    for_columns(width, last)
    shift, scale, gate1 = found[0], found[1], found[2]
    whole = jnp.concatenate([shift, scale, gate1, sums[0], sums[1], gate2[...]], axis=1)
    size = whole.shape[1] // tp
    clips = (da_o[0].shape[0] - own) // -(-size // width)
    for r in range(tp):
        value = whole[:, :size]
        for q in range(1, tp):
            here = lax.rem(rank[0] - r + tp, tp) == q
            value = jnp.where(here, whole[:, q * size : (q + 1) * size], value)
        for g in range(-(-size // width)):
            part = value[:, g * width : (g + 1) * width].astype(BF16)
            da_o[r][own + g * clips : own + (g + 1) * clips, : part.shape[1]] = part
        da_o[r].send()


def token_rows(tp, scalars, ins, outs):
    tok, g1, hot, mods, x2, live = ins[2 * tp :]
    both_o, cols_o = outs
    own, width = g1.shape
    n, inv = norm_parts(tok[:own].astype(F32))
    scale = 1.0 + expand(hot[:own], mods[1])
    gate = expand(hot[:own], mods[5])
    sums = total(ins[:tp])
    both_o[:own] = (g1[...] + norm_back(sums[:own] * scale, n, inv)).astype(BF16)
    both_o[own:] = ((x2[...] + gate * total(ins[tp : 2 * tp])) * live[:own]).astype(BF16)
    both_o.send()
    clips, size = cols_o.shape
    for g in range(-(-size // width)):
        at = own + g * clips
        part = sums[at : at + clips, : size - g * width]
        cols_o[:, g * width : g * width + part.shape[1]] = part


def place_rows(tp, scalars, ins, outs):
    (rank,) = scalars
    results, canon = outs[:-1], outs[-1]
    fmax, seqs = results[0].shape[:2]
    own_seqs = seqs // tp
    own = ins[0].shape[0] // 2
    for k in range(tp):
        canon[lax.rem(rank[0] - k + tp, tp)] = ins[k][...]
    for i, out in enumerate(results):
        for f in range(fmax):
            for q in range(tp):
                at = i * own + f * own_seqs
                out[f, q * own_seqs : (q + 1) * own_seqs] = canon[q, at : at + own_seqs]
        out.send()


def weight_grads(pairs, scalars, ins, outs):
    out = outs[0].bufs[0]
    refs = [item.ref() for item in ins]
    step = math.gcd(out.shape[0], 128)
    filled = sum(refs[2 * j + 1].shape[1] for j in range(pairs))
    if filled < out.shape[1]:
        out[:, filled:] = jnp.zeros((out.shape[0], out.shape[1] - filled), BF16)

    def some(i, carry):
        at = pl.ds(pl.multiple_of(i * step, step), step)
        start = 0
        for j in range(pairs):
            left, right = refs[2 * j], refs[2 * j + 1]
            width = right.shape[1]
            out[at, start : start + width] = dot_tn(left[:, at], right[...]).astype(BF16)
            start += width
        return carry

    lax.fori_loop(0, out.shape[0] // step, some, 0)


def finish_mlp(scalars, ins, outs):
    up_o, down_o = outs
    hid = up_o.shape[1]
    value = total(ins)
    up_o[...] = value[:, :hid]
    up_o.send()
    down_o[...] = value[:, hid:]


def caption_chunks(tp, scalars, ins, outs):
    (rank,) = scalars
    w_kv, d_kv = ins
    feats = outs[0].shape[1]
    w_kv[:8]
    for r, out in enumerate(outs):
        block = lax.rem(rank[0] - r + tp, tp)
        at = pl.ds(pl.multiple_of(block * feats, 8), feats)
        out[...] = dot_nt(d_kv[...], w_kv[at, :]).astype(BF16)
        out.send()


def finish_rest(scalars, ins, outs):
    (value,) = ins
    q2_o, kv2_o, out2_o, qkv_o, out_o = outs
    inner = q2_o.shape[1]
    half = value.shape[1] // 2

    def part(i):
        at = (i // 4) * half + (i % 4) * inner
        return value[:, at : at + inner].astype(F32)

    q2_o[...] = part(0)
    q2_o.send()
    for i in range(2):
        kv2_o[:, i, :] = part(1 + i)
    kv2_o.send()
    out2_o[...] = part(3)
    out2_o.send()
    for i in range(3):
        qkv_o[i] = part(4 + i)
    qkv_o.send()
    out_o[...] = part(7)


def join_rows(keys, clips, scalars, ins, outs):
    (out_o,) = outs
    value = total(ins)
    half = value.shape[1] // 2
    out_o[...] = value.astype(BF16)
    cond = value[keys : keys + clips, :half] + value[keys : keys + clips, half:]
    high = cond.astype(BF16)
    out_o[keys : keys + clips, :half] = high
    out_o[keys : keys + clips, half:] = (cond - high.astype(F32)).astype(BF16)


def place_captions(clips, scalars, ins, outs):
    (cap_len,) = scalars
    parts, condition = ins
    out_o, cond_o, rows, turned = outs
    slots = out_o.shape[2]
    keys, feats = rows.shape
    blocks = parts.shape[0]
    size = keys // blocks
    half = cond_o.shape[1] // blocks
    wide = parts.shape[2] // 2
    conds = []
    for m in range(blocks):
        rows[m * size : (m + 1) * size] = parts[m, :size, :feats]
        value = parts[m, size : size + clips].astype(F32)
        conds.append(value[:, :half] + value[:, wide : wide + half])
    value = condition[...]
    sig = jax.nn.sigmoid(value)
    cond_o[...] = jnp.concatenate(conds, axis=1) * (sig + value * sig * (1.0 - sig))
    cond_o.send()
    slot = lax.broadcasted_iota(jnp.int32, (keys, slots), 1)
    key = lax.broadcasted_iota(jnp.int32, (keys, slots), 0)
    target = out_o.bufs[0]
    turned[...] = rows[...].T

    def some(c, start):
        pick = (slot + start == key) & (slot < cap_len[c])
        target[c] = dot_nn(turned[...], jnp.where(pick, 1.0, 0.0).astype(BF16))
        return start + cap_len[c]

    lax.fori_loop(0, clips, some, jnp.int32(0))


def ada_grads(scalars, ins, outs):
    mod_cols, scaled, w_ada = ins
    grad_o, cond_o = outs
    high = mod_cols[...].astype(BF16)
    low = (mod_cols[...] - high.astype(F32)).astype(BF16)
    grad_o[...] = dot_tn(scaled[...], high) + dot_tn(scaled[...], low)
    grad_o.send()
    cond = split_dot(dot_nt, mod_cols[...], w_ada[...])
    top = cond.astype(BF16)
    half = cond_o.shape[1] // 2
    cond_o[...] = jnp.zeros(cond_o.shape, BF16)
    cond_o[:, : cond.shape[1]] = top
    cond_o[:, half : half + cond.shape[1]] = (cond - top.astype(F32)).astype(BF16)


def after(value, *first):
    return lax.optimization_barrier((value,) + first)[0]


def tp_gather(value, tp):
    return [value] + [
        lax.ppermute(value, "tp", [(i, (i + k) % tp) for i in range(tp)]) for k in range(1, tp)
    ]


def tp_scatter(chunks, tp):
    return [chunks[0]] + [
        lax.ppermute(chunks[r], "tp", [(i, (i - r) % tp) for i in range(tp)]) for r in range(1, tp)
    ]


def seq_xor(value, mask, nseq):
    return lax.ppermute(value, "seq", [(i, i ^ mask) for i in range(nseq)])


def seq_total(value, nseq):
    mask = 1
    while mask < nseq:
        value = value + seq_xor(value, mask, nseq)
        mask *= 2
    return value


def far_gather(value, nseq):
    return [value] + [seq_xor(value, m, nseq) for m in range(2, nseq, 2)]


def near_gather(far, nseq):
    pieces = []
    for value in far:
        pieces += [value, seq_xor(value, 1, nseq)]
    return pieces


def padded(value, size, axis):
    if value.shape[axis] == size:
        return value
    pads = [(0, 0)] * value.ndim
    pads[axis] = (0, size - value.shape[axis])
    return jnp.pad(value, pads)


def shards(
    tokens,
    cotangent,
    caption,
    condition,
    frames,
    cap_len,
    clip_of,
    w_qkv,
    w_out,
    w_query2,
    w_kv2,
    w_out2,
    w_up,
    w_down,
    w_ada,
):
    tp, nseq = lax.axis_size("tp"), lax.axis_size("seq")
    me, spot = lax.axis_index("tp"), lax.axis_index("seq")
    seqs, fmax, width = tokens.shape
    clips, slots = caption.shape[:2]
    inner, hid = w_query2.shape[1], w_up.shape[1]
    heads = inner // HDIM
    drows = w_query2.shape[0]
    own_seqs = seqs // tp
    own = -(-own_seqs * fmax // 8) * 8
    rows = tp * own
    clip_pad = 8
    keys = -(-(clips * slots // 2) // 128) * 128
    mod_size = 6 * width // tp
    rank = jnp.stack([me, spot]).astype(jnp.int32)
    part = functools.partial

    tok, g3, hot, row_clip, row_id, key_id, live, turned = call(
        part(prepare_rows, tp),
        [
            sds((rows, width)),
            sds((rows, width)),
            sds((rows, clip_pad)),
            sds((rows, 1), jnp.int32),
            sds((rows, 1), jnp.int32),
            sds((1, rows), jnp.int32),
            sds((rows, 1), F32),
            sds((clip_pad, rows)),
        ],
        [tokens.transpose(1, 0, 2), cotangent.transpose(1, 0, 2)],
        work=[sds((tp, own, width))],
        smem=[rank, clip_of, frames],
        name="prepare_rows",
    )
    cap, key_clip = call(
        live_captions,
        [sds((keys, width)), sds((1, keys), jnp.int32)],
        [caption],
        smem=[cap_len],
        name="live_captions",
    )
    lane = lambda n: -(-n // 128) * 128
    section = jnp.concatenate(
        [padded(w_query2, lane(inner), 1), w_kv2.reshape(drows, 2 * inner)], axis=1
    )
    full_b = lax.all_gather(section, "seq", axis=0, tiled=True)
    pack_a = jnp.concatenate([w_qkv.reshape(drows, 3 * inner), w_out.T], axis=1)
    scaled = jax.nn.silu(condition).astype(BF16)
    scaled_own = lax.dynamic_slice_in_dim(scaled, spot * drows, drows, 1)
    mod_part = jnp.dot(scaled_own, w_ada, preferred_element_type=F32)
    mod_part = seq_total(mod_part, nseq)
    far_a = far_gather(after(pack_a, mod_part), nseq)
    z_pack = jnp.concatenate([w_query2, w_out2.T], axis=1)
    groups = mod_size // (2 * inner)
    high = lax.reduce_precision(mod_part, 8, 7)
    mod_rows = [
        part_[:, g * 2 * inner : (g + 1) * 2 * inner].astype(BF16)
        for part_ in (high, mod_part - high)
        for g in range(groups)
    ]
    z_rest = tp_gather(jnp.concatenate([z_pack] + mod_rows, axis=0), tp)
    z_rest = lax.optimization_barrier((*z_rest, tok, *far_a[1:]))[:tp]
    (mods,) = call(
        part(modulations, tp, clips, drows),
        [sds((6, clip_pad, width), F32)],
        [Near(p) for p in z_rest],
        smem=[rank],
        name="modulations",
    )
    z_q2 = [p[:drows, :inner] for p in z_rest[1:]]
    z_out2 = [p[:drows, inner:] for p in z_rest]
    pack_c = jnp.concatenate(
        z_out2 + [padded(w_up, lane(hid), 1), padded(w_down.T, lane(hid), 1)], axis=1
    )
    full_c = lax.all_gather(pack_c, "seq", axis=0, tiled=True)
    full_d = lax.all_gather(jnp.concatenate(z_q2, axis=1), "seq", axis=0, tiled=True)
    w_q2 = Cols(full_b, 0, lane(inner))
    w_kv = Cols(full_b, lane(inner), 2 * inner)
    w_d = Cols(full_d, 0, full_d.shape[1])

    w_a = Blocks(near_gather(far_a, nseq))

    outs = call(
        part(frame_forward, tp),
        [
            sds((rows, width)),
            sds((rows, 3 * inner)),
            sds((heads, rows, rows)),
            sds((rows, inner)),
        ]
        + [sds((own, width))] * tp,
        [tok, hot, mods, row_id, key_id, w_a],
        smem=[rank],
        work=[sds((3, heads, rows, HDIM)), sds((heads, rows, HDIM))],
        name="frame_forward",
    )
    attn_in, qkv, probs, frame_out = outs[:4]
    branch_parts = tp_scatter(outs[4:], tp)
    x1_own, low_own, own_b1 = call(
        part(first_rows, tp),
        [sds((own, width), F32), sds((own, width)), sds((own, width), F32)],
        [*far(branch_parts), tok, hot, mods],
        order=[cap],
        name="first_rows",
    )
    low_parts = tp_gather(low_own, tp)
    (kv,) = call(
        key_values,
        [sds((keys, 2 * inner))],
        [cap, w_kv],
        name="key_values",
    )
    first_low, cq, cprobs, cross_out, cross_pack = call(
        part(cross_forward, tp, inner),
        [
            sds((rows, width)),
            sds((rows, inner)),
            sds((heads, rows, keys)),
            sds((rows, inner)),
            sds((own, tp * inner)),
        ],
        [*far(low_parts), row_clip, key_clip, w_q2, kv],
        work=[
            sds((heads, rows, HDIM)),
            sds((2, heads, keys, HDIM)),
            sds((heads, rows, HDIM)),
        ],
        name="cross_forward",
    )
    cross_parts = tp_gather(cross_pack, tp)
    outs = call(
        part(mlp_both, tp, inner),
        [
            sds((own, width), F32),
            sds((rows, width)),
            sds((rows, hid)),
            sds((rows, width)),
            sds((rows, hid)),
        ]
        + [sds((clip_pad, width), F32)]
        + [sds((own, width))] * (2 * tp),
        [
            *far(cross_parts),
            hot,
            mods,
            g3,
            Cols(full_c, 0, width),
            x1_own,
            first_low,
            Cols(full_c, width, lane(hid)),
            Cols(full_c, width + lane(hid), lane(hid)),
            turned,
        ],
        smem=[rank],
        name="mlp_both",
    )
    x2_own, mlp_in, hidden, d_b3, d_pre = outs[:5]
    sum_gate2 = outs[5]
    dm_chunks, b3_chunks = outs[6 : 6 + tp], outs[6 + tp :]

    dm_parts = tp_scatter(dm_chunks, tp)
    (grad_one,) = call(
        part(weight_grads, 2),
        [sds((width, 2 * hid))],
        [mlp_in, d_pre, d_b3, hidden],
        name="grads_mlp",
    )
    g2_own, db2_own, sums_two = call(
        part(second_back, tp),
        [sds((own, width), F32), sds((own, width)), sds((2, clip_pad, width), F32)],
        [*far(dm_parts), x2_own, g3, hot, mods, turned],
        order=[grad_one],
        name="second_back",
    )
    sum_one = lax.psum_scatter(after(grad_one, db2_own), "seq", scatter_dimension=0, tiled=True)
    db2_parts = tp_gather(db2_own, tp)
    d_b2, d_cq, d_kv, dcq_pack, kv_rel = call(
        part(cross_back, tp, inner),
        [
            sds((rows, width)),
            sds((rows, inner)),
            sds((keys, 2 * inner)),
            sds((own, tp * inner)),
            sds((nseq, keys // nseq, 2 * inner)),
        ],
        [*far(db2_parts), Cols(full_c, 0, lane(inner)), cprobs, kv, cq],
        work=[
            sds((heads, rows, HDIM)),
            sds((2, heads, keys, HDIM)),
            sds((heads, rows, HDIM)),
            sds((heads, rows, HDIM)),
            sds((heads, rows, keys)),
            sds((2, heads, keys, HDIM)),
        ],
        smem=[rank],
        name="cross_back",
    )
    dcq_parts = tp_gather(dcq_pack, tp)
    (grad_two,) = call(
        part(weight_grads, 3),
        [Half((width, 2 * lane(4 * inner)), 0, lane(4 * inner))],
        [first_low, d_cq, cap, d_kv, d_b2, cross_out],
        name="grads_cross",
    )
    half = nseq // 2
    kv_away = seq_xor(kv_rel[half:], 1, nseq)
    kv_sums = (kv_rel[:half].astype(F32) + kv_away.astype(F32)).astype(BF16)
    outs = call(
        part(frame_back, tp, inner),
        [sds((own, width), F32), sds((rows, width)), sds((rows, 3 * inner))]
        + [sds((own + clip_pad * -(-mod_size // width), width))] * tp,
        [
            *far(dcq_parts),
            w_q2,
            w_d,
            hot,
            mods,
            d_b2,
            g2_own,
            w_a,
            qkv,
            probs,
            tok,
            own_b1,
            sums_two,
            sum_gate2,
            turned,
        ],
        smem=[rank],
        order=[Near(kv_sums)],
        work=[
            sds((3, heads, rows, HDIM)),
            sds((heads, rows, HDIM)),
            sds((3, heads, rows, HDIM)),
            sds((rows, width)),
            sds((rows, width), F32),
            sds((3, clip_pad, width), F32),
        ],
        name="frame_back",
    )
    g1_own, d_b1, d_qkv = outs[:3]
    da_chunks = outs[3:]
    b3_parts = tp_scatter([after(b, grad_two, *dcq_parts[1:]) for b in b3_chunks], tp)
    da_parts = tp_scatter([after(d, *b3_parts[1:]) for d in da_chunks], tp)
    (grad_three,) = call(
        part(weight_grads, 2),
        [Half((width, 2 * lane(4 * inner)), lane(4 * inner), lane(4 * inner))],
        [attn_in, d_qkv, d_b1, frame_out],
        order=[grad_two],
        keep=True,
        name="grads_frame",
    )
    sum_rest = lax.psum_scatter(
        after(grad_three, *da_parts[1:]), "seq", scatter_dimension=0, tiled=True
    )
    grad_up, grad_down = call(
        finish_mlp,
        [sds((drows, hid), F32), sds((drows, hid), F32)],
        [sum_one],
        name="finish_mlp",
    )
    both_own, mod_cols = call(
        part(token_rows, tp),
        [sds((2 * own, width)), sds((clip_pad, mod_size), F32)],
        [*far(da_parts), *far(b3_parts), tok, g1_own, hot, mods, x2_own, live],
        order=[grad_three],
        name="token_rows",
    )
    both_parts = tp_gather(both_own, tp)
    kv_sums = after(kv_sums, both_own)
    kv_own = kv_sums[0].astype(F32)
    for c in range(1, half):
        kv_own = kv_own + seq_xor(kv_sums[c], 2 * c, nseq).astype(F32)
    kv_own = kv_own.astype(BF16)
    feats = width // tp
    cap_chunks = call(
        part(caption_chunks, tp),
        [sds((keys // nseq, feats))] * tp,
        [w_kv, Near(kv_own)],
        smem=[rank],
        name="caption_chunks",
    )
    mod_cols = seq_total(mod_cols, nseq)

    span = max(feats, 2 * drows)
    grad_ada, cond_rows = call(
        ada_grads,
        [sds(w_ada.shape, F32), sds((clip_pad, span))],
        [Near(mod_cols), Near(padded(scaled_own, clip_pad, 0)), w_ada],
        order=[grad_up],
        name="ada_grads",
    )
    shared = [jnp.concatenate([padded(c, span, 1), cond_rows], axis=0) for c in cap_chunks]
    shared = tp_scatter([after(c, *both_parts[1:]) for c in shared], tp)
    (block,) = call(
        part(join_rows, keys // nseq, clips),
        [sds((keys // nseq + clip_pad, span))],
        far(shared),
        name="join_rows",
    )
    blocks = lax.all_gather(block, "seq", axis=0)
    d_tokens, output = call(
        part(place_rows, tp),
        [sds((fmax, seqs, width))] * 2,
        far(both_parts),
        work=[sds((tp, 2 * own, width))],
        smem=[rank],
        name="place_rows",
    )

    d_caption, d_condition = call(
        part(place_captions, clips),
        [sds((clips, feats, slots), F32), sds((clips, width), F32)],
        [Near(blocks), condition],
        work=[sds((keys, feats)), sds((feats, keys))],
        smem=[cap_len],
        order=[output, grad_ada],
        name="place_captions",
    )

    grad_q2, grad_kv2, grad_out2, grad_qkv, grad_out = call(
        finish_rest,
        [
            sds((drows, inner), F32),
            sds((drows, 2, inner), F32),
            sds((drows, inner), F32),
            sds((3, drows, inner), F32),
            sds((drows, inner), F32),
        ],
        [sum_rest],
        order=[d_caption],
        name="finish_rest",
    )

    return (
        output.transpose(1, 0, 2),
        d_tokens.transpose(1, 0, 2),
        d_caption.transpose(0, 2, 1),
        d_condition,
        grad_qkv.transpose(1, 0, 2),
        grad_out.T,
        grad_q2,
        grad_kv2,
        grad_out2.T,
        grad_up,
        grad_down.T,
        grad_ada,
    )


def solution(mesh):
    return jax.shard_map(
        shards,
        mesh=mesh,
        in_specs=(
            P("seq", None, None),
            P("seq", None, None),
            P(),
            P(),
            P(),
            P(),
            P("seq"),
            P("seq", None, "tp"),
            P("tp", "seq"),
            P("seq", "tp"),
            P("seq", None, "tp"),
            P("tp", "seq"),
            P("seq", "tp"),
            P("tp", "seq"),
            P("seq", "tp"),
        ),
        out_specs=(
            P("seq", None, None),
            P("seq", None, None),
            P(None, None, "tp"),
            P(),
            P("seq", None, "tp"),
            P("tp", "seq"),
            P("seq", "tp"),
            P("seq", None, "tp"),
            P("tp", "seq"),
            P("seq", "tp"),
            P("tp", "seq"),
            P("seq", "tp"),
        ),
        check_vma=False,
    )
```

```python
import functools
import math

import jax
import jax.numpy as jnp
from jax import lax
from jax.experimental import pallas as pl
from jax.experimental.pallas import tpu as pltpu
from jax.sharding import PartitionSpec as P

HDIM = 72
EPSILON = 1e-06
NEG_FILL = -1e30
F32 = jnp.float32
BF16 = jnp.bfloat16
SCALE = HDIM ** (-0.5)
VMEM_LIMIT = 48 << 20


def dot_nn(a, b):
    return lax.dot_general(a, b, (((1,), (0,)), ((), ())), preferred_element_type=F32)


def dot_nt(a, b):
    return lax.dot_general(a, b, (((1,), (1,)), ((), ())), preferred_element_type=F32)


def dot_tn(a, b):
    return lax.dot_general(a, b, (((0,), (0,)), ((), ())), preferred_element_type=F32)


def sds(shape, dtype=BF16):
    return jax.ShapeDtypeStruct(shape, dtype)


class Blocks:
    def __init__(self, pieces):
        self.pieces = pieces


class Cols:
    def __init__(self, whole, start, size):
        self.whole, self.start, self.size = whole, start, size


class Near:
    def __init__(self, whole):
        self.whole = whole


class Half:
    def __init__(self, shape, start, size):
        self.shape, self.dtype, self.start, self.size = shape, BF16, start, size


class In:
    def __init__(self, buf, copies):
        self.buf, self.copies, self.ready = buf, copies, not copies

    @property
    def shape(self):
        return self.buf.shape

    def ref(self):
        if not self.ready:
            for copy in self.copies:
                copy.wait()
            self.ready = True
        return self.buf

    def __getitem__(self, index):
        return self.ref()[index]


class Out:
    def __init__(self, bufs, copies):
        self.bufs, self.copies, self.sent = bufs, copies, False

    @property
    def shape(self):
        return self.bufs[0].shape

    def __getitem__(self, index):
        return self.bufs[0][index]

    def __setitem__(self, index, value):
        self.bufs[0][index] = value

    def send(self):
        if not self.sent:
            for copy in self.copies:
                copy.start()
            self.sent = True


def call(body, outs, ins, *, name, smem=(), order=(), keep=False, work=(), limit=VMEM_LIMIT):
    vmem, hbm = pl.BlockSpec(memory_space=pltpu.VMEM), pl.BlockSpec(memory_space=pltpu.HBM)
    pin = lambda value: pltpu.with_memory_space_constraint(value, pltpu.HBM)
    ops, in_specs, in_plan, scratch_in = [], [], [], []
    n_in = 0
    for arg in ins:
        if isinstance(arg, Near):
            in_plan.append((len(ops), None, arg, 0))
            ops.append(arg.whole)
            in_specs.append(vmem)
            continue
        pieces = arg.pieces if isinstance(arg, Blocks) else [arg.whole if isinstance(arg, Cols) else arg]
        shape = pieces[0].shape
        if isinstance(arg, Blocks):
            shape = (shape[0] * len(pieces),) + shape[1:]
        elif isinstance(arg, Cols):
            shape = (shape[0], arg.size)
        in_plan.append((len(ops), len(scratch_in), arg, n_in))
        scratch_in.append(pltpu.VMEM(shape, pieces[0].dtype))
        n_in += len(pieces)
        ops += [pin(p) for p in pieces]
        in_specs += [hbm] * len(pieces)
    n_read = len(ops)
    for arg in order:
        ops.append(arg.whole if isinstance(arg, Near) else pin(arg))
        in_specs.append(vmem if isinstance(arg, Near) else hbm)
    results, out_plan, scratch_out = [], [], []
    n_out = 0
    for out in outs:
        out_plan.append((len(results), len(scratch_out), out, n_out))
        results.append(out)
        wide = (out.shape[0], out.size) if isinstance(out, Half) else out.shape
        scratch_out.append(pltpu.VMEM(wide, out.dtype))
        n_out += 1
    n_s, n_i, n_o = len(smem), len(ops), len(results)

    def kernel(*refs):
        scalars = refs[:n_s]
        src = refs[n_s : n_s + n_read]
        dst = refs[n_s + n_i : n_s + n_i + n_o]
        scratch = refs[n_s + n_i + n_o :]
        bufs = scratch[: len(scratch_in)]
        obufs = scratch[len(scratch_in) : len(scratch_in) + len(scratch_out)]
        extra = list(scratch[len(scratch_in) + len(scratch_out) : -2])
        in_sem, out_sem = scratch[-2:]
        lazy = []
        for start, at, arg, sem in in_plan:
            if at is None:
                lazy.append(In(src[start], []))
                continue
            copies = []
            if isinstance(arg, Blocks):
                rows = src[start].shape[0]
                for m in range(len(arg.pieces)):
                    block = lax.bitwise_xor(scalars[0][1], m)
                    place = bufs[at].at[pl.ds(pl.multiple_of(block * rows, 8), rows)]
                    copies.append(pltpu.make_async_copy(src[start + m], place, in_sem.at[sem + m]))
            else:
                part = src[start]
                if isinstance(arg, Cols):
                    part = part.at[:, pl.ds(arg.start, arg.size)]
                copies.append(pltpu.make_async_copy(part, bufs[at], in_sem.at[sem]))
            for copy in copies:
                copy.start()
            lazy.append(In(bufs[at], copies))
        made = []
        for first, at, out, sem in out_plan:
            place = dst[first]
            if isinstance(out, Half):
                place = place.at[:, pl.ds(out.start, out.size)]
            copy = pltpu.make_async_copy(obufs[at], place, out_sem.at[sem])
            made.append(Out([obufs[at]], [copy]))
        body(scalars, lazy, made + extra)
        for item in lazy:
            if not item.ready:
                item[...]
        for out in made:
            out.send()
        for out in made:
            for copy in out.copies:
                copy.wait()

    moved = sum(a.size * a.dtype.itemsize for a in ops[:n_read])
    moved += sum(math.prod(o.shape) * jnp.dtype(o.dtype).itemsize for o in results)
    return pl.pallas_call(
        kernel,
        out_shape=tuple(pltpu.HBM(o.shape, o.dtype) for o in results),
        in_specs=[pl.BlockSpec(memory_space=pltpu.SMEM)] * n_s + in_specs,
        out_specs=tuple([hbm] * n_o),
        scratch_shapes=scratch_in
        + scratch_out
        + [pltpu.VMEM(w.shape, w.dtype) for w in work]
        + [pltpu.SemaphoreType.DMA((max(n_in, 1),)), pltpu.SemaphoreType.DMA((max(n_out, 1),))],
        input_output_aliases={n_s + n_read: 0} if keep else {},
        compiler_params=pltpu.CompilerParams(vmem_limit_bytes=limit),
        cost_estimate=pl.CostEstimate(flops=0, transcendentals=0, bytes_accessed=moved),
        name=name,
    )(*smem, *ops)


def norm_parts(rows):
    center = rows - jnp.mean(rows, -1, keepdims=True)
    inv = lax.rsqrt(jnp.mean(center * center, -1, keepdims=True) + EPSILON)
    return center * inv, inv


def high_low(value):
    high = value.astype(BF16)
    return jnp.concatenate([high, (value - high.astype(F32)).astype(BF16)], axis=0)


def expand(hot, table):
    return dot_nn(hot, high_low(table))


def clip_sums(clips_hot, values):
    return dot_nn(clips_hot, values.astype(BF16))


def norm_back(grad, n, inv):
    return inv * (grad - jnp.mean(grad, -1, keepdims=True) - n * jnp.mean(grad * n, -1, keepdims=True))


def softmax_rows(scores):
    top = jnp.max(scores, -1, keepdims=True)
    weights = jnp.exp(scores - top)
    return weights / jnp.sum(weights, -1, keepdims=True)


def pack_rows(out, value, tp):
    own, n = value.shape[0] // tp, value.shape[1]
    for r in range(tp):
        out[:, r * n : (r + 1) * n] = value[r * own : (r + 1) * own]


def unpack_heads(pieces, tp, n):
    pieces = [p[...] for p in pieces]
    rows = []
    for b in range(tp):
        cols = []
        for k in range(tp):
            r = (b - k) % tp
            cols.append(pieces[k][:, r * n : (r + 1) * n])
        rows.append(jnp.concatenate(cols, axis=1))
    return jnp.concatenate(rows, axis=0)


def far(parts):
    return [parts[0]] + [Near(p) for p in parts[1:]]


def put_heads(work, value, start=0):
    for h in range(work.shape[0]):
        work[h] = value[:, start + h * HDIM : start + (h + 1) * HDIM]


def take_heads(work):
    return jnp.concatenate([work[h] for h in range(work.shape[0])], axis=1)


def for_heads(count, body):
    def step(h, carry):
        body(h)
        return carry

    lax.fori_loop(0, count, step, 0)


def for_columns(width, body, most=384):
    size = math.gcd(width, most)

    def step(i, carry):
        body(pl.ds(pl.multiple_of(i * size, size), size))
        return carry

    lax.fori_loop(0, width // size, step, 0)


def total(parts):
    value = parts[0][...].astype(F32)
    for part in parts[1:]:
        value = value + part[...].astype(F32)
    return value


def prepare_rows(tp, scalars, ins, outs):
    rank, clip_of, frames = scalars
    tok_o, g3_o, hot_o, clip_o, id_o, key_o, live_o, turned_o, canon = outs
    rows, width = tok_o.shape
    own = rows // tp
    fmax, seqs = ins[0].shape[:2]
    own_seqs = seqs // tp
    used = own_seqs * fmax
    row = lax.broadcasted_iota(jnp.int32, (own, 1), 0)
    spot = lax.rem(row, own_seqs)
    place = lax.broadcasted_iota(jnp.int32, key_o.shape, 1)
    keys = jnp.full(key_o.shape, -2, jnp.int32)
    owner = jnp.full(key_o.shape, -1, jnp.int32)
    alive = []
    for k in range(tp):
        base = lax.rem(rank[0] - k + tp, tp) * own_seqs
        at = slice(k * own, (k + 1) * own)
        clip = jnp.full((own, 1), -1, jnp.int32)
        name = jnp.full((own, 1), -1, jnp.int32)
        limit = jnp.zeros((own, 1), jnp.int32)
        inside = place - k * own
        mine = (inside >= 0) & (inside < used)
        turn = lax.rem(jnp.maximum(inside, 0), own_seqs)
        for j in range(own_seqs):
            c = clip_of[base + j]
            count = frames[c] * own_seqs
            here = (spot == j) & (row < used)
            clip = jnp.where(here, c, clip)
            name = jnp.where(here, k * own_seqs + j, name)
            limit = jnp.where(here, count, limit)
            there = mine & (turn == j)
            owner = jnp.where(there, c, owner)
            keys = jnp.where(there & (inside < count), k * own_seqs + j, keys)
        live = jnp.where(row < limit, 1.0, 0.0)
        alive.append(live)
        live_o[at] = live
        clip_o[at] = clip
        id_o[at] = name
        lane = lax.broadcasted_iota(jnp.int32, (own, hot_o.shape[1]), 1)
        pick = (lane == clip) | ((lane == clip + hot_o.shape[1] // 2) & (clip >= 0))
        hot_o[at] = jnp.where(pick, 1.0, 0.0).astype(BF16)
    key_o[...] = keys
    which = lax.broadcasted_iota(jnp.int32, turned_o.shape, 0)
    turned_o[...] = jnp.where(which == owner, 1.0, 0.0).astype(BF16)
    for source, out, mask in ((ins[0], tok_o, False), (ins[1], g3_o, True)):
        if own > used:
            canon[:, used:] = jnp.zeros((tp, own - used, width), BF16)
        for f in range(fmax):
            for q in range(tp):
                group = source[f, q * own_seqs : (q + 1) * own_seqs]
                canon[q, f * own_seqs : (f + 1) * own_seqs] = group
        for k in range(tp):
            value = canon[lax.rem(rank[0] - k + tp, tp)]
            if mask:
                value = (value.astype(F32) * alive[k]).astype(BF16)
            out[k * own : (k + 1) * own] = value
        out.send()


def live_captions(scalars, ins, outs):
    (cap_len,) = scalars
    (caption,) = ins
    cap_o, clip_o = outs
    keys = cap_o.shape[0]
    clips, slots = caption.shape[:2]
    col = lax.broadcasted_iota(jnp.int32, (1, keys), 1)
    clip = jnp.full((1, keys), -9, jnp.int32)
    start = jnp.int32(0)
    spans = []
    for c in range(clips):
        end = start + cap_len[c]
        clip = jnp.where((col >= start) & (col < end), c, clip)
        spans.append((start, end))
        start = end
    clip_o[...] = clip
    source, target = caption.ref(), cap_o.bufs[0]
    step = math.gcd(keys, 128)

    def some(i, carry):
        row = lax.broadcasted_iota(jnp.int32, (step, slots), 0) + i * step
        slot = lax.broadcasted_iota(jnp.int32, (step, slots), 1)
        value = jnp.zeros((step, target.shape[1]), F32)
        for c, (begin, end) in enumerate(spans):
            pick = (row - begin == slot) & (row < end)
            value = value + dot_nn(jnp.where(pick, 1.0, 0.0).astype(BF16), source[c])
        target[pl.ds(pl.multiple_of(i * step, step), step)] = value.astype(BF16)
        return carry

    lax.fori_loop(0, keys // step, some, 0)


def modulations(tp, clips, first, scalars, ins, outs):
    (rank,) = scalars
    (mods_o,) = outs
    width = mods_o.shape[2]
    groups = (ins[0].shape[0] - first) // (2 * clips)

    def joined(ref):
        cols = []
        for g in range(groups):
            at = first + g * clips
            high = ref[at : at + clips].astype(F32)
            cols.append(high + ref[at + groups * clips : at + (groups + 1) * clips].astype(F32))
        return jnp.concatenate(cols, axis=1)

    parts = [joined(ref) for ref in ins]
    cols = []
    for q in range(tp):
        value = parts[0]
        for k in range(1, tp):
            value = jnp.where(lax.rem(rank[0] - k + tp, tp) == q, parts[k], value)
        cols.append(value)
    whole = jnp.concatenate(cols, axis=1)
    mods_o[...] = jnp.zeros(mods_o.shape, F32)
    for j in range(6):
        mods_o[j, :clips] = whole[:, j * width : (j + 1) * width]


def frame_forward(tp, scalars, ins, outs):
    tok, hot, mods, row_id, key_id, w_a = ins
    attn_o, qkv_o, prob_o, fo_o = outs[:4]
    branch_o = outs[4:-2]
    heads, made = outs[-2:]
    inner = fo_o.shape[1]
    own = branch_o[0].shape[0]
    n, _ = norm_parts(tok[...].astype(F32))
    low = (n * (1.0 + expand(hot[...], mods[1])) + expand(hot[...], mods[0])).astype(BF16)
    attn_o[...] = low
    attn_o.send()
    qkv = dot_nn(low, w_a[:, : 3 * inner]).astype(BF16)
    qkv_o[...] = qkv
    qkv_o.send()
    allowed = row_id[...] == key_id[...]
    for i in range(3):
        put_heads(heads.at[i], qkv, i * inner)
    prob = prob_o.bufs[0]

    def one(h):
        scores = dot_nt(heads[0, h], heads[1, h]) * SCALE
        probs = softmax_rows(jnp.where(allowed, scores, NEG_FILL)).astype(BF16)
        prob[h] = probs
        made[h] = dot_nn(probs, heads[2, h]).astype(BF16)

    for_heads(inner // HDIM, one)
    result = take_heads(made)
    prob_o.send()
    fo_o[...] = result
    fo_o.send()
    weights, low_out = w_a.ref(), fo_o.bufs[0]

    def last(cols):
        branch = dot_nt(low_out[...], weights[cols, 3 * inner : 4 * inner]).astype(BF16)
        for r in range(tp):
            branch_o[r].bufs[0][:, cols] = branch[r * own : (r + 1) * own]

    for_columns(weights.shape[0], last)
    for out in branch_o:
        out.send()


def first_rows(tp, scalars, ins, outs):
    tok, hot, mods = ins[tp:]
    x1_o, low_o, branch_o = outs
    own = x1_o.shape[0]
    gate = expand(hot[:own], mods[2])
    branch = total(ins[:tp])
    branch_o[...] = branch
    branch_o.send()
    first = tok[:own].astype(F32) + gate * branch
    x1_o[...] = first
    low_o[...] = first.astype(BF16)


def key_values(scalars, ins, outs):
    cap, w_kv = (item.ref() for item in ins)
    kv = outs[0].bufs[0]
    step = math.gcd(kv.shape[0], 128)

    def some(i, carry):
        at = pl.ds(pl.multiple_of(i * step, 16), step)
        kv[at] = dot_nn(cap[at], w_kv[...]).astype(BF16)
        return carry

    lax.fori_loop(0, kv.shape[0] // step, some, 0)


def cross_forward(tp, inner, scalars, ins, outs):
    row_clip, key_clip, w_q2, kv = ins[tp:]
    low_o, cq_o, prob_o, co_o, pack_o, query, pair, made = outs
    low = jnp.concatenate([r[...] for r in ins[:tp]], axis=0)
    low_o[...] = low
    low_o.send()
    cq = dot_nn(low, w_q2[:, :inner]).astype(BF16)
    cq_o[...] = cq
    cq_o.send()
    allowed = row_clip[...] == key_clip[...]
    put_heads(query, cq)
    for i in range(2):
        put_heads(pair.at[i], kv.ref(), i * inner)
    prob = prob_o.bufs[0]

    def one(h):
        scores = jnp.where(allowed, dot_nt(query[h], pair[0, h]) * SCALE, NEG_FILL)
        probs = softmax_rows(scores).astype(BF16)
        prob[h] = probs
        made[h] = dot_nn(probs, pair[1, h]).astype(BF16)

    for_heads(inner // HDIM, one)
    result = take_heads(made)
    pack_rows(pack_o, result, tp)
    pack_o.send()
    prob_o.send()
    co_o[...] = result


GELU_C = 0.7978845608028654


def mlp_both(tp, inner, scalars, ins, outs):
    pieces = ins[:tp]
    hot, mods, g3, w_out2, first, low_first, w_up, w_down, turned = ins[tp:]
    x2_o, mlp_o, hid_o, db3_o, dpre_o, sums_o = outs[:6]
    dm_o, b3_o = outs[6 : 6 + tp], outs[6 + tp :]
    own, width = x2_o.shape
    hid = hid_o.shape[1]
    d_b3 = (expand(hot[...], mods[5]) * g3[...].astype(F32)).astype(BF16)
    db3_o[...] = d_b3
    db3_o.send()
    rows = unpack_heads(pieces, tp, inner)
    branch = dot_nt(rows, w_out2[...])
    second = jnp.concatenate(
        [first[...] + branch[:own], low_first[own:].astype(F32) + branch[own:]], axis=0
    )
    x2_o[...] = second[:own]
    x2_o.send()
    n, _ = norm_parts(second)
    mlp_o[...] = (n * (1.0 + expand(hot[...], mods[4])) + expand(hot[...], mods[3])).astype(BF16)
    mlp_o.send()
    low, d_low, hiddens, d_pres = (o.bufs[0] for o in (mlp_o, db3_o, hid_o, dpre_o))
    up, down = w_up.ref(), w_down.ref()

    def some(cols):
        pre = dot_nn(low[...], up[:, cols])
        th = jnp.tanh(GELU_C * (pre + 0.044715 * (pre * pre * pre)))
        hiddens[:, cols] = (0.5 * pre * (1.0 + th)).astype(BF16)
        slope = 0.5 * (1.0 + th) + 0.5 * pre * (1.0 - th * th) * (
            GELU_C * (1.0 + 3.0 * 0.044715 * (pre * pre))
        )
        d_pres[:, cols] = (slope * dot_nn(d_low[...], down[:, cols])).astype(BF16)

    if hid % 128:
        some(slice(0, hid))
    else:
        for_columns(hid, some)
    hid_o.send()
    dpre_o.send()
    turn, held, found = turned[...], g3.ref(), sums_o.bufs[0]

    def back(cols):
        d_m = dot_nt(d_pres[...], up[cols, :hid]).astype(BF16)
        for r in range(tp):
            dm_o[r].bufs[0][:, cols] = d_m[r * own : (r + 1) * own]

    for_columns(width, back)
    for out in dm_o:
        out.send()

    def ahead(cols):
        b3 = dot_nt(hiddens[...], down[cols, :hid]).astype(BF16)
        for r in range(tp):
            b3_o[r].bufs[0][:, cols] = b3[r * own : (r + 1) * own]
        found[:, cols] = clip_sums(turn, b3.astype(F32) * held[:, cols].astype(F32))

    for_columns(width, ahead)


def second_back(tp, scalars, ins, outs):
    x2, g3, hot, mods, turned = ins[tp:]
    g2_o, db2_o, sums_o = outs
    own = g2_o.shape[0]
    n, inv = norm_parts(x2[...])
    scale = 1.0 + expand(hot[:own], mods[4])
    d_m = total(ins[:tp])
    g2 = g3[:own].astype(F32) + norm_back(d_m * scale, n, inv)
    db2_o[...] = g2.astype(BF16)
    db2_o.send()
    g2_o[...] = g2
    sums_o[0] = clip_sums(turned[:, :own], d_m)
    sums_o[1] = clip_sums(turned[:, :own], d_m * n)


def cross_back(tp, inner, scalars, ins, outs):
    (rank,) = scalars
    w_out2, prob, kv, cq = ins[tp:]
    db2_o, dcq_o, dkv_o, pack_o, near_o, away_o, query, pair, grads, made, scores, back, rel = outs
    d_b2 = jnp.concatenate([r[...] for r in ins[:tp]], axis=0)
    db2_o[...] = d_b2
    db2_o.send()
    d_co = dot_nn(d_b2, w_out2[:, :inner]).astype(BF16)
    put_heads(grads, d_co)
    put_heads(query, cq.ref())
    for i in range(2):
        put_heads(pair.at[i], kv.ref(), i * inner)
    probs = prob.ref()

    def one(h):
        wide = probs[h].astype(F32)
        d_p = dot_nt(grads[h], pair[1, h])
        d_s = (wide * (d_p - jnp.sum(wide * d_p, -1, keepdims=True))).astype(BF16)
        scores[h] = d_s
        made[h] = (dot_nn(d_s, pair[0, h]) * SCALE).astype(BF16)

    for_heads(inner // HDIM, one)
    result = take_heads(made)
    pack_rows(pack_o, result, tp)
    pack_o.send()
    dcq_o[...] = result
    dcq_o.send()

    def two(h):
        back[0, h] = (dot_tn(scores[h], query[h]) * SCALE).astype(BF16)
        back[1, h] = dot_tn(probs[h], grads[h]).astype(BF16)

    for_heads(inner // HDIM, two)
    d_kv = jnp.concatenate([take_heads(back.at[0]), take_heads(back.at[1])], axis=1)
    blocks, size = rel.shape[:2]
    for b in range(blocks):
        other = lax.bitwise_xor(rank[1], b)
        rel[(other % 2) * (blocks // 2) + other // 2] = d_kv[b * size : (b + 1) * size]
    away_o[...] = rel[blocks // 2 :]
    away_o.send()
    near_o[...] = rel[: blocks // 2]
    near_o.send()
    dkv_o[...] = d_kv


def frame_back(tp, inner, scalars, ins, outs):
    pieces = ins[:tp]
    (rank,) = scalars
    w_q2, w_far, hot, mods, d_b2, g2, w_a, qkv, prob, tok, own_b1, sums, gate2, turned = ins[tp:]
    g1_o, db1_o, dqkv_o = outs[:3]
    da_o = outs[3:-6]
    heads, grads, made, cqs, norms, found = outs[-6:]
    own, width = g1_o.shape
    d_cq = unpack_heads(pieces, tp, inner)
    cqs[...] = d_cq
    near_w, far_w, held, second, table = (r.ref() for r in (w_q2, w_far, d_b2, g2, mods))
    pick = hot[...]
    g1s, d_b1s = g1_o.bufs[0], db1_o.bufs[0]

    def first(cols):
        d_x1 = dot_nt(cqs[:, :inner], near_w[cols, :inner]) + dot_nt(cqs[:, inner:], far_w[cols])
        g1s[:, cols] = second[:, cols] + d_x1[:own]
        gate = expand(pick, table[2, :, cols])
        d_b1s[:, cols] = (gate * (held[:, cols].astype(F32) + d_x1)).astype(BF16)

    for_columns(width, first)
    g1_o.send()
    db1_o.send()
    d_fo = dot_nn(d_b1s[...], w_a[:, 3 * inner : 4 * inner]).astype(BF16)
    put_heads(grads, d_fo)
    for i in range(3):
        put_heads(heads.at[i], qkv.ref(), i * inner)
    probs = prob.ref()

    def one(h):
        grad = grads[h]
        wide = probs[h].astype(F32)
        made[2, h] = dot_tn(probs[h], grad).astype(BF16)
        d_p = dot_nt(grad, heads[2, h])
        d_s = (wide * (d_p - jnp.sum(wide * d_p, -1, keepdims=True))).astype(BF16)
        made[0, h] = (dot_nn(d_s, heads[1, h]) * SCALE).astype(BF16)
        made[1, h] = (dot_tn(d_s, heads[0, h]) * SCALE).astype(BF16)

    for_heads(inner // HDIM, one)
    d_qkv = jnp.concatenate([take_heads(made.at[i]) for i in range(3)], axis=1)
    dqkv_o[...] = d_qkv
    d_qkvs = dqkv_o.bufs[0]
    dqkv_o.send()
    n, _ = norm_parts(tok[...].astype(F32))
    norms[...] = n
    weights, turn, extra = w_a.ref(), turned[...], own_b1.ref()

    def last(cols):
        low = dot_nt(d_qkvs[...], weights[cols, : 3 * inner]).astype(BF16)
        for r in range(tp):
            da_o[r].bufs[0][:own, cols] = low[r * own : (r + 1) * own]
        found[0, :, cols] = dot_nn(turn, low)
        found[1, :, cols] = clip_sums(turn, low.astype(F32) * norms[:, cols])
        found[2, :, cols] = clip_sums(turn[:, :own], g1s[:, cols] * extra[:, cols])

    for_columns(width, last)
    shift, scale, gate1 = found[0], found[1], found[2]
    whole = jnp.concatenate([shift, scale, gate1, sums[0], sums[1], gate2[...]], axis=1)
    size = whole.shape[1] // tp
    clips = (da_o[0].shape[0] - own) // -(-size // width)
    for r in range(tp):
        value = whole[:, :size]
        for q in range(1, tp):
            here = lax.rem(rank[0] - r + tp, tp) == q
            value = jnp.where(here, whole[:, q * size : (q + 1) * size], value)
        for g in range(-(-size // width)):
            part = value[:, g * width : (g + 1) * width].astype(BF16)
            da_o[r][own + g * clips : own + (g + 1) * clips, : part.shape[1]] = part
        da_o[r].send()


def token_rows(tp, scalars, ins, outs):
    tok, g1, hot, mods, x2, live = ins[2 * tp :]
    tok_o, out_o, cols_o = outs
    own, width = g1.shape
    n, inv = norm_parts(tok[:own].astype(F32))
    scale = 1.0 + expand(hot[:own], mods[1])
    gate = expand(hot[:own], mods[5])
    sums = total(ins[:tp])
    tok_o[...] = (g1[...] + norm_back(sums[:own] * scale, n, inv)).astype(BF16)
    tok_o.send()
    out_o[...] = ((x2[...] + gate * total(ins[tp : 2 * tp])) * live[:own]).astype(BF16)
    out_o.send()
    clips, size = cols_o.shape
    for g in range(-(-size // width)):
        at = own + g * clips
        part = sums[at : at + clips, : size - g * width]
        cols_o[:, g * width : g * width + part.shape[1]] = part


def place_rows(tp, scalars, ins, outs):
    (rank,) = scalars
    out, canon = outs
    fmax, seqs = out.shape[:2]
    own_seqs = seqs // tp
    for k in range(tp):
        canon[lax.rem(rank[0] - k + tp, tp)] = ins[k][...]
    for f in range(fmax):
        for q in range(tp):
            at = f * own_seqs
            out[f, q * own_seqs : (q + 1) * own_seqs] = canon[q, at : at + own_seqs]


def weight_grads(pairs, scalars, ins, outs):
    out = outs[0].bufs[0]
    refs = [item.ref() for item in ins]
    step = math.gcd(out.shape[0], 128)
    filled = sum(refs[2 * j + 1].shape[1] for j in range(pairs))
    if filled < out.shape[1]:
        out[:, filled:] = jnp.zeros((out.shape[0], out.shape[1] - filled), BF16)

    def some(i, carry):
        at = pl.ds(pl.multiple_of(i * step, step), step)
        start = 0
        for j in range(pairs):
            left, right = refs[2 * j], refs[2 * j + 1]
            width = right.shape[1]
            out[at, start : start + width] = dot_tn(left[:, at], right[...]).astype(BF16)
            start += width
        return carry

    lax.fori_loop(0, out.shape[0] // step, some, 0)


def finish_mlp(scalars, ins, outs):
    up_o, down_o = outs
    hid = up_o.shape[1]
    value = total(ins)
    up_o[...] = value[:, :hid]
    up_o.send()
    down_o[...] = value[:, hid:]


def caption_chunks(tp, scalars, ins, outs):
    (rank,) = scalars
    w_kv, d_kv = ins
    feats = outs[0].shape[1]
    w_kv[:8]
    for r, out in enumerate(outs):
        block = lax.rem(rank[0] - r + tp, tp)
        at = pl.ds(pl.multiple_of(block * feats, 8), feats)
        out[...] = dot_nt(d_kv[...], w_kv[at, :]).astype(BF16)
        out.send()


def finish_rest(scalars, ins, outs):
    (value,) = ins
    q2_o, kv2_o, out2_o, qkv_o, out_o = outs
    inner = q2_o.shape[1]
    half = value.shape[1] // 2

    def part(i):
        at = (i // 4) * half + (i % 4) * inner
        return value[:, at : at + inner].astype(F32)

    q2_o[...] = part(0)
    q2_o.send()
    for i in range(2):
        kv2_o[:, i, :] = part(1 + i)
    kv2_o.send()
    out2_o[...] = part(3)
    out2_o.send()
    for i in range(3):
        qkv_o[i] = part(4 + i)
    qkv_o.send()
    out_o[...] = part(7)


def join_rows(keys, clips, scalars, ins, outs):
    (out_o,) = outs
    value = total(ins)
    half = value.shape[1] // 2
    out_o[...] = value.astype(BF16)
    cond = value[keys : keys + clips, :half] + value[keys : keys + clips, half:]
    high = cond.astype(BF16)
    out_o[keys : keys + clips, :half] = high
    out_o[keys : keys + clips, half:] = (cond - high.astype(F32)).astype(BF16)


def place_captions(clips, scalars, ins, outs):
    (cap_len,) = scalars
    parts, condition = ins
    out_o, cond_o, rows, turned = outs
    slots = out_o.shape[2]
    keys, feats = rows.shape
    blocks = parts.shape[0]
    size = keys // blocks
    half = cond_o.shape[1] // blocks
    wide = parts.shape[2] // 2
    conds = []
    for m in range(blocks):
        rows[m * size : (m + 1) * size] = parts[m, :size, :feats]
        value = parts[m, size : size + clips].astype(F32)
        conds.append(value[:, :half] + value[:, wide : wide + half])
    value = condition[...]
    sig = jax.nn.sigmoid(value)
    cond_o[...] = jnp.concatenate(conds, axis=1) * (sig + value * sig * (1.0 - sig))
    cond_o.send()
    slot = lax.broadcasted_iota(jnp.int32, (keys, slots), 1)
    key = lax.broadcasted_iota(jnp.int32, (keys, slots), 0)
    target = out_o.bufs[0]
    turned[...] = rows[...].T

    def some(c, start):
        pick = (slot + start == key) & (slot < cap_len[c])
        target[c] = dot_nn(turned[...], jnp.where(pick, 1.0, 0.0).astype(BF16))
        return start + cap_len[c]

    lax.fori_loop(0, clips, some, jnp.int32(0))


def ada_grads(scalars, ins, outs):
    mod_cols, scaled, w_ada = ins
    grad_o, cond_o = outs
    both = high_low(mod_cols[...])
    count = both.shape[0] // 2
    grad_o[...] = dot_tn(jnp.concatenate([scaled[...], scaled[...]], axis=0), both)
    grad_o.send()
    cond = dot_nt(both, w_ada[...])
    cond = cond[:count] + cond[count:]
    top = cond.astype(BF16)
    half = cond_o.shape[1] // 2
    cond_o[...] = jnp.zeros(cond_o.shape, BF16)
    cond_o[:, : cond.shape[1]] = top
    cond_o[:, half : half + cond.shape[1]] = (cond - top.astype(F32)).astype(BF16)


def after(value, *first):
    return lax.optimization_barrier((value,) + first)[0]


def tp_gather(value, tp):
    return [value] + [
        lax.ppermute(value, "tp", [(i, (i + k) % tp) for i in range(tp)]) for k in range(1, tp)
    ]


def tp_scatter(chunks, tp):
    return [chunks[0]] + [
        lax.ppermute(chunks[r], "tp", [(i, (i - r) % tp) for i in range(tp)]) for r in range(1, tp)
    ]


def seq_xor(value, mask, nseq):
    return lax.ppermute(value, "seq", [(i, i ^ mask) for i in range(nseq)])


def seq_total(value, nseq):
    mask = 1
    while mask < nseq:
        value = value + seq_xor(value, mask, nseq)
        mask *= 2
    return value


def far_gather(value, nseq):
    return [value] + [seq_xor(value, m, nseq) for m in range(2, nseq, 2)]


def near_gather(far, nseq):
    pieces = []
    for value in far:
        pieces += [value, seq_xor(value, 1, nseq)]
    return pieces


def padded(value, size, axis):
    if value.shape[axis] == size:
        return value
    pads = [(0, 0)] * value.ndim
    pads[axis] = (0, size - value.shape[axis])
    return jnp.pad(value, pads)


def shards(
    tokens,
    cotangent,
    caption,
    condition,
    frames,
    cap_len,
    clip_of,
    w_qkv,
    w_out,
    w_query2,
    w_kv2,
    w_out2,
    w_up,
    w_down,
    w_ada,
):
    tp, nseq = lax.axis_size("tp"), lax.axis_size("seq")
    me, spot = lax.axis_index("tp"), lax.axis_index("seq")
    seqs, fmax, width = tokens.shape
    clips, slots = caption.shape[:2]
    inner, hid = w_query2.shape[1], w_up.shape[1]
    heads = inner // HDIM
    drows = w_query2.shape[0]
    own_seqs = seqs // tp
    own = -(-own_seqs * fmax // 8) * 8
    rows = tp * own
    clip_pad = 8
    keys = -(-(clips * slots // 2) // 128) * 128
    mod_size = 6 * width // tp
    rank = jnp.stack([me, spot]).astype(jnp.int32)
    part = functools.partial

    tok, g3, hot, row_clip, row_id, key_id, live, turned = call(
        part(prepare_rows, tp),
        [
            sds((rows, width)),
            sds((rows, width)),
            sds((rows, 2 * clip_pad)),
            sds((rows, 1), jnp.int32),
            sds((rows, 1), jnp.int32),
            sds((1, rows), jnp.int32),
            sds((rows, 1), F32),
            sds((clip_pad, rows)),
        ],
        [tokens.transpose(1, 0, 2), cotangent.transpose(1, 0, 2)],
        work=[sds((tp, own, width))],
        smem=[rank, clip_of, frames],
        name="prepare_rows",
    )
    cap, key_clip = call(
        live_captions,
        [sds((keys, width)), sds((1, keys), jnp.int32)],
        [caption],
        smem=[cap_len],
        name="live_captions",
    )
    lane = lambda n: -(-n // 128) * 128
    section = jnp.concatenate(
        [padded(w_query2, lane(inner), 1), w_kv2.reshape(drows, 2 * inner)], axis=1
    )
    full_b = lax.all_gather(section, "seq", axis=0, tiled=True)
    pack_a = jnp.concatenate([w_qkv.reshape(drows, 3 * inner), w_out.T], axis=1)
    scaled = jax.nn.silu(condition).astype(BF16)
    scaled_own = lax.dynamic_slice_in_dim(scaled, spot * drows, drows, 1)
    mod_part = jnp.dot(scaled_own, w_ada, preferred_element_type=F32)
    mod_part = seq_total(mod_part, nseq)
    far_a = far_gather(after(pack_a, mod_part), nseq)
    z_pack = jnp.concatenate([w_query2, w_out2.T], axis=1)
    groups = mod_size // (2 * inner)
    high = lax.reduce_precision(mod_part, 8, 7)
    mod_rows = [
        part_[:, g * 2 * inner : (g + 1) * 2 * inner].astype(BF16)
        for part_ in (high, mod_part - high)
        for g in range(groups)
    ]
    z_rest = tp_gather(jnp.concatenate([z_pack] + mod_rows, axis=0), tp)
    z_rest = lax.optimization_barrier((*z_rest, tok, *far_a[1:]))[:tp]
    (mods,) = call(
        part(modulations, tp, clips, drows),
        [sds((6, clip_pad, width), F32)],
        [Near(p) for p in z_rest],
        smem=[rank],
        name="modulations",
    )
    z_q2 = [p[:drows, :inner] for p in z_rest[1:]]
    z_out2 = [p[:drows, inner:] for p in z_rest]
    pack_c = jnp.concatenate(
        z_out2 + [padded(w_up, lane(hid), 1), padded(w_down.T, lane(hid), 1)], axis=1
    )
    full_c = lax.all_gather(pack_c, "seq", axis=0, tiled=True)
    full_d = lax.all_gather(jnp.concatenate(z_q2, axis=1), "seq", axis=0, tiled=True)
    w_q2 = Cols(full_b, 0, lane(inner))
    w_kv = Cols(full_b, lane(inner), 2 * inner)
    w_d = Cols(full_d, 0, full_d.shape[1])

    w_a = Blocks(near_gather(far_a, nseq))

    outs = call(
        part(frame_forward, tp),
        [
            sds((rows, width)),
            sds((rows, 3 * inner)),
            sds((heads, rows, rows)),
            sds((rows, inner)),
        ]
        + [sds((own, width))] * tp,
        [tok, hot, mods, row_id, key_id, w_a],
        smem=[rank],
        work=[sds((3, heads, rows, HDIM)), sds((heads, rows, HDIM))],
        name="frame_forward",
    )
    attn_in, qkv, probs, frame_out = outs[:4]
    branch_parts = tp_scatter(outs[4:], tp)
    x1_own, low_own, own_b1 = call(
        part(first_rows, tp),
        [sds((own, width), F32), sds((own, width)), sds((own, width), F32)],
        [*far(branch_parts), tok, hot, mods],
        order=[cap],
        name="first_rows",
    )
    low_parts = tp_gather(low_own, tp)
    (kv,) = call(
        key_values,
        [sds((keys, 2 * inner))],
        [cap, w_kv],
        name="key_values",
    )
    first_low, cq, cprobs, cross_out, cross_pack = call(
        part(cross_forward, tp, inner),
        [
            sds((rows, width)),
            sds((rows, inner)),
            sds((heads, rows, keys)),
            sds((rows, inner)),
            sds((own, tp * inner)),
        ],
        [*far(low_parts), row_clip, key_clip, w_q2, kv],
        work=[
            sds((heads, rows, HDIM)),
            sds((2, heads, keys, HDIM)),
            sds((heads, rows, HDIM)),
        ],
        name="cross_forward",
    )
    cross_parts = tp_gather(cross_pack, tp)
    outs = call(
        part(mlp_both, tp, inner),
        [
            sds((own, width), F32),
            sds((rows, width)),
            sds((rows, hid)),
            sds((rows, width)),
            sds((rows, hid)),
        ]
        + [sds((clip_pad, width), F32)]
        + [sds((own, width))] * (2 * tp),
        [
            *far(cross_parts),
            hot,
            mods,
            g3,
            Cols(full_c, 0, width),
            x1_own,
            first_low,
            Cols(full_c, width, lane(hid)),
            Cols(full_c, width + lane(hid), lane(hid)),
            turned,
        ],
        smem=[rank],
        name="mlp_both",
    )
    x2_own, mlp_in, hidden, d_b3, d_pre = outs[:5]
    sum_gate2 = outs[5]
    dm_chunks, b3_chunks = outs[6 : 6 + tp], outs[6 + tp :]

    dm_parts = tp_scatter(dm_chunks, tp)
    (grad_one,) = call(
        part(weight_grads, 2),
        [sds((width, 2 * hid))],
        [mlp_in, d_pre, d_b3, hidden],
        name="grads_mlp",
    )
    g2_own, db2_own, sums_two = call(
        part(second_back, tp),
        [sds((own, width), F32), sds((own, width)), sds((2, clip_pad, width), F32)],
        [*far(dm_parts), x2_own, g3, hot, mods, turned],
        order=[grad_one],
        name="second_back",
    )
    sum_one = lax.psum_scatter(after(grad_one, db2_own), "seq", scatter_dimension=0, tiled=True)
    db2_parts = tp_gather(db2_own, tp)
    d_b2, d_cq, d_kv, dcq_pack, kv_near, kv_away = call(
        part(cross_back, tp, inner),
        [
            sds((rows, width)),
            sds((rows, inner)),
            sds((keys, 2 * inner)),
            sds((own, tp * inner)),
            sds((nseq // 2, keys // nseq, 2 * inner)),
            sds((nseq // 2, keys // nseq, 2 * inner)),
        ],
        [*far(db2_parts), Cols(full_c, 0, lane(inner)), cprobs, kv, cq],
        work=[
            sds((heads, rows, HDIM)),
            sds((2, heads, keys, HDIM)),
            sds((heads, rows, HDIM)),
            sds((heads, rows, HDIM)),
            sds((heads, rows, keys)),
            sds((2, heads, keys, HDIM)),
            sds((nseq, keys // nseq, 2 * inner)),
        ],
        smem=[rank],
        name="cross_back",
    )
    dcq_parts = tp_gather(dcq_pack, tp)
    (grad_two,) = call(
        part(weight_grads, 3),
        [Half((width, 2 * lane(4 * inner)), 0, lane(4 * inner))],
        [first_low, d_cq, cap, d_kv, d_b2, cross_out],
        name="grads_cross",
    )
    half = nseq // 2
    kv_away = seq_xor(kv_away, 1, nseq)
    kv_sums = (kv_near.astype(F32) + kv_away.astype(F32)).astype(BF16)
    outs = call(
        part(frame_back, tp, inner),
        [sds((own, width), F32), sds((rows, width)), sds((rows, 3 * inner))]
        + [sds((own + clip_pad * -(-mod_size // width), width))] * tp,
        [
            *far(dcq_parts),
            w_q2,
            w_d,
            hot,
            mods,
            d_b2,
            g2_own,
            w_a,
            qkv,
            probs,
            tok,
            own_b1,
            sums_two,
            sum_gate2,
            turned,
        ],
        smem=[rank],
        order=[Near(kv_sums)],
        work=[
            sds((3, heads, rows, HDIM)),
            sds((heads, rows, HDIM)),
            sds((3, heads, rows, HDIM)),
            sds((rows, width)),
            sds((rows, width), F32),
            sds((3, clip_pad, width), F32),
        ],
        name="frame_back",
    )
    g1_own, d_b1, d_qkv = outs[:3]
    da_chunks = outs[3:]
    b3_parts = tp_scatter([after(b, grad_two, *dcq_parts[1:]) for b in b3_chunks], tp)
    da_parts = tp_scatter([after(d, *b3_parts[1:]) for d in da_chunks], tp)
    (grad_three,) = call(
        part(weight_grads, 2),
        [Half((width, 2 * lane(4 * inner)), lane(4 * inner), lane(4 * inner))],
        [attn_in, d_qkv, d_b1, frame_out],
        order=[grad_two],
        keep=True,
        name="grads_frame",
    )
    sum_rest = lax.psum_scatter(
        after(grad_three, *da_parts[1:]), "seq", scatter_dimension=0, tiled=True
    )
    grad_up, grad_down = call(
        finish_mlp,
        [sds((drows, hid), F32), sds((drows, hid), F32)],
        [sum_one],
        name="finish_mlp",
    )
    dtok_own, out_own, mod_cols = call(
        part(token_rows, tp),
        [sds((own, width)), sds((own, width)), sds((clip_pad, mod_size), F32)],
        [*far(da_parts), *far(b3_parts), tok, g1_own, hot, mods, x2_own, live],
        order=[grad_three],
        name="token_rows",
    )
    dtok_parts = tp_gather(dtok_own, tp)
    kv_sums = after(kv_sums, dtok_own)
    kv_own = kv_sums[0].astype(F32)
    for c in range(1, half):
        kv_own = kv_own + seq_xor(kv_sums[c], 2 * c, nseq).astype(F32)
    kv_own = kv_own.astype(BF16)
    feats = width // tp
    cap_chunks = call(
        part(caption_chunks, tp),
        [sds((keys // nseq, feats))] * tp,
        [w_kv, Near(kv_own)],
        smem=[rank],
        name="caption_chunks",
    )
    mod_cols = seq_total(mod_cols, nseq)

    span = max(feats, 2 * drows)
    grad_ada, cond_rows = call(
        ada_grads,
        [sds(w_ada.shape, F32), sds((clip_pad, span))],
        [Near(mod_cols), Near(padded(scaled_own, clip_pad, 0)), w_ada],
        name="ada_grads",
    )
    shared = [jnp.concatenate([padded(c, span, 1), cond_rows], axis=0) for c in cap_chunks]
    shared = tp_scatter([after(c, *dtok_parts[1:]) for c in shared], tp)
    def placed(parts, name, order=()):
        return call(
            part(place_rows, tp),
            [sds((fmax, seqs, width))],
            far(parts),
            work=[sds((tp, own, width))],
            smem=[rank],
            order=order,
            name=name,
        )[0]

    d_tokens = placed(dtok_parts, "place_tokens", [grad_up])
    (block,) = call(
        part(join_rows, keys // nseq, clips),
        [sds((keys // nseq + clip_pad, span))],
        far(shared),
        order=[d_tokens],
        name="join_rows",
    )
    out_parts = tp_gather(after(out_own, block), tp)
    blocks = lax.all_gather(block, "seq", axis=0)

    d_caption, d_condition = call(
        part(place_captions, clips),
        [sds((clips, feats, slots), F32), sds((clips, width), F32)],
        [Near(blocks), condition],
        work=[sds((keys, feats)), sds((feats, keys))],
        smem=[cap_len],
        order=[grad_ada],
        name="place_captions",
    )

    output = placed(out_parts, "place_output", [d_caption])
    grad_q2, grad_kv2, grad_out2, grad_qkv, grad_out = call(
        finish_rest,
        [
            sds((drows, inner), F32),
            sds((drows, 2, inner), F32),
            sds((drows, inner), F32),
            sds((3, drows, inner), F32),
            sds((drows, inner), F32),
        ],
        [sum_rest],
        order=[output],
        name="finish_rest",
    )

    return (
        output.transpose(1, 0, 2),
        d_tokens.transpose(1, 0, 2),
        d_caption.transpose(0, 2, 1),
        d_condition,
        grad_qkv.transpose(1, 0, 2),
        grad_out.T,
        grad_q2,
        grad_kv2,
        grad_out2.T,
        grad_up,
        grad_down.T,
        grad_ada,
    )


def solution(mesh):
    return jax.shard_map(
        shards,
        mesh=mesh,
        in_specs=(
            P("seq", None, None),
            P("seq", None, None),
            P(),
            P(),
            P(),
            P(),
            P("seq"),
            P("seq", None, "tp"),
            P("tp", "seq"),
            P("seq", "tp"),
            P("seq", None, "tp"),
            P("tp", "seq"),
            P("seq", "tp"),
            P("tp", "seq"),
            P("seq", "tp"),
        ),
        out_specs=(
            P("seq", None, None),
            P("seq", None, None),
            P(None, None, "tp"),
            P(),
            P("seq", None, "tp"),
            P("tp", "seq"),
            P("seq", "tp"),
            P("seq", None, "tp"),
            P("tp", "seq"),
            P("seq", "tp"),
            P("tp", "seq"),
            P("seq", "tp"),
        ),
        check_vma=False,
    )
```

```python
import functools
import math

import jax
import jax.numpy as jnp
from jax import lax
from jax.experimental import pallas as pl
from jax.experimental.pallas import tpu as pltpu
from jax.sharding import PartitionSpec as P

HDIM = 72
EPSILON = 1e-06
NEG_FILL = -1e30
F32 = jnp.float32
BF16 = jnp.bfloat16
SCALE = HDIM ** (-0.5)
VMEM_LIMIT = 48 << 20


def dot_nn(a, b):
    return lax.dot_general(a, b, (((1,), (0,)), ((), ())), preferred_element_type=F32)


def dot_nt(a, b):
    return lax.dot_general(a, b, (((1,), (1,)), ((), ())), preferred_element_type=F32)


def dot_tn(a, b):
    return lax.dot_general(a, b, (((0,), (0,)), ((), ())), preferred_element_type=F32)


def sds(shape, dtype=BF16):
    return jax.ShapeDtypeStruct(shape, dtype)


class Blocks:
    def __init__(self, pieces):
        self.pieces = pieces


class Cols:
    def __init__(self, whole, start, size):
        self.whole, self.start, self.size = whole, start, size


class Near:
    def __init__(self, whole):
        self.whole = whole


class Half:
    def __init__(self, shape, start, size):
        self.shape, self.dtype, self.start, self.size = shape, BF16, start, size


class In:
    def __init__(self, buf, copies):
        self.buf, self.copies, self.ready = buf, copies, not copies

    @property
    def shape(self):
        return self.buf.shape

    def ref(self):
        if not self.ready:
            for copy in self.copies:
                copy.wait()
            self.ready = True
        return self.buf

    def __getitem__(self, index):
        return self.ref()[index]


class Out:
    def __init__(self, bufs, copies):
        self.bufs, self.copies, self.sent = bufs, copies, False

    @property
    def shape(self):
        return self.bufs[0].shape

    def __getitem__(self, index):
        return self.bufs[0][index]

    def __setitem__(self, index, value):
        self.bufs[0][index] = value

    def send(self):
        if not self.sent:
            for copy in self.copies:
                copy.start()
            self.sent = True


def call(body, outs, ins, *, name, smem=(), order=(), keep=False, work=(), limit=VMEM_LIMIT):
    vmem, hbm = pl.BlockSpec(memory_space=pltpu.VMEM), pl.BlockSpec(memory_space=pltpu.HBM)
    pin = lambda value: pltpu.with_memory_space_constraint(value, pltpu.HBM)
    ops, in_specs, in_plan, scratch_in = [], [], [], []
    n_in = 0
    for arg in ins:
        if isinstance(arg, Near):
            in_plan.append((len(ops), None, arg, 0))
            ops.append(arg.whole)
            in_specs.append(vmem)
            continue
        pieces = arg.pieces if isinstance(arg, Blocks) else [arg.whole if isinstance(arg, Cols) else arg]
        shape = pieces[0].shape
        if isinstance(arg, Blocks):
            shape = (shape[0] * len(pieces),) + shape[1:]
        elif isinstance(arg, Cols):
            shape = (shape[0], arg.size)
        in_plan.append((len(ops), len(scratch_in), arg, n_in))
        scratch_in.append(pltpu.VMEM(shape, pieces[0].dtype))
        n_in += len(pieces)
        ops += [pin(p) for p in pieces]
        in_specs += [hbm] * len(pieces)
    n_read = len(ops)
    for arg in order:
        ops.append(arg.whole if isinstance(arg, Near) else pin(arg))
        in_specs.append(vmem if isinstance(arg, Near) else hbm)
    results, out_plan, scratch_out = [], [], []
    n_out = 0
    for out in outs:
        out_plan.append((len(results), len(scratch_out), out, n_out))
        results.append(out)
        wide = (out.shape[0], out.size) if isinstance(out, Half) else out.shape
        scratch_out.append(pltpu.VMEM(wide, out.dtype))
        n_out += 1
    n_s, n_i, n_o = len(smem), len(ops), len(results)

    def kernel(*refs):
        scalars = refs[:n_s]
        src = refs[n_s : n_s + n_read]
        dst = refs[n_s + n_i : n_s + n_i + n_o]
        scratch = refs[n_s + n_i + n_o :]
        bufs = scratch[: len(scratch_in)]
        obufs = scratch[len(scratch_in) : len(scratch_in) + len(scratch_out)]
        extra = list(scratch[len(scratch_in) + len(scratch_out) : -2])
        in_sem, out_sem = scratch[-2:]
        lazy = []
        for start, at, arg, sem in in_plan:
            if at is None:
                lazy.append(In(src[start], []))
                continue
            copies = []
            if isinstance(arg, Blocks):
                rows = src[start].shape[0]
                for m in range(len(arg.pieces)):
                    block = lax.bitwise_xor(scalars[0][1], m)
                    place = bufs[at].at[pl.ds(pl.multiple_of(block * rows, 8), rows)]
                    copies.append(pltpu.make_async_copy(src[start + m], place, in_sem.at[sem + m]))
            else:
                part = src[start]
                if isinstance(arg, Cols):
                    part = part.at[:, pl.ds(arg.start, arg.size)]
                copies.append(pltpu.make_async_copy(part, bufs[at], in_sem.at[sem]))
            for copy in copies:
                copy.start()
            lazy.append(In(bufs[at], copies))
        made = []
        for first, at, out, sem in out_plan:
            place = dst[first]
            if isinstance(out, Half):
                place = place.at[:, pl.ds(out.start, out.size)]
            copy = pltpu.make_async_copy(obufs[at], place, out_sem.at[sem])
            made.append(Out([obufs[at]], [copy]))
        body(scalars, lazy, made + extra)
        for item in lazy:
            if not item.ready:
                item[...]
        for out in made:
            out.send()
        for out in made:
            for copy in out.copies:
                copy.wait()

    moved = sum(a.size * a.dtype.itemsize for a in ops[:n_read])
    moved += sum(math.prod(o.shape) * jnp.dtype(o.dtype).itemsize for o in results)
    return pl.pallas_call(
        kernel,
        out_shape=tuple(pltpu.HBM(o.shape, o.dtype) for o in results),
        in_specs=[pl.BlockSpec(memory_space=pltpu.SMEM)] * n_s + in_specs,
        out_specs=tuple([hbm] * n_o),
        scratch_shapes=scratch_in
        + scratch_out
        + [pltpu.VMEM(w.shape, w.dtype) for w in work]
        + [pltpu.SemaphoreType.DMA((max(n_in, 1),)), pltpu.SemaphoreType.DMA((max(n_out, 1),))],
        input_output_aliases={n_s + n_read: 0} if keep else {},
        compiler_params=pltpu.CompilerParams(vmem_limit_bytes=limit),
        cost_estimate=pl.CostEstimate(flops=0, transcendentals=0, bytes_accessed=moved),
        name=name,
    )(*smem, *ops)


def norm_parts(rows):
    center = rows - jnp.mean(rows, -1, keepdims=True)
    inv = lax.rsqrt(jnp.mean(center * center, -1, keepdims=True) + EPSILON)
    return center * inv, inv


def high_low(value):
    high = value.astype(BF16)
    return jnp.concatenate([high, (value - high.astype(F32)).astype(BF16)], axis=0)


def expand(hot, table):
    return dot_nn(hot, high_low(table))


def clip_sums(clips_hot, values):
    return dot_nn(clips_hot, values.astype(BF16))


def norm_back(grad, n, inv):
    return inv * (grad - jnp.mean(grad, -1, keepdims=True) - n * jnp.mean(grad * n, -1, keepdims=True))


def softmax_rows(scores):
    top = jnp.max(scores, -1, keepdims=True)
    weights = jnp.exp(scores - top)
    return weights / jnp.sum(weights, -1, keepdims=True)


def pack_rows(out, value, tp):
    own, n = value.shape[0] // tp, value.shape[1]
    for r in range(tp):
        out[:, r * n : (r + 1) * n] = value[r * own : (r + 1) * own]


def unpack_heads(pieces, tp, n):
    pieces = [p[...] for p in pieces]
    rows = []
    for b in range(tp):
        cols = []
        for k in range(tp):
            r = (b - k) % tp
            cols.append(pieces[k][:, r * n : (r + 1) * n])
        rows.append(jnp.concatenate(cols, axis=1))
    return jnp.concatenate(rows, axis=0)


def far(parts):
    return [parts[0]] + [Near(p) for p in parts[1:]]


def put_heads(work, value, start=0):
    for h in range(work.shape[0]):
        work[h] = value[:, start + h * HDIM : start + (h + 1) * HDIM]


def take_heads(work):
    return jnp.concatenate([work[h] for h in range(work.shape[0])], axis=1)


def for_heads(count, body):
    def step(h, carry):
        body(h)
        return carry

    lax.fori_loop(0, count, step, 0)


def for_columns(width, body, most=384):
    size = math.gcd(width, most)

    def step(i, carry):
        body(pl.ds(pl.multiple_of(i * size, size), size))
        return carry

    lax.fori_loop(0, width // size, step, 0)


def total(parts):
    value = parts[0][...].astype(F32)
    for part in parts[1:]:
        value = value + part[...].astype(F32)
    return value


def prepare_rows(tp, scalars, ins, outs):
    rank, clip_of, frames = scalars
    tok_o, g3_o, hot_o, clip_o, id_o, key_o, live_o, turned_o, canon = outs
    rows, width = tok_o.shape
    own = rows // tp
    fmax, seqs = ins[0].shape[:2]
    own_seqs = seqs // tp
    used = own_seqs * fmax
    row = lax.broadcasted_iota(jnp.int32, (own, 1), 0)
    spot = lax.rem(row, own_seqs)
    place = lax.broadcasted_iota(jnp.int32, key_o.shape, 1)
    keys = jnp.full(key_o.shape, -2, jnp.int32)
    owner = jnp.full(key_o.shape, -1, jnp.int32)
    alive = []
    for k in range(tp):
        base = lax.rem(rank[0] - k + tp, tp) * own_seqs
        at = slice(k * own, (k + 1) * own)
        clip = jnp.full((own, 1), -1, jnp.int32)
        name = jnp.full((own, 1), -1, jnp.int32)
        limit = jnp.zeros((own, 1), jnp.int32)
        inside = place - k * own
        mine = (inside >= 0) & (inside < used)
        turn = lax.rem(jnp.maximum(inside, 0), own_seqs)
        for j in range(own_seqs):
            c = clip_of[base + j]
            count = frames[c] * own_seqs
            here = (spot == j) & (row < used)
            clip = jnp.where(here, c, clip)
            name = jnp.where(here, k * own_seqs + j, name)
            limit = jnp.where(here, count, limit)
            there = mine & (turn == j)
            owner = jnp.where(there, c, owner)
            keys = jnp.where(there & (inside < count), k * own_seqs + j, keys)
        live = jnp.where(row < limit, 1.0, 0.0)
        alive.append(live)
        live_o[at] = live
        clip_o[at] = clip
        id_o[at] = name
        lane = lax.broadcasted_iota(jnp.int32, (own, hot_o.shape[1]), 1)
        pick = (lane == clip) | ((lane == clip + hot_o.shape[1] // 2) & (clip >= 0))
        hot_o[at] = jnp.where(pick, 1.0, 0.0).astype(BF16)
    key_o[...] = keys
    which = lax.broadcasted_iota(jnp.int32, turned_o.shape, 0)
    turned_o[...] = jnp.where(which == owner, 1.0, 0.0).astype(BF16)
    for source, out, mask in ((ins[0], tok_o, False), (ins[1], g3_o, True)):
        if own > used:
            canon[:, used:] = jnp.zeros((tp, own - used, width), BF16)
        for f in range(fmax):
            for q in range(tp):
                group = source[f, q * own_seqs : (q + 1) * own_seqs]
                canon[q, f * own_seqs : (f + 1) * own_seqs] = group
        for k in range(tp):
            value = canon[lax.rem(rank[0] - k + tp, tp)]
            if mask:
                value = (value.astype(F32) * alive[k]).astype(BF16)
            out[k * own : (k + 1) * own] = value
        out.send()


def live_captions(scalars, ins, outs):
    (cap_len,) = scalars
    (caption,) = ins
    cap_o, clip_o = outs
    keys = cap_o.shape[0]
    clips, slots = caption.shape[:2]
    col = lax.broadcasted_iota(jnp.int32, (1, keys), 1)
    clip = jnp.full((1, keys), -9, jnp.int32)
    start = jnp.int32(0)
    spans = []
    for c in range(clips):
        end = start + cap_len[c]
        clip = jnp.where((col >= start) & (col < end), c, clip)
        spans.append((start, end))
        start = end
    clip_o[...] = clip
    source, target = caption.ref(), cap_o.bufs[0]
    step = math.gcd(keys, 128)

    def some(i, carry):
        row = lax.broadcasted_iota(jnp.int32, (step, slots), 0) + i * step
        slot = lax.broadcasted_iota(jnp.int32, (step, slots), 1)
        value = jnp.zeros((step, target.shape[1]), F32)
        for c, (begin, end) in enumerate(spans):
            pick = (row - begin == slot) & (row < end)
            value = value + dot_nn(jnp.where(pick, 1.0, 0.0).astype(BF16), source[c])
        target[pl.ds(pl.multiple_of(i * step, step), step)] = value.astype(BF16)
        return carry

    lax.fori_loop(0, keys // step, some, 0)


def modulations(tp, clips, first, scalars, ins, outs):
    (rank,) = scalars
    (mods_o,) = outs
    width = mods_o.shape[2]
    groups = (ins[0].shape[0] - first) // (2 * clips)

    def joined(ref):
        cols = []
        for g in range(groups):
            at = first + g * clips
            high = ref[at : at + clips].astype(F32)
            cols.append(high + ref[at + groups * clips : at + (groups + 1) * clips].astype(F32))
        return jnp.concatenate(cols, axis=1)

    parts = [joined(ref) for ref in ins]
    cols = []
    for q in range(tp):
        value = parts[0]
        for k in range(1, tp):
            value = jnp.where(lax.rem(rank[0] - k + tp, tp) == q, parts[k], value)
        cols.append(value)
    whole = jnp.concatenate(cols, axis=1)
    mods_o[...] = jnp.zeros(mods_o.shape, F32)
    for j in range(6):
        mods_o[j, :clips] = whole[:, j * width : (j + 1) * width]


def frame_forward(tp, scalars, ins, outs):
    tok, hot, mods, row_id, key_id, w_a = ins
    attn_o, qkv_o, prob_o, fo_o = outs[:4]
    branch_o = outs[4:-2]
    heads, made = outs[-2:]
    inner = fo_o.shape[1]
    own = branch_o[0].shape[0]
    n, _ = norm_parts(tok[...].astype(F32))
    low = (n * (1.0 + expand(hot[...], mods[1])) + expand(hot[...], mods[0])).astype(BF16)
    attn_o[...] = low
    attn_o.send()
    qkv = dot_nn(low, w_a[:, : 3 * inner]).astype(BF16)
    qkv_o[...] = qkv
    qkv_o.send()
    allowed = row_id[...] == key_id[...]
    for i in range(3):
        put_heads(heads.at[i], qkv, i * inner)
    prob = prob_o.bufs[0]

    def one(h):
        scores = dot_nt(heads[0, h], heads[1, h]) * SCALE
        probs = softmax_rows(jnp.where(allowed, scores, NEG_FILL)).astype(BF16)
        prob[h] = probs
        made[h] = dot_nn(probs, heads[2, h]).astype(BF16)

    for_heads(inner // HDIM, one)
    result = take_heads(made)
    prob_o.send()
    fo_o[...] = result
    fo_o.send()
    weights, low_out = w_a.ref(), fo_o.bufs[0]

    def last(cols):
        branch = dot_nt(low_out[...], weights[cols, 3 * inner : 4 * inner]).astype(BF16)
        for r in range(tp):
            branch_o[r].bufs[0][:, cols] = branch[r * own : (r + 1) * own]

    last(slice(0, weights.shape[0]))
    for out in branch_o:
        out.send()


def first_rows(tp, scalars, ins, outs):
    tok, hot, mods = ins[tp:]
    x1_o, low_o, branch_o = outs
    own = x1_o.shape[0]
    gate = expand(hot[:own], mods[2])
    branch = total(ins[:tp])
    branch_o[...] = branch
    branch_o.send()
    first = tok[:own].astype(F32) + gate * branch
    x1_o[...] = first
    low_o[...] = first.astype(BF16)


def key_values(scalars, ins, outs):
    cap, w_kv = (item.ref() for item in ins)
    kv = outs[0].bufs[0]
    step = math.gcd(kv.shape[0], 128)

    def some(i, carry):
        at = pl.ds(pl.multiple_of(i * step, 16), step)
        kv[at] = dot_nn(cap[at], w_kv[...]).astype(BF16)
        return carry

    lax.fori_loop(0, kv.shape[0] // step, some, 0)


def cross_forward(tp, inner, scalars, ins, outs):
    row_clip, key_clip, w_q2, kv = ins[tp:]
    low_o, cq_o, prob_o, co_o, pack_o, query, pair, made = outs
    low = jnp.concatenate([r[...] for r in ins[:tp]], axis=0)
    low_o[...] = low
    low_o.send()
    cq = dot_nn(low, w_q2[:, :inner]).astype(BF16)
    cq_o[...] = cq
    cq_o.send()
    allowed = row_clip[...] == key_clip[...]
    put_heads(query, cq)
    for i in range(2):
        put_heads(pair.at[i], kv.ref(), i * inner)
    prob = prob_o.bufs[0]

    def one(h):
        scores = jnp.where(allowed, dot_nt(query[h], pair[0, h]) * SCALE, NEG_FILL)
        probs = softmax_rows(scores).astype(BF16)
        prob[h] = probs
        made[h] = dot_nn(probs, pair[1, h]).astype(BF16)

    for_heads(inner // HDIM, one)
    result = take_heads(made)
    pack_rows(pack_o, result, tp)
    pack_o.send()
    prob_o.send()
    co_o[...] = result


GELU_C = 0.7978845608028654


def mlp_both(tp, inner, scalars, ins, outs):
    pieces = ins[:tp]
    hot, mods, g3, w_out2, first, low_first, w_up, w_down, turned = ins[tp:]
    x2_o, mlp_o, hid_o, db3_o, dpre_o, sums_o = outs[:6]
    dm_o, b3_o = outs[6 : 6 + tp], outs[6 + tp :]
    own, width = x2_o.shape
    hid = hid_o.shape[1]
    d_b3 = (expand(hot[...], mods[5]) * g3[...].astype(F32)).astype(BF16)
    db3_o[...] = d_b3
    db3_o.send()
    rows = unpack_heads(pieces, tp, inner)
    branch = dot_nt(rows, w_out2[...])
    second = jnp.concatenate(
        [first[...] + branch[:own], low_first[own:].astype(F32) + branch[own:]], axis=0
    )
    x2_o[...] = second[:own]
    x2_o.send()
    n, _ = norm_parts(second)
    mlp_o[...] = (n * (1.0 + expand(hot[...], mods[4])) + expand(hot[...], mods[3])).astype(BF16)
    mlp_o.send()
    low, d_low, hiddens, d_pres = (o.bufs[0] for o in (mlp_o, db3_o, hid_o, dpre_o))
    up, down = w_up.ref(), w_down.ref()

    def some(cols):
        pre = dot_nn(low[...], up[:, cols])
        th = jnp.tanh(GELU_C * (pre + 0.044715 * (pre * pre * pre)))
        hiddens[:, cols] = (0.5 * pre * (1.0 + th)).astype(BF16)
        slope = 0.5 * (1.0 + th) + 0.5 * pre * (1.0 - th * th) * (
            GELU_C * (1.0 + 3.0 * 0.044715 * (pre * pre))
        )
        d_pres[:, cols] = (slope * dot_nn(d_low[...], down[:, cols])).astype(BF16)

    if hid % 128:
        some(slice(0, hid))
    else:
        for_columns(hid, some)
    hid_o.send()
    dpre_o.send()
    turn, held, found = turned[...], g3.ref(), sums_o.bufs[0]

    def back(cols):
        d_m = dot_nt(d_pres[...], up[cols, :hid]).astype(BF16)
        for r in range(tp):
            dm_o[r].bufs[0][:, cols] = d_m[r * own : (r + 1) * own]

    for_columns(width, back)
    for out in dm_o:
        out.send()

    def ahead(cols):
        b3 = dot_nt(hiddens[...], down[cols, :hid]).astype(BF16)
        for r in range(tp):
            b3_o[r].bufs[0][:, cols] = b3[r * own : (r + 1) * own]
        found[:, cols] = clip_sums(turn, b3.astype(F32) * held[:, cols].astype(F32))

    for_columns(width, ahead)


def second_back(tp, scalars, ins, outs):
    x2, g3, hot, mods, turned = ins[tp:]
    g2_o, db2_o, sums_o = outs
    own = g2_o.shape[0]
    n, inv = norm_parts(x2[...])
    scale = 1.0 + expand(hot[:own], mods[4])
    d_m = total(ins[:tp])
    g2 = g3[:own].astype(F32) + norm_back(d_m * scale, n, inv)
    db2_o[...] = g2.astype(BF16)
    db2_o.send()
    g2_o[...] = g2
    sums_o[0] = clip_sums(turned[:, :own], d_m)
    sums_o[1] = clip_sums(turned[:, :own], d_m * n)


def cross_back(tp, inner, scalars, ins, outs):
    (rank,) = scalars
    w_out2, prob, kv, cq = ins[tp:]
    db2_o, dcq_o, dkv_o, pack_o, near_o, away_o, query, pair, grads, made, scores, back, rel = outs
    d_b2 = jnp.concatenate([r[...] for r in ins[:tp]], axis=0)
    db2_o[...] = d_b2
    db2_o.send()
    d_co = dot_nn(d_b2, w_out2[:, :inner]).astype(BF16)
    put_heads(grads, d_co)
    put_heads(query, cq.ref())
    for i in range(2):
        put_heads(pair.at[i], kv.ref(), i * inner)
    probs = prob.ref()

    def one(h):
        wide = probs[h].astype(F32)
        d_p = dot_nt(grads[h], pair[1, h])
        d_s = (wide * (d_p - jnp.sum(wide * d_p, -1, keepdims=True))).astype(BF16)
        scores[h] = d_s
        made[h] = (dot_nn(d_s, pair[0, h]) * SCALE).astype(BF16)

    for_heads(inner // HDIM, one)
    result = take_heads(made)
    pack_rows(pack_o, result, tp)
    pack_o.send()
    dcq_o[...] = result
    dcq_o.send()

    def two(h):
        back[0, h] = (dot_tn(scores[h], query[h]) * SCALE).astype(BF16)
        back[1, h] = dot_tn(probs[h], grads[h]).astype(BF16)

    for_heads(inner // HDIM, two)
    d_kv = jnp.concatenate([take_heads(back.at[0]), take_heads(back.at[1])], axis=1)
    blocks, size = rel.shape[:2]
    for b in range(blocks):
        other = lax.bitwise_xor(rank[1], b)
        rel[(other % 2) * (blocks // 2) + other // 2] = d_kv[b * size : (b + 1) * size]
    away_o[...] = rel[blocks // 2 :]
    away_o.send()
    near_o[...] = rel[: blocks // 2]
    near_o.send()
    dkv_o[...] = d_kv


def frame_back(tp, inner, scalars, ins, outs):
    pieces = ins[:tp]
    (rank,) = scalars
    w_q2, w_far, hot, mods, d_b2, g2, w_a, qkv, prob, tok, own_b1, sums, gate2, turned = ins[tp:]
    g1_o, db1_o, dqkv_o = outs[:3]
    da_o = outs[3:-6]
    heads, grads, made, cqs, norms, found = outs[-6:]
    own, width = g1_o.shape
    d_cq = unpack_heads(pieces, tp, inner)
    cqs[...] = d_cq
    near_w, far_w, held, second, table = (r.ref() for r in (w_q2, w_far, d_b2, g2, mods))
    pick = hot[...]
    g1s, d_b1s = g1_o.bufs[0], db1_o.bufs[0]

    def first(cols):
        d_x1 = dot_nt(cqs[:, :inner], near_w[cols, :inner]) + dot_nt(cqs[:, inner:], far_w[cols])
        g1s[:, cols] = second[:, cols] + d_x1[:own]
        gate = expand(pick, table[2, :, cols])
        d_b1s[:, cols] = (gate * (held[:, cols].astype(F32) + d_x1)).astype(BF16)

    for_columns(width, first)
    g1_o.send()
    db1_o.send()
    d_fo = dot_nn(d_b1s[...], w_a[:, 3 * inner : 4 * inner]).astype(BF16)
    put_heads(grads, d_fo)
    for i in range(3):
        put_heads(heads.at[i], qkv.ref(), i * inner)
    probs = prob.ref()

    def one(h):
        grad = grads[h]
        wide = probs[h].astype(F32)
        made[2, h] = dot_tn(probs[h], grad).astype(BF16)
        d_p = dot_nt(grad, heads[2, h])
        d_s = (wide * (d_p - jnp.sum(wide * d_p, -1, keepdims=True))).astype(BF16)
        made[0, h] = (dot_nn(d_s, heads[1, h]) * SCALE).astype(BF16)
        made[1, h] = (dot_tn(d_s, heads[0, h]) * SCALE).astype(BF16)

    for_heads(inner // HDIM, one)
    d_qkv = jnp.concatenate([take_heads(made.at[i]) for i in range(3)], axis=1)
    dqkv_o[...] = d_qkv
    d_qkvs = dqkv_o.bufs[0]
    dqkv_o.send()
    n, _ = norm_parts(tok[...].astype(F32))
    norms[...] = n
    weights, turn, extra = w_a.ref(), turned[...], own_b1.ref()

    def last(cols):
        low = dot_nt(d_qkvs[...], weights[cols, : 3 * inner]).astype(BF16)
        for r in range(tp):
            da_o[r].bufs[0][:own, cols] = low[r * own : (r + 1) * own]
        found[0, :, cols] = dot_nn(turn, low)
        found[1, :, cols] = clip_sums(turn, low.astype(F32) * norms[:, cols])
        found[2, :, cols] = clip_sums(turn[:, :own], g1s[:, cols] * extra[:, cols])

    for_columns(width, last)
    shift, scale, gate1 = found[0], found[1], found[2]
    whole = jnp.concatenate([shift, scale, gate1, sums[0], sums[1], gate2[...]], axis=1)
    size = whole.shape[1] // tp
    clips = (da_o[0].shape[0] - own) // -(-size // width)
    for r in range(tp):
        value = whole[:, :size]
        for q in range(1, tp):
            here = lax.rem(rank[0] - r + tp, tp) == q
            value = jnp.where(here, whole[:, q * size : (q + 1) * size], value)
        for g in range(-(-size // width)):
            part = value[:, g * width : (g + 1) * width].astype(BF16)
            da_o[r][own + g * clips : own + (g + 1) * clips, : part.shape[1]] = part
        da_o[r].send()


def token_rows(tp, scalars, ins, outs):
    tok, g1, hot, mods, x2, live = ins[2 * tp :]
    tok_o, out_o, cols_o = outs
    own, width = g1.shape
    n, inv = norm_parts(tok[:own].astype(F32))
    scale = 1.0 + expand(hot[:own], mods[1])
    gate = expand(hot[:own], mods[5])
    sums = total(ins[:tp])
    tok_o[...] = (g1[...] + norm_back(sums[:own] * scale, n, inv)).astype(BF16)
    tok_o.send()
    out_o[...] = ((x2[...] + gate * total(ins[tp : 2 * tp])) * live[:own]).astype(BF16)
    out_o.send()
    clips, size = cols_o.shape
    for g in range(-(-size // width)):
        at = own + g * clips
        part = sums[at : at + clips, : size - g * width]
        cols_o[:, g * width : g * width + part.shape[1]] = part


def place_rows(tp, scalars, ins, outs):
    (rank,) = scalars
    out, canon = outs
    fmax, seqs = out.shape[:2]
    own_seqs = seqs // tp
    for k in range(tp):
        canon[lax.rem(rank[0] - k + tp, tp)] = ins[k][...]
    for f in range(fmax):
        for q in range(tp):
            at = f * own_seqs
            out[f, q * own_seqs : (q + 1) * own_seqs] = canon[q, at : at + own_seqs]


def weight_grads(pairs, scalars, ins, outs):
    out = outs[0].bufs[0]
    refs = [item.ref() for item in ins]
    step = math.gcd(out.shape[0], 128)
    filled = sum(refs[2 * j + 1].shape[1] for j in range(pairs))
    if filled < out.shape[1]:
        out[:, filled:] = jnp.zeros((out.shape[0], out.shape[1] - filled), BF16)

    def some(i, carry):
        at = pl.ds(pl.multiple_of(i * step, step), step)
        start = 0
        for j in range(pairs):
            left, right = refs[2 * j], refs[2 * j + 1]
            width = right.shape[1]
            out[at, start : start + width] = dot_tn(left[:, at], right[...]).astype(BF16)
            start += width
        return carry

    lax.fori_loop(0, out.shape[0] // step, some, 0)


def finish_mlp(scalars, ins, outs):
    up_o, down_o = outs
    hid = up_o.shape[1]
    value = total(ins)
    up_o[...] = value[:, :hid]
    up_o.send()
    down_o[...] = value[:, hid:]


def caption_chunks(tp, scalars, ins, outs):
    (rank,) = scalars
    w_kv, d_kv = ins
    feats = outs[0].shape[1]
    w_kv[:8]
    for r, out in enumerate(outs):
        block = lax.rem(rank[0] - r + tp, tp)
        at = pl.ds(pl.multiple_of(block * feats, 8), feats)
        out[...] = dot_nt(d_kv[...], w_kv[at, :]).astype(BF16)
        out.send()


def finish_rest(scalars, ins, outs):
    (value,) = ins
    q2_o, kv2_o, out2_o, qkv_o, out_o = outs
    inner = q2_o.shape[1]
    half = value.shape[1] // 2

    def part(i):
        at = (i // 4) * half + (i % 4) * inner
        return value[:, at : at + inner].astype(F32)

    q2_o[...] = part(0)
    q2_o.send()
    for i in range(2):
        kv2_o[:, i, :] = part(1 + i)
    kv2_o.send()
    out2_o[...] = part(3)
    out2_o.send()
    for i in range(3):
        qkv_o[i] = part(4 + i)
    qkv_o.send()
    out_o[...] = part(7)


def join_rows(keys, clips, scalars, ins, outs):
    (out_o,) = outs
    value = total(ins)
    half = value.shape[1] // 2
    out_o[...] = value.astype(BF16)
    cond = value[keys : keys + clips, :half] + value[keys : keys + clips, half:]
    high = cond.astype(BF16)
    out_o[keys : keys + clips, :half] = high
    out_o[keys : keys + clips, half:] = (cond - high.astype(F32)).astype(BF16)


def place_captions(clips, scalars, ins, outs):
    (cap_len,) = scalars
    parts, condition = ins
    out_o, cond_o, rows, turned = outs
    slots = out_o.shape[2]
    keys, feats = rows.shape
    blocks = parts.shape[0]
    size = keys // blocks
    half = cond_o.shape[1] // blocks
    wide = parts.shape[2] // 2
    conds = []
    for m in range(blocks):
        rows[m * size : (m + 1) * size] = parts[m, :size, :feats]
        value = parts[m, size : size + clips].astype(F32)
        conds.append(value[:, :half] + value[:, wide : wide + half])
    value = condition[...]
    sig = jax.nn.sigmoid(value)
    cond_o[...] = jnp.concatenate(conds, axis=1) * (sig + value * sig * (1.0 - sig))
    cond_o.send()
    slot = lax.broadcasted_iota(jnp.int32, (keys, slots), 1)
    key = lax.broadcasted_iota(jnp.int32, (keys, slots), 0)
    target = out_o.bufs[0]
    turned[...] = rows[...].T

    def some(c, start):
        pick = (slot + start == key) & (slot < cap_len[c])
        target[c] = dot_nn(turned[...], jnp.where(pick, 1.0, 0.0).astype(BF16))
        return start + cap_len[c]

    lax.fori_loop(0, clips, some, jnp.int32(0))


def ada_grads(scalars, ins, outs):
    mod_cols, scaled, w_ada = ins
    grad_o, cond_o = outs
    both = high_low(mod_cols[...])
    count = both.shape[0] // 2
    grad_o[...] = dot_tn(jnp.concatenate([scaled[...], scaled[...]], axis=0), both)
    grad_o.send()
    cond = dot_nt(both, w_ada[...])
    cond = cond[:count] + cond[count:]
    top = cond.astype(BF16)
    half = cond_o.shape[1] // 2
    cond_o[...] = jnp.zeros(cond_o.shape, BF16)
    cond_o[:, : cond.shape[1]] = top
    cond_o[:, half : half + cond.shape[1]] = (cond - top.astype(F32)).astype(BF16)


def after(value, *first):
    return lax.optimization_barrier((value,) + first)[0]


def tp_gather(value, tp):
    return [value] + [
        lax.ppermute(value, "tp", [(i, (i + k) % tp) for i in range(tp)]) for k in range(1, tp)
    ]


def tp_scatter(chunks, tp):
    return [chunks[0]] + [
        lax.ppermute(chunks[r], "tp", [(i, (i - r) % tp) for i in range(tp)]) for r in range(1, tp)
    ]


def seq_xor(value, mask, nseq):
    return lax.ppermute(value, "seq", [(i, i ^ mask) for i in range(nseq)])


def seq_total(value, nseq):
    mask = 1
    while mask < nseq:
        value = value + seq_xor(value, mask, nseq)
        mask *= 2
    return value


def far_gather(value, nseq):
    return [value] + [seq_xor(value, m, nseq) for m in range(2, nseq, 2)]


def near_gather(far, nseq):
    pieces = []
    for value in far:
        pieces += [value, seq_xor(value, 1, nseq)]
    return pieces


def padded(value, size, axis):
    if value.shape[axis] == size:
        return value
    pads = [(0, 0)] * value.ndim
    pads[axis] = (0, size - value.shape[axis])
    return jnp.pad(value, pads)


def shards(
    tokens,
    cotangent,
    caption,
    condition,
    frames,
    cap_len,
    clip_of,
    w_qkv,
    w_out,
    w_query2,
    w_kv2,
    w_out2,
    w_up,
    w_down,
    w_ada,
):
    tp, nseq = lax.axis_size("tp"), lax.axis_size("seq")
    me, spot = lax.axis_index("tp"), lax.axis_index("seq")
    seqs, fmax, width = tokens.shape
    clips, slots = caption.shape[:2]
    inner, hid = w_query2.shape[1], w_up.shape[1]
    heads = inner // HDIM
    drows = w_query2.shape[0]
    own_seqs = seqs // tp
    own = -(-own_seqs * fmax // 8) * 8
    rows = tp * own
    clip_pad = 8
    keys = -(-(clips * slots // 2) // 128) * 128
    mod_size = 6 * width // tp
    rank = jnp.stack([me, spot]).astype(jnp.int32)
    part = functools.partial

    tok, g3, hot, row_clip, row_id, key_id, live, turned = call(
        part(prepare_rows, tp),
        [
            sds((rows, width)),
            sds((rows, width)),
            sds((rows, 2 * clip_pad)),
            sds((rows, 1), jnp.int32),
            sds((rows, 1), jnp.int32),
            sds((1, rows), jnp.int32),
            sds((rows, 1), F32),
            sds((clip_pad, rows)),
        ],
        [tokens.transpose(1, 0, 2), cotangent.transpose(1, 0, 2)],
        work=[sds((tp, own, width))],
        smem=[rank, clip_of, frames],
        name="prepare_rows",
    )
    cap, key_clip = call(
        live_captions,
        [sds((keys, width)), sds((1, keys), jnp.int32)],
        [caption],
        smem=[cap_len],
        name="live_captions",
    )
    lane = lambda n: -(-n // 128) * 128
    section = jnp.concatenate(
        [padded(w_query2, lane(inner), 1), w_kv2.reshape(drows, 2 * inner)], axis=1
    )
    full_b = lax.all_gather(section, "seq", axis=0, tiled=True)
    pack_a = jnp.concatenate([w_qkv.reshape(drows, 3 * inner), w_out.T], axis=1)
    scaled = jax.nn.silu(condition).astype(BF16)
    scaled_own = lax.dynamic_slice_in_dim(scaled, spot * drows, drows, 1)
    mod_part = jnp.dot(scaled_own, w_ada, preferred_element_type=F32)
    mod_part = seq_total(mod_part, nseq)
    far_a = far_gather(after(pack_a, mod_part), nseq)
    z_pack = jnp.concatenate([w_query2, w_out2.T], axis=1)
    groups = mod_size // (2 * inner)
    high = lax.reduce_precision(mod_part, 8, 7)
    mod_rows = [
        part_[:, g * 2 * inner : (g + 1) * 2 * inner].astype(BF16)
        for part_ in (high, mod_part - high)
        for g in range(groups)
    ]
    z_rest = tp_gather(jnp.concatenate([z_pack] + mod_rows, axis=0), tp)
    z_rest = lax.optimization_barrier((*z_rest, tok, *far_a[1:]))[:tp]
    (mods,) = call(
        part(modulations, tp, clips, drows),
        [sds((6, clip_pad, width), F32)],
        [Near(p) for p in z_rest],
        smem=[rank],
        name="modulations",
    )
    z_q2 = [p[:drows, :inner] for p in z_rest[1:]]
    z_out2 = [p[:drows, inner:] for p in z_rest]
    pack_c = jnp.concatenate(
        z_out2 + [padded(w_up, lane(hid), 1), padded(w_down.T, lane(hid), 1)], axis=1
    )
    full_c = lax.all_gather(pack_c, "seq", axis=0, tiled=True)
    full_d = lax.all_gather(jnp.concatenate(z_q2, axis=1), "seq", axis=0, tiled=True)
    w_q2 = Cols(full_b, 0, lane(inner))
    w_kv = Cols(full_b, lane(inner), 2 * inner)
    w_d = Cols(full_d, 0, full_d.shape[1])

    w_a = Blocks(near_gather(far_a, nseq))

    outs = call(
        part(frame_forward, tp),
        [
            sds((rows, width)),
            sds((rows, 3 * inner)),
            sds((heads, rows, rows)),
            sds((rows, inner)),
        ]
        + [sds((own, width))] * tp,
        [tok, hot, mods, row_id, key_id, w_a],
        smem=[rank],
        work=[sds((3, heads, rows, HDIM)), sds((heads, rows, HDIM))],
        name="frame_forward",
    )
    attn_in, qkv, probs, frame_out = outs[:4]
    branch_parts = tp_scatter(outs[4:], tp)
    x1_own, low_own, own_b1 = call(
        part(first_rows, tp),
        [sds((own, width), F32), sds((own, width)), sds((own, width), F32)],
        [*far(branch_parts), tok, hot, mods],
        order=[cap],
        name="first_rows",
    )
    low_parts = tp_gather(low_own, tp)
    (kv,) = call(
        key_values,
        [sds((keys, 2 * inner))],
        [cap, w_kv],
        name="key_values",
    )
    first_low, cq, cprobs, cross_out, cross_pack = call(
        part(cross_forward, tp, inner),
        [
            sds((rows, width)),
            sds((rows, inner)),
            sds((heads, rows, keys)),
            sds((rows, inner)),
            sds((own, tp * inner)),
        ],
        [*far(low_parts), row_clip, key_clip, w_q2, kv],
        work=[
            sds((heads, rows, HDIM)),
            sds((2, heads, keys, HDIM)),
            sds((heads, rows, HDIM)),
        ],
        name="cross_forward",
    )
    cross_parts = tp_gather(cross_pack, tp)
    outs = call(
        part(mlp_both, tp, inner),
        [
            sds((own, width), F32),
            sds((rows, width)),
            sds((rows, hid)),
            sds((rows, width)),
            sds((rows, hid)),
        ]
        + [sds((clip_pad, width), F32)]
        + [sds((own, width))] * (2 * tp),
        [
            *far(cross_parts),
            hot,
            mods,
            g3,
            Cols(full_c, 0, width),
            x1_own,
            first_low,
            Cols(full_c, width, lane(hid)),
            Cols(full_c, width + lane(hid), lane(hid)),
            turned,
        ],
        smem=[rank],
        name="mlp_both",
    )
    x2_own, mlp_in, hidden, d_b3, d_pre = outs[:5]
    sum_gate2 = outs[5]
    dm_chunks, b3_chunks = outs[6 : 6 + tp], outs[6 + tp :]

    dm_parts = tp_scatter(dm_chunks, tp)
    (grad_one,) = call(
        part(weight_grads, 2),
        [sds((width, 2 * hid))],
        [mlp_in, d_pre, d_b3, hidden],
        name="grads_mlp",
    )
    g2_own, db2_own, sums_two = call(
        part(second_back, tp),
        [sds((own, width), F32), sds((own, width)), sds((2, clip_pad, width), F32)],
        [*far(dm_parts), x2_own, g3, hot, mods, turned],
        order=[grad_one],
        name="second_back",
    )
    sum_one = lax.psum_scatter(after(grad_one, db2_own), "seq", scatter_dimension=0, tiled=True)
    db2_parts = tp_gather(db2_own, tp)
    d_b2, d_cq, d_kv, dcq_pack, kv_near, kv_away = call(
        part(cross_back, tp, inner),
        [
            sds((rows, width)),
            sds((rows, inner)),
            sds((keys, 2 * inner)),
            sds((own, tp * inner)),
            sds((nseq // 2, keys // nseq, 2 * inner)),
            sds((nseq // 2, keys // nseq, 2 * inner)),
        ],
        [*far(db2_parts), Cols(full_c, 0, lane(inner)), cprobs, kv, cq],
        work=[
            sds((heads, rows, HDIM)),
            sds((2, heads, keys, HDIM)),
            sds((heads, rows, HDIM)),
            sds((heads, rows, HDIM)),
            sds((heads, rows, keys)),
            sds((2, heads, keys, HDIM)),
            sds((nseq, keys // nseq, 2 * inner)),
        ],
        smem=[rank],
        name="cross_back",
    )
    dcq_parts = tp_gather(dcq_pack, tp)
    (grad_two,) = call(
        part(weight_grads, 3),
        [Half((width, 2 * lane(4 * inner)), 0, lane(4 * inner))],
        [first_low, d_cq, cap, d_kv, d_b2, cross_out],
        name="grads_cross",
    )
    half = nseq // 2
    kv_away = seq_xor(kv_away, 1, nseq)
    kv_sums = (kv_near.astype(F32) + kv_away.astype(F32)).astype(BF16)
    outs = call(
        part(frame_back, tp, inner),
        [sds((own, width), F32), sds((rows, width)), sds((rows, 3 * inner))]
        + [sds((own + clip_pad * -(-mod_size // width), width))] * tp,
        [
            *far(dcq_parts),
            w_q2,
            w_d,
            hot,
            mods,
            d_b2,
            g2_own,
            w_a,
            qkv,
            probs,
            tok,
            own_b1,
            sums_two,
            sum_gate2,
            turned,
        ],
        smem=[rank],
        order=[Near(kv_sums)],
        work=[
            sds((3, heads, rows, HDIM)),
            sds((heads, rows, HDIM)),
            sds((3, heads, rows, HDIM)),
            sds((rows, width)),
            sds((rows, width), F32),
            sds((3, clip_pad, width), F32),
        ],
        name="frame_back",
    )
    g1_own, d_b1, d_qkv = outs[:3]
    da_chunks = outs[3:]
    b3_parts = tp_scatter([after(b, grad_two, *dcq_parts[1:]) for b in b3_chunks], tp)
    da_parts = tp_scatter([after(d, *b3_parts[1:]) for d in da_chunks], tp)
    (grad_three,) = call(
        part(weight_grads, 2),
        [Half((width, 2 * lane(4 * inner)), lane(4 * inner), lane(4 * inner))],
        [attn_in, d_qkv, d_b1, frame_out],
        order=[grad_two],
        keep=True,
        name="grads_frame",
    )
    sum_rest = lax.psum_scatter(
        after(grad_three, *da_parts[1:]), "seq", scatter_dimension=0, tiled=True
    )
    grad_up, grad_down = call(
        finish_mlp,
        [sds((drows, hid), F32), sds((drows, hid), F32)],
        [sum_one],
        name="finish_mlp",
    )
    dtok_own, out_own, mod_cols = call(
        part(token_rows, tp),
        [sds((own, width)), sds((own, width)), sds((clip_pad, mod_size), F32)],
        [*far(da_parts), *far(b3_parts), tok, g1_own, hot, mods, x2_own, live],
        order=[grad_three],
        name="token_rows",
    )
    dtok_parts = tp_gather(dtok_own, tp)
    kv_sums = after(kv_sums, dtok_own)
    kv_own = kv_sums[0].astype(F32)
    for c in range(1, half):
        kv_own = kv_own + seq_xor(kv_sums[c], 2 * c, nseq).astype(F32)
    kv_own = kv_own.astype(BF16)
    feats = width // tp
    cap_chunks = call(
        part(caption_chunks, tp),
        [sds((keys // nseq, feats))] * tp,
        [w_kv, Near(kv_own)],
        smem=[rank],
        name="caption_chunks",
    )
    mod_cols = seq_total(mod_cols, nseq)

    span = max(feats, 2 * drows)
    grad_ada, cond_rows = call(
        ada_grads,
        [sds(w_ada.shape, F32), sds((clip_pad, span))],
        [Near(mod_cols), Near(padded(scaled_own, clip_pad, 0)), w_ada],
        name="ada_grads",
    )
    shared = [jnp.concatenate([padded(c, span, 1), cond_rows], axis=0) for c in cap_chunks]
    shared = tp_scatter([after(c, *dtok_parts[1:]) for c in shared], tp)
    def placed(parts, name, order=()):
        return call(
            part(place_rows, tp),
            [sds((fmax, seqs, width))],
            far(parts),
            work=[sds((tp, own, width))],
            smem=[rank],
            order=order,
            name=name,
        )[0]

    d_tokens = placed(dtok_parts, "place_tokens", [grad_up])
    (block,) = call(
        part(join_rows, keys // nseq, clips),
        [sds((keys // nseq + clip_pad, span))],
        far(shared),
        order=[d_tokens],
        name="join_rows",
    )
    out_parts = tp_gather(after(out_own, block), tp)
    blocks = lax.all_gather(block, "seq", axis=0)

    d_caption, d_condition = call(
        part(place_captions, clips),
        [sds((clips, feats, slots), F32), sds((clips, width), F32)],
        [Near(blocks), condition],
        work=[sds((keys, feats)), sds((feats, keys))],
        smem=[cap_len],
        order=[grad_ada],
        name="place_captions",
    )

    output = placed(out_parts, "place_output", [d_caption])
    grad_q2, grad_kv2, grad_out2, grad_qkv, grad_out = call(
        finish_rest,
        [
            sds((drows, inner), F32),
            sds((drows, 2, inner), F32),
            sds((drows, inner), F32),
            sds((3, drows, inner), F32),
            sds((drows, inner), F32),
        ],
        [sum_rest],
        order=[output],
        name="finish_rest",
    )

    return (
        output.transpose(1, 0, 2),
        d_tokens.transpose(1, 0, 2),
        d_caption.transpose(0, 2, 1),
        d_condition,
        grad_qkv.transpose(1, 0, 2),
        grad_out.T,
        grad_q2,
        grad_kv2,
        grad_out2.T,
        grad_up,
        grad_down.T,
        grad_ada,
    )


def solution(mesh):
    return jax.shard_map(
        shards,
        mesh=mesh,
        in_specs=(
            P("seq", None, None),
            P("seq", None, None),
            P(),
            P(),
            P(),
            P(),
            P("seq"),
            P("seq", None, "tp"),
            P("tp", "seq"),
            P("seq", "tp"),
            P("seq", None, "tp"),
            P("tp", "seq"),
            P("seq", "tp"),
            P("tp", "seq"),
            P("seq", "tp"),
        ),
        out_specs=(
            P("seq", None, None),
            P("seq", None, None),
            P(None, None, "tp"),
            P(),
            P("seq", None, "tp"),
            P("tp", "seq"),
            P("seq", "tp"),
            P("seq", None, "tp"),
            P("tp", "seq"),
            P("seq", "tp"),
            P("tp", "seq"),
            P("seq", "tp"),
        ),
        check_vma=False,
    )
```
